32 devices in a mesh: pipe: 2 (over core), tensor: 4 (over y, x), dp: 4 (over z).
Axes of the slice: x: 2, y: 2, z: 4, core: 2. Of those that a mesh axis runs over, the one named last changes fastest.
Arguments:
- layer_input: bfloat16 [2, 512, 768], P(None, 'dp'), may hold values from -6 to 6
- enc_states: bfloat16 [2, 1024, 768], P(None, 'dp'), may hold values from -6 to 6
- out_grad: bfloat16 [2, 512, 768], P(None, 'dp'), may hold values from -6 to 6
- dec_seg: int32 [2, 512], P(None, 'dp'), may hold values from 0 to 3, as said below
- enc_seg: int32 [2, 1024], P(None, 'dp'), may hold values from 0 to 3, as said below
- buckets: int32 [128], replicated, may hold values from 0 to 31, as said below
- sa_q: bfloat16 [2, 768, 768], P('pipe', 'dp', 'tensor'), may hold values from -0.02734375 to 0.02734375
- sa_k: bfloat16 [2, 768, 768], P('pipe', 'dp', 'tensor'), may hold values from -0.21875 to 0.21875
- sa_v: bfloat16 [2, 768, 768], P('pipe', 'dp', 'tensor'), may hold values from -0.21875 to 0.21875
- sa_o: bfloat16 [2, 768, 768], P('pipe', 'tensor', 'dp'), may hold values from -0.875 to 0.875
- ca_q: bfloat16 [2, 768, 768], P('pipe', 'dp', 'tensor'), may hold values from -0.02734375 to 0.02734375
- ca_k: bfloat16 [2, 768, 768], P('pipe', 'dp', 'tensor'), may hold values from -0.21875 to 0.21875
- ca_v: bfloat16 [2, 768, 768], P('pipe', 'dp', 'tensor'), may hold values from -0.21875 to 0.21875
- ca_o: bfloat16 [2, 768, 768], P('pipe', 'tensor', 'dp'), may hold values from -0.875 to 0.875
- ff_gate: bfloat16 [2, 768, 2048], P('pipe', 'dp', 'tensor'), may hold values from -0.21875 to 0.21875
- ff_up: bfloat16 [2, 768, 2048], P('pipe', 'dp', 'tensor'), may hold values from -0.21875 to 0.21875
- ff_down: bfloat16 [2, 2048, 768], P('pipe', 'tensor', 'dp'), may hold values from -0.125 to 0.125
- norm_gains: bfloat16 [2, 3, 768], P('pipe', None, 'dp'), may hold values from 0.5 to 1.5
- rel_table: bfloat16 [2, 32, 12], P('pipe', 'dp', 'tensor'), may hold values from -4 to 4
Outputs:
- section_out: bfloat16 [2, 2, 512, 768], P('pipe', None, 'dp')
- section_in_grad: float32 [2, 2, 512, 768], P('pipe', None, 'dp')
- enc_grad: float32 [2, 2, 1024, 768], P('pipe', None, 'dp', 'tensor')
- grad_sa_q: float32 [2, 768, 768], P('pipe', 'dp', 'tensor')
- grad_sa_k: float32 [2, 768, 768], P('pipe', 'dp', 'tensor')
- grad_sa_v: float32 [2, 768, 768], P('pipe', 'dp', 'tensor')
- grad_sa_o: float32 [2, 768, 768], P('pipe', 'tensor', 'dp')
- grad_ca_q: float32 [2, 768, 768], P('pipe', 'dp', 'tensor')
- grad_ca_k: float32 [2, 768, 768], P('pipe', 'dp', 'tensor')
- grad_ca_v: float32 [2, 768, 768], P('pipe', 'dp', 'tensor')
- grad_ca_o: float32 [2, 768, 768], P('pipe', 'tensor', 'dp')
- grad_ff_gate: float32 [2, 768, 2048], P('pipe', 'dp', 'tensor')
- grad_ff_up: float32 [2, 768, 2048], P('pipe', 'dp', 'tensor')
- grad_ff_down: float32 [2, 2048, 768], P('pipe', 'tensor', 'dp')
- grad_norm_gains: float32 [2, 3, 768], P('pipe', None, 'dp')
- grad_rel_table: float32 [2, 32, 12], P('pipe', 'dp', 'tensor')
The draws below stay inside these ranges and needn't reach their ends.
Inputs may be any that keep to these rules, and one draw needn't show every extreme that they name: `dec_seg`: within each aligned block of 128 entries (one micro-batch of one group) the ids start at 0, never fall, and step up by one at exactly 3 positions. `enc_seg`: within each aligned block of 256 entries the ids start at 0, never fall, and step up by one at exactly 3 positions, so every decoder sequence has encoder tokens of its own id. `buckets`: Non-decreasing in the distance, 0 at distance 0, rising by at most one a step, and reaching 31.
All inputs are finite; a program needn't handle non-finite values.
Results may differ from the reference program's by a relative error of at most 0.033.
Values may be sent and summed in bfloat16 or wider, within the bound.
A program may use at most 128 MiB of HBM per device.

```python
from functools import partial
import jax
import jax.numpy as jnp
from jax import lax

D = 768
HEADS = 12
HEAD = 64
FF = 2048
BUCKETS = 32
MAXD = 128
INNER = 768
MB_TOK = 128
ENC_TOK = 256
SEQS = 4
MICRO = 2
SECTIONS = 2
ROWS = 512
ENC_ROWS = 1024


def segment_ids(base_key, slot_count, block_width):
    key_list = jax.random.split(base_key, slot_count)

    def cut_points(single_key):
        return jax.random.permutation(single_key, block_width - 1)[:SEQS - 1] + 1
    cut_table = jax.vmap(cut_points)(key_list)
    positions = jnp.arange(block_width, dtype=jnp.int32)
    return jnp.sum((positions[None, :, None] >= cut_table[:, None, :]).astype(jnp.int32), axis=-1).astype(jnp.int32)


def draw_dec_seg(key, part):
    return segment_ids(jax.random.fold_in(key, 11), MICRO * (ROWS // MB_TOK), MB_TOK).reshape(MICRO, ROWS)


def draw_enc_seg(key, part):
    return segment_ids(jax.random.fold_in(key, 12), MICRO * (ENC_ROWS // ENC_TOK), ENC_TOK).reshape(MICRO, ENC_ROWS)


def draw_buckets(key, part):
    cut_table = jax.random.permutation(jax.random.fold_in(key, 13), MAXD - 1)[:BUCKETS - 1] + 1
    positions = jnp.arange(MAXD, dtype=jnp.int32)
    return jnp.sum((positions[:, None] >= cut_table[None, :]).astype(jnp.int32), axis=-1).astype(jnp.int32)


def levels(key, extent, pieces, smallest, largest):
    loudness = 1.0
    for position, shards_of in pieces:
        draws = jax.random.uniform(jax.random.fold_in(jax.random.fold_in(key, 6), position), (shards_of,), jnp.float32, smallest / len(pieces), largest / len(pieces))
        loudness = loudness * jnp.repeat(jnp.exp(draws), extent[position] // shards_of).reshape((-1,) + (1,) * (len(extent) - 1 - position))
    return loudness


def bell_draw(rng, dims, deviation, most, shards=(), held_as=jnp.bfloat16):
    array = jax.random.normal(rng, dims, jnp.float32) * deviation
    if len(shards) > 0:
        array = levels(rng, dims, shards, -0.22, 0.18) * array
    return jnp.clip(array, min=-most, max=most).astype(held_as)


def setup_inputs(seed: int = 0) -> dict:
    streams_of = jax.random.split(jax.random.key(seed), 20)
    return {
        "layer_input": bell_draw(streams_of[0], (MICRO, ROWS, D), 1.0, 6.0, ((1, 4),)),
        "enc_states": bell_draw(streams_of[1], (MICRO, ENC_ROWS, D), 1.0, 6.0, ((1, 4),)),
        "out_grad": bell_draw(streams_of[2], (MICRO, ROWS, D), 1.0, 6.0, ((1, 4),)),
        "dec_seg": draw_dec_seg(jax.random.fold_in(streams_of[19], 71), 0),
        "enc_seg": draw_enc_seg(jax.random.fold_in(streams_of[19], 71), 0),
        "buckets": draw_buckets(jax.random.fold_in(streams_of[19], 71), 0),
        "sa_q": bell_draw(streams_of[6], (SECTIONS, D, INNER), (D * HEAD) ** -0.5, 0.02734375, ((0, 2), (1, 4), (2, 4))),
        "sa_k": bell_draw(streams_of[7], (SECTIONS, D, INNER), D ** -0.5, 0.21875, ((0, 2), (1, 4), (2, 4))),
        "sa_v": bell_draw(streams_of[8], (SECTIONS, D, INNER), D ** -0.5, 0.21875, ((0, 2), (1, 4), (2, 4))),
        "sa_o": bell_draw(streams_of[9], (SECTIONS, INNER, D), (INNER // 16) ** -0.5, 0.875, ((0, 2), (1, 4), (2, 4))),
        "ca_q": bell_draw(streams_of[10], (SECTIONS, D, INNER), (D * HEAD) ** -0.5, 0.02734375, ((0, 2), (1, 4), (2, 4))),
        "ca_k": bell_draw(streams_of[11], (SECTIONS, D, INNER), D ** -0.5, 0.21875, ((0, 2), (1, 4), (2, 4))),
        "ca_v": bell_draw(streams_of[12], (SECTIONS, D, INNER), D ** -0.5, 0.21875, ((0, 2), (1, 4), (2, 4))),
        "ca_o": bell_draw(streams_of[13], (SECTIONS, INNER, D), (INNER // 16) ** -0.5, 0.875, ((0, 2), (1, 4), (2, 4))),
        "ff_gate": bell_draw(streams_of[14], (SECTIONS, D, FF), D ** -0.5, 0.21875, ((0, 2), (1, 4), (2, 4))),
        "ff_up": bell_draw(streams_of[15], (SECTIONS, D, FF), D ** -0.5, 0.21875, ((0, 2), (1, 4), (2, 4))),
        "ff_down": bell_draw(streams_of[16], (SECTIONS, FF, D), FF ** -0.5, 0.125, ((0, 2), (1, 4), (2, 4))),
        "norm_gains": jnp.clip(1.0 + 0.1 * jax.random.normal(streams_of[17], (SECTIONS, 3, D), jnp.float32), 0.5, 1.5).astype(jnp.bfloat16),
        "rel_table": bell_draw(streams_of[18], (SECTIONS, BUCKETS, HEADS), 1.0, 4.0, ((0, 2), (1, 4), (2, 4))),
    }


EPS = 1e-06

def product(form, left_side, right_side):
    return jnp.einsum(form, left_side.astype(jnp.float32), right_side.astype(jnp.float32))

def rms_norm(values, gain):
    return values * lax.rsqrt(lax.optimization_barrier(jnp.mean(values * values, axis=-1, keepdims=True)) + EPS) * gain

def norm_back(values, gain, cotangent):
    _, pull_back = jax.vjp(rms_norm, values, gain)
    return pull_back(cotangent)

def gelu_tanh(values):
    return jax.nn.gelu(values, approximate=True)

def bucket_table(buckets):
    return (buckets[:, None] == jnp.arange(BUCKETS, dtype=jnp.int32)[None, :]).astype(jnp.float32)

def distance_bias(one_hot, table):
    return jnp.dot(one_hot, table.astype(jnp.float32), precision=lax.Precision.HIGHEST).T

def build_masks(dec_ids, enc_ids):
    row_count = dec_ids.shape[0]
    row_ids = jnp.arange(row_count, dtype=jnp.int32)
    allowed_self = (dec_ids[:, None] == dec_ids[None, :]) & (row_ids[None, :] <= row_ids[:, None])
    allowed_cross = dec_ids[:, None] == enc_ids[None, :]
    distance = jnp.clip(row_ids[:, None] - row_ids[None, :], 0, MAXD - 1).astype(jnp.int32)
    return (allowed_self, allowed_cross, distance)

def shard_sum(operands):
    running = None
    for left_side, right_side in operands:
        term = product('rk,kd->rd', left_side, right_side)
        running = term if running is None else running + term
    return running

def split_heads(values, head_count):
    return values.reshape(values.shape[0], head_count, values.shape[1] // head_count)

def attend(query, key_rows, value_rows, bias_block, allowed, head_count):
    query_heads = split_heads(query, head_count)
    key_heads = split_heads(key_rows, head_count)
    value_heads = split_heads(value_rows, head_count)
    scores = product('qhd,khd->hqk', query_heads, key_heads)
    if bias_block is not None:
        scores = scores + bias_block
    scores = jnp.where(allowed[None], scores, -1e+30)
    log_total = jnp.log(lax.optimization_barrier(jnp.sum(jnp.exp(scores), axis=-1, keepdims=True)))
    probs = jnp.exp(scores - log_total).astype(jnp.bfloat16)
    attended = product('hqk,khd->qhd', probs, value_heads)
    return (attended.reshape(query.shape[0], query.shape[1]).astype(jnp.bfloat16), log_total)

def attend_back(grad_attended, query, key_rows, value_rows, bias_block, allowed, log_total, attended, head_count):
    query_heads = split_heads(query, head_count)
    key_heads = split_heads(key_rows, head_count)
    value_heads = split_heads(value_rows, head_count)
    scores = product('qhd,khd->hqk', query_heads, key_heads)
    if bias_block is not None:
        scores = scores + bias_block
    scores = jnp.where(allowed[None], scores, -1e+30)
    probs = jnp.exp(scores - log_total)
    probs_low = probs.astype(jnp.bfloat16)
    grad_heads = split_heads(grad_attended, head_count)
    grad_values = product('hqk,qhd->khd', probs_low, grad_heads)
    grad_probs = product('qhd,khd->hqk', grad_heads, value_heads)
    delta = lax.optimization_barrier(jnp.sum(grad_heads.astype(jnp.float32) * split_heads(attended, head_count).astype(jnp.float32), axis=-1))
    grad_scores = probs * (grad_probs - delta.T[:, :, None])
    scores_low = grad_scores.astype(jnp.bfloat16)
    grad_query = product('hqk,khd->qhd', scores_low, key_heads)
    grad_keys = product('hqk,qhd->khd', scores_low, query_heads)
    grad_query = grad_query.reshape(query.shape).astype(jnp.bfloat16)
    grad_keys = grad_keys.reshape(key_rows.shape).astype(jnp.bfloat16)
    grad_values = grad_values.reshape(value_rows.shape).astype(jnp.bfloat16)
    return (grad_query, grad_keys, grad_values, grad_scores)

def layer_forward(hidden_in, enc_block, allowed_self, allowed_cross, bias_block, weights, reduce_sum):
    w_query, w_key, w_value, c_query, c_key, c_value, w_gate, w_up, w_out, c_out, w_down, gains = weights
    head_count = w_query.shape[1] // HEAD
    resid_zero = hidden_in.astype(jnp.float32)
    normed_one = rms_norm(resid_zero, gains[0]).astype(jnp.bfloat16)
    self_query = product('rd,di->ri', normed_one, w_query).astype(jnp.bfloat16)
    self_keys = product('rd,di->ri', normed_one, w_key).astype(jnp.bfloat16)
    self_values = product('rd,di->ri', normed_one, w_value).astype(jnp.bfloat16)
    self_out, self_lse = attend(self_query, self_keys, self_values, bias_block, allowed_self, head_count)
    resid_one = resid_zero + reduce_sum(((self_out, w_out),))
    normed_two = rms_norm(resid_one, gains[1]).astype(jnp.bfloat16)
    cross_query = product('rd,di->ri', normed_two, c_query).astype(jnp.bfloat16)
    cross_keys = product('ed,di->ei', enc_block, c_key).astype(jnp.bfloat16)
    cross_values = product('ed,di->ei', enc_block, c_value).astype(jnp.bfloat16)
    cross_out, cross_lse = attend(cross_query, cross_keys, cross_values, None, allowed_cross, head_count)
    resid_two = resid_one + reduce_sum(((cross_out, c_out),))
    normed_three = rms_norm(resid_two, gains[2]).astype(jnp.bfloat16)
    gate_pre = product('rd,df->rf', normed_three, w_gate)
    up_pre = product('rd,df->rf', normed_three, w_up)
    hidden = (gelu_tanh(gate_pre) * up_pre).astype(jnp.bfloat16)
    result = resid_two + reduce_sum(((hidden, w_down),))
    saved_state = (normed_one, self_query, self_keys, self_values, self_lse, self_out, resid_one, normed_two, cross_query, cross_keys, cross_values, cross_lse, cross_out, resid_two, normed_three, gate_pre, up_pre, hidden)
    return (result, saved_state)

def layer_backward(grad_out, hidden_in, enc_block, saved_state, allowed_self, allowed_cross, bias_block, distance, weights, reduce_sum):
    w_query, w_key, w_value, c_query, c_key, c_value, w_gate, w_up, w_out, c_out, w_down, gains = weights
    normed_one, self_query, self_keys, self_values, self_lse, self_out, resid_one, normed_two, cross_query, cross_keys, cross_values, cross_lse, cross_out, resid_two, normed_three, gate_pre, up_pre, hidden = saved_state
    head_count = w_query.shape[1] // HEAD
    resid_zero = hidden_in.astype(jnp.float32)
    grad_three_low = grad_out.astype(jnp.bfloat16)
    grad_down = product('rf,rd->fd', hidden, grad_three_low)
    grad_hidden = product('rd,fd->rf', grad_three_low, w_down)
    gelu_value, gelu_pull = jax.vjp(gelu_tanh, gate_pre)
    grad_gate_pre = gelu_pull(grad_hidden * up_pre)[0].astype(jnp.bfloat16)
    grad_up_pre = (grad_hidden * gelu_value).astype(jnp.bfloat16)
    grad_gate = product('rd,rf->df', normed_three, grad_gate_pre)
    grad_up = product('rd,rf->df', normed_three, grad_up_pre)
    grad_normed = reduce_sum(((grad_gate_pre, w_gate.T), (grad_up_pre, w_up.T)))
    back_three, gain_three = norm_back(resid_two, gains[2], grad_normed)
    grad_two = grad_out + back_three
    grad_two_low = grad_two.astype(jnp.bfloat16)
    grad_c_out = product('ri,rd->id', cross_out, grad_two_low)
    grad_cross = product('rd,id->ri', grad_two_low, c_out).astype(jnp.bfloat16)
    grad_cross_query, grad_cross_keys, grad_cross_values, _ = attend_back(grad_cross, cross_query, cross_keys, cross_values, None, allowed_cross, cross_lse, cross_out, head_count)
    grad_c_query = product('rd,ri->di', normed_two, grad_cross_query)
    grad_c_key = product('ed,ei->di', enc_block, grad_cross_keys)
    grad_c_value = product('ed,ei->di', enc_block, grad_cross_values)
    grad_enc = product('ei,di->ed', grad_cross_keys, c_key) + product('ei,di->ed', grad_cross_values, c_value)
    grad_normed = reduce_sum(((grad_cross_query, c_query.T),))
    back_two, gain_two = norm_back(resid_one, gains[1], grad_normed)
    grad_one = grad_two + back_two
    grad_one_low = grad_one.astype(jnp.bfloat16)
    grad_w_out = product('ri,rd->id', self_out, grad_one_low)
    grad_self = product('rd,id->ri', grad_one_low, w_out).astype(jnp.bfloat16)
    grad_query, grad_keys, grad_values, grad_scores = attend_back(grad_self, self_query, self_keys, self_values, bias_block, allowed_self, self_lse, self_out, head_count)
    grad_distance = jax.ops.segment_sum(grad_scores.reshape(head_count, -1).T, distance.reshape(-1), num_segments=MAXD)
    grad_w_query = product('rd,ri->di', normed_one, grad_query)
    grad_w_key = product('rd,ri->di', normed_one, grad_keys)
    grad_w_value = product('rd,ri->di', normed_one, grad_values)
    grad_normed = reduce_sum(((grad_query, w_query.T), (grad_keys, w_key.T), (grad_values, w_value.T)))
    back_one, gain_one = norm_back(resid_zero, gains[0], grad_normed)
    grad_input = grad_one + back_one
    grads = (grad_w_query, grad_w_key, grad_w_value, grad_c_query, grad_c_key, grad_c_value, grad_gate, grad_up, grad_w_out, grad_c_out, grad_down, jnp.stack([gain_one, gain_two, gain_three]), grad_distance)
    return (grad_input, grad_enc, grads)

def zero_grads(inner_width, hidden_width, head_count):
    return (jnp.zeros((D, inner_width), jnp.float32),) * 6 + (jnp.zeros((D, hidden_width), jnp.float32),) * 2 + (jnp.zeros((inner_width, D), jnp.float32),) * 2 + (jnp.zeros((hidden_width, D), jnp.float32), jnp.zeros((3, D), jnp.float32), jnp.zeros((MAXD, head_count), jnp.float32))

def forward_slot(weights, by_dist, slot_item):
    hidden_in, enc_block, dec_ids, enc_ids = slot_item
    allowed_self, allowed_cross, distance = build_masks(dec_ids, enc_ids)
    bias_block = jnp.take(by_dist, distance, axis=1)
    result, _ = layer_forward(hidden_in, enc_block, allowed_self, allowed_cross, bias_block, weights, shard_sum)
    return result.astype(jnp.bfloat16)

def backward_slot(weights, by_dist, carried, slot_item):
    hidden_in, enc_block, dec_ids, enc_ids, upstream = slot_item
    allowed_self, allowed_cross, distance = build_masks(dec_ids, enc_ids)
    bias_block = jnp.take(by_dist, distance, axis=1)
    _, saved_state = layer_forward(hidden_in, enc_block, allowed_self, allowed_cross, bias_block, weights, shard_sum)
    grad_input, grad_enc, grads = layer_backward(upstream, hidden_in, enc_block, saved_state, allowed_self, allowed_cross, bias_block, distance, weights, shard_sum)
    return (jax.tree.map(lambda a, b: a + b, carried, grads), (grad_input, grad_enc))

def reference(layer_input, enc_states, out_grad, dec_seg, enc_seg, buckets, sa_q, sa_k, sa_v, sa_o, ca_q, ca_k, ca_v, ca_o, ff_gate, ff_up, ff_down, norm_gains, rel_table):
    slot_count = ROWS // MB_TOK
    inputs_now = layer_input.reshape(MICRO, slot_count, MB_TOK, D)
    encoder = enc_states.reshape(MICRO, slot_count, ENC_TOK, D)
    dec_ids = dec_seg.reshape(MICRO, slot_count, MB_TOK)
    enc_ids = enc_seg.reshape(MICRO, slot_count, ENC_TOK)
    one_hot = bucket_table(buckets)
    section_weights = []
    section_bias = []
    for section_id in range(SECTIONS):
        section_weights.append((sa_q[section_id], sa_k[section_id], sa_v[section_id], ca_q[section_id], ca_k[section_id], ca_v[section_id], ff_gate[section_id], ff_up[section_id], sa_o[section_id], ca_o[section_id], ff_down[section_id], norm_gains[section_id].astype(jnp.float32)))
        section_bias.append(distance_bias(one_hot, rel_table[section_id]))
    section_inputs = []
    section_outputs = []
    for section_id in range(SECTIONS):
        runner = partial(forward_slot, section_weights[section_id], section_bias[section_id])
        outputs = jnp.stack([lax.map(runner, (inputs_now[micro_id], encoder[micro_id], dec_ids[micro_id], enc_ids[micro_id])) for micro_id in range(MICRO)])
        section_inputs.append(inputs_now)
        section_outputs.append(outputs)
        inputs_now = outputs
    cotangent = out_grad.reshape(MICRO, slot_count, MB_TOK, D).astype(jnp.float32)
    in_grads = [None] * SECTIONS
    enc_grads = [None] * SECTIONS
    all_grads = [None] * SECTIONS
    for section_id in reversed(range(SECTIONS)):
        runner = partial(backward_slot, section_weights[section_id], section_bias[section_id])
        carried = zero_grads(INNER, FF, HEADS)
        micro_inputs = []
        micro_enc = []
        for micro_id in range(MICRO):
            carried, (grad_input, grad_enc) = lax.scan(runner, carried, (section_inputs[section_id][micro_id], encoder[micro_id], dec_ids[micro_id], enc_ids[micro_id], cotangent[micro_id]))
            micro_inputs.append(grad_input)
            micro_enc.append(grad_enc)
        grad_stack = jnp.stack(micro_inputs)
        in_grads[section_id] = grad_stack.reshape(MICRO, ROWS, D)
        enc_grads[section_id] = jnp.stack(micro_enc).reshape(MICRO, ENC_ROWS, D)
        table_grad = jnp.dot(one_hot.T, carried[12], precision=lax.Precision.HIGHEST)
        all_grads[section_id] = carried[:12] + (table_grad,)
        cotangent = lax.optimization_barrier(grad_stack.astype(jnp.bfloat16)).astype(jnp.float32)
    stacked = [jnp.stack([all_grads[section_id][index] for section_id in range(SECTIONS)]) for index in range(13)]
    section_out = jnp.stack([outputs.reshape(MICRO, ROWS, D) for outputs in section_outputs])
    return (section_out, jnp.stack(in_grads), jnp.stack(enc_grads), stacked[0], stacked[1], stacked[2], stacked[8], stacked[3], stacked[4], stacked[5], stacked[9], stacked[6], stacked[7], stacked[10], stacked[11], stacked[12])
```

```python
import functools

import jax
import jax.numpy as jnp
from jax import lax
from jax.experimental import pallas as pl
from jax.experimental.pallas import tpu as pltpu
from jax.sharding import PartitionSpec as P

D = 768
HEAD = 64
BUCKETS = 32
MAXD = 128
EPS = 1e-06
AHEAD = 2

F32 = jnp.float32
BF16 = jnp.bfloat16
MESH = pl.DeviceIdType.MESH


def dot_nn(a, b):
    return lax.dot_general(a, b, (((1,), (0,)), ((), ())), preferred_element_type=F32)


def dot_nt(a, b):
    return lax.dot_general(a, b, (((1,), (1,)), ((), ())), preferred_element_type=F32)


def dot_tn(a, b):
    return lax.dot_general(a, b, (((0,), (0,)), ((), ())), preferred_element_type=F32)


def norm_scale(values):
    return lax.rsqrt(jnp.mean(values * values, axis=-1, keepdims=True) + EPS)


def norm_back(values, gain, cotangent):
    scale = norm_scale(values)
    scaled = cotangent * gain
    inner = jnp.mean(scaled * values, axis=-1, keepdims=True)
    back = scale * scaled - values * (scale * scale * scale * inner)
    gain_grad = jnp.sum(cotangent * values * scale, axis=0, keepdims=True)
    return back, gain_grad


def gelu_parts(u):
    root = 0.7978845608028654
    cube = 0.044715
    t = jnp.tanh(root * (u + cube * u * u * u))
    value = 0.5 * u * (1.0 + t)
    slope = 0.5 * (1.0 + t) + 0.5 * u * (1.0 - t * t) * (root * (1.0 + 3.0 * cube * u * u))
    return value, slope


def head_masks(heads):
    lane = lax.broadcasted_iota(jnp.int32, (1, heads * HEAD), 1)
    return [
        ((lane >= h * HEAD) & (lane < (h + 1) * HEAD)).astype(F32).astype(BF16)
        for h in range(heads)
    ]


def spread_heads(values, masks):
    return jnp.concatenate([values * m for m in masks], axis=0)


def join_heads(values, masks):
    rows = values.shape[0] // len(masks)
    total = None
    for h, m in enumerate(masks):
        term = values[h * rows : (h + 1) * rows] * m.astype(F32)
        total = term if total is None else total + term
    return total


def each(low, high, run):
    if high - low <= 4:
        for k in range(low, high):
            run(k)
    else:
        lax.fori_loop(low, high, lambda k, c: (run(k), c)[1], 0)


def layout(inner, ff):
    sa, ca = 3 * ff, 3 * ff + 4 * inner
    sent = ((sa, 4 * inner), (ca, 4 * inner), (0, 2 * ff), (2 * ff, ff))
    summed = ((0, 3 * ff), (ca, 4 * inner), (sa, 4 * inner))
    return sent, summed


def main_kernel(
    dims,
    h_ref,
    enc_ref,
    up_ref,
    dec_ref,
    seg_ref,
    buck_ref,
    wq_ref,
    wk_ref,
    wv_ref,
    wo_ref,
    cq_ref,
    ck_ref,
    cv_ref,
    co_ref,
    gate_ref,
    upw_ref,
    down_ref,
    gain_ref,
    tab_ref,
    sum_out,
    sect_out,
    ingrad_out,
    enc_out,
    small_out,
    w_ref,
    small_w,
    gains_s,
    bias_s,
    bmap_s,
    x_in,
    g_in,
    r_one,
    r_two,
    n_one,
    n_two,
    n_three,
    qkv_s,
    so_s,
    p_s,
    cq_s,
    ckv_s,
    co_s,
    pc_s,
    gu_s,
    hid_s,
    send_one,
    recv_one,
    send_two,
    recv_two,
    enc_send,
    enc_own,
    enc_recv,
    grad_s,
    swap_s,
    part_s,
    relay_s,
    total_s,
    ingrad_s,
    table_s,
    small_g,
    sem_send,
    sem_recv,
    sem_enc_send,
    sem_enc_recv,
    sem_own_send,
    sem_own_recv,
    sem_z_send,
    sem_z_recv,
    sem_p_send,
    sem_p_recv,
    sem_sw_send,
    sem_sw_recv,
    sem_g_send,
    sem_g_recv,
    sem_r_recv,
    sem_f_send,
    sem_f_recv,
    sem_o_send,
    sem_o_recv,
    sem_sm_send,
    sem_sm_recv,
    sem_sg_send,
    sem_sg_recv,
):
    layers, dp, rows, inner, ff, heads, chunk, table_rows = dims
    half = rows // 2
    p = lax.axis_index("pipe")
    o = 1 - p
    g = lax.axis_index("dp")
    t = lax.axis_index("tensor")
    near = t + 1 - 2 * (t % 2)
    far = t + 2 - 4 * ((t // 2) % 2)
    both = far + 1 - 2 * (far % 2)
    peers = (near, far, both)
    way = 1 - 2 * (g // ((dp + 1) // 2))
    line = dp == 4
    masks = head_masks(heads)
    c_q = 3 * ff
    c_so = c_q + 3 * inner
    c_cq = c_q + 4 * inner
    c_ck = c_q + 5 * inner
    c_cv = c_q + 6 * inner
    c_co = c_q + 7 * inner
    c_end = c_q + 8 * inner
    sent, summed = layout(inner, ff)
    offsets = (0, summed[0][1] // 2, (summed[0][1] + summed[1][1]) // 2)

    barrier = pltpu.get_barrier_semaphore()

    def greet(ids):
        pl.semaphore_signal(barrier, inc=1, device_id=ids, device_id_type=MESH)

    for peer in peers:
        greet({"tensor": peer})
    greet({"pipe": o})

    def greet_group(k):
        s = lax.rem(g + k, dp)
        greet({"dp": s})
        greet({"dp": s, "pipe": o})

    each(1, dp, greet_group)

    def copy_to(src, dst, sem_a, sem_b, ids):
        return pltpu.make_async_remote_copy(
            src_ref=src,
            dst_ref=dst,
            send_sem=sem_a,
            recv_sem=sem_b,
            device_id=ids,
            device_id_type=MESH,
        )

    def other(k):
        return lax.rem(g + dp + way * k, dp)

    def pack(c, value):
        a, n = sent[c]
        w_ref[p, g, :, a : a + n] = value

    small_w[p, g] = jnp.zeros(small_w.shape[2:], F32)
    small_w[p, g, 0:3, 0:chunk] = gain_ref[...].astype(F32)
    small_w[p, g, 8 : 8 + table_rows, 0:heads] = tab_ref[...].astype(F32)
    pack(
        0, jnp.concatenate([wq_ref[...], wk_ref[...], wv_ref[...], wo_ref[...].T], axis=1)
    )
    pl.semaphore_wait(barrier, 3 + 1 + 2 * (dp - 1))

    def small_copy(ids, src_p, src_g, k, way_p):
        view = small_w.at[src_p, src_g]
        return copy_to(
            view, view, sem_sm_send.at[way_p, k], sem_sm_recv.at[src_p, src_g], ids
        )

    small_copy({"pipe": o}, p, g, 0, 1).start()

    def small_start(k):
        small_copy({"dp": other(k)}, p, g, k, 0).start()
        small_copy({"dp": other(k), "pipe": o}, p, g, k, 1).start()

    each(1, dp, small_start)

    def own_copy(c):
        a, n = sent[c]
        return copy_to(
            w_ref.at[p, g, :, a : a + n],
            w_ref.at[p, g, :, a : a + n],
            sem_own_send.at[c],
            sem_own_recv.at[c],
            {"pipe": o},
        )

    def own_arrival(c):
        a, n = sent[c]
        view = w_ref.at[o, g, :, a : a + n]
        copy_to(view, view, sem_own_send.at[c], sem_own_recv.at[c], {"pipe": o}).wait_recv()

    def view_of(l, c, s, side):
        a, n = sent[c]
        width = n // 2
        return w_ref.at[l, s, :, pl.ds(pl.multiple_of(a + side * width, 128), width)]

    def z_copy(l, c, s, target, sem):
        view = view_of(l, c, s, p)
        return copy_to(
            view, view, sem_z_send.at[l, c, sem], sem_z_recv.at[l, c, s], {"dp": target}
        )

    def p_copy(l, c, s, side):
        view = view_of(l, c, s, side)
        return copy_to(view, view, sem_p_send.at[l, c, s], sem_p_recv.at[l, c, s], {"pipe": o})

    def far_apart(a, b):
        return jnp.abs(a - b) == dp - 1

    def unless_relayed(s, run):
        if line:
            pl.when(jnp.logical_not(far_apart(g, s)))(run)
        else:
            run()

    def issue(l, c):
        @pl.when(l != p)
        def _():
            own_arrival(c)

        def start(k):
            s = other(dp - k)
            unless_relayed(s, lambda: z_copy(l, c, g, s, s).start())

        each(1, dp, start)

    def relays(s, run):
        if line:
            inside = (g == 1) | (g == 2)
            pl.when(inside & (s == lax.rem(g + 2, dp)))(run)

    def poll(l, c):
        def arrive(k):
            s = other(k)
            z_copy(l, c, s, s, s).wait_recv()
            relays(s, lambda: z_copy(l, c, s, dp - 1 - s, g).start())
            p_copy(l, c, s, p).start()

        each(1, dp, arrive)
        each(1, dp, lambda k: p_copy(l, c, other(k), o).wait_recv())

    own_copy(0).start()
    pack(
        1, jnp.concatenate([cq_ref[...], ck_ref[...], cv_ref[...], co_ref[...].T], axis=1)
    )
    own_copy(1).start()
    issue(0, 0)
    pack(2, jnp.concatenate([gate_ref[...], upw_ref[...]], axis=1))
    own_copy(2).start()
    pack(3, down_ref[...].T)
    own_copy(3).start()
    for c in range(1, AHEAD):
        issue(0, c)

    def issue_after(l, c):
        nl, nc = l + (c + AHEAD) // 4, (c + AHEAD) % 4
        if nc == c + AHEAD:
            issue(nl, nc)
        else:

            @pl.when(nl < layers)
            def _():
                issue(nl, nc)

    ri = lax.broadcasted_iota(jnp.int32, (rows, rows), 0)
    ci = lax.broadcasted_iota(jnp.int32, (rows, rows), 1)
    dec_row = dec_ref[pl.ds(p, 1), :].astype(F32)
    enc_row = seg_ref[pl.ds(p, 1), :].astype(F32)
    dec_col = jnp.sum(jnp.where(ri == ci, dec_row, 0.0), axis=1, keepdims=True)
    allowed = (dec_col == dec_row) & (ci <= ri)
    cmask = jnp.where(dec_col == enc_row, 0.0, -1e30)
    bi = lax.broadcasted_iota(jnp.int32, (BUCKETS, MAXD), 0)
    starts = jnp.sum(jnp.where(buck_ref[...] < bi, 1.0, 0.0), axis=1, keepdims=True)
    dist = jnp.clip(ri - ci, 0, MAXD - 1).astype(F32)
    bmap = jnp.zeros((rows, rows), F32)
    for b in range(1, BUCKETS):
        bmap = bmap + jnp.where(dist >= starts[b : b + 1], 1.0, 0.0)
    bmap_s[...] = bmap

    def small_arrive(k):
        s = other(k)
        small_copy({"dp": s}, p, s, k, 0).wait_recv()
        small_copy({"dp": s}, o, s, k, 0).wait_recv()

    each(1, dp, small_arrive)
    small_copy({"pipe": o}, o, g, 0, 1).wait_recv()
    for l in range(layers):
        for n in range(3):
            gains_s[l, n : n + 1] = jnp.concatenate(
                [small_w[l, s, n : n + 1, 0:chunk] for s in range(dp)], axis=1
            )
        for h in range(heads):
            bias = jnp.zeros((rows, rows), F32)
            for b in range(BUCKETS):
                r = 8 + b % table_rows
                value = small_w[l, b // table_rows, r : r + 1, h : h + 1]
                bias = jnp.where(bmap == float(b), value, bias)
            bias_s[l, h * rows : (h + 1) * rows] = jnp.where(allowed, bias, -1e30)

    def weights(l, a, b):
        return w_ref[l, :, :, a:b].reshape(D, b - a)

    def first_copy(slot, part):
        return copy_to(
            send_one.at[slot, part],
            recv_one.at[slot, part],
            sem_send.at[slot, part],
            sem_recv.at[slot, part],
            {"tensor": near if part == 0 else far},
        )

    def second_copy(slot, part):
        return copy_to(
            send_two.at[slot, part],
            recv_two.at[slot, part],
            sem_send.at[slot, part + 2],
            sem_recv.at[slot, part + 2],
            {"tensor": far if part == 0 else near},
        )

    def sum_start(slot, make_half):
        for part in range(2):
            send_one[slot, part] = make_half(part).astype(BF16)
            first_copy(slot, part).start()

    def sum_middle(slot):
        for part in range(2):
            first_copy(slot, part).wait()
            value = send_one[slot, part].astype(F32) + recv_one[slot, part].astype(F32)
            send_two[slot, part] = value.astype(BF16)
            second_copy(slot, part).start()

    def sum_end(slot):
        pieces = []
        for part in range(2):
            second_copy(slot, part).wait()
            pieces.append(send_two[slot, part].astype(F32) + recv_two[slot, part].astype(F32))
        return jnp.concatenate(pieces, axis=0)

    def all_sum(slot, make_half, cover=None, later=None):
        sum_start(slot, make_half)
        if cover is not None:
            cover()
        sum_middle(slot)
        if later is not None:
            later()
        return sum_end(slot)

    x_in[0] = h_ref[p]
    enc = enc_ref[p]

    def make_result(l):
        def make_three(part):
            return dot_nt(
                hid_s[l, part * half : (part + 1) * half], weights(l, 2 * ff, 3 * ff)
            )

        return make_three

    def forward(l, carry):
        poll(l, 0)
        issue_after(l, 0)
        x0 = x_in[l].astype(F32)
        n1 = (x0 * norm_scale(x0) * gains_s[l, 0:1]).astype(BF16)
        n_one[l] = n1
        qkv = dot_nn(n1, weights(l, c_q, c_so)).astype(BF16)
        qkv_s[l] = qkv
        q = qkv[:, :inner]
        k = qkv[:, inner : 2 * inner]
        v = qkv[:, 2 * inner :]
        e = jnp.exp(dot_nt(spread_heads(q, masks), k) + bias_s[l])
        prob = e * (1.0 / jnp.sum(e, axis=-1, keepdims=True))
        p_s[l] = prob
        so_s[l] = join_heads(dot_nn(prob.astype(BF16), v), masks).astype(BF16)

        def make_one(part):
            return dot_nt(so_s[l, part * half : (part + 1) * half], weights(l, c_so, c_cq))

        def cover_one():
            poll(l, 1)
            issue_after(l, 1)
            ckv_s[l] = dot_nn(enc, weights(l, c_ck, c_co)).astype(BF16)

        x1 = x0 + all_sum(3 * l, make_one, cover_one)
        r_one[l] = x1
        n2 = (x1 * norm_scale(x1) * gains_s[l, 1:2]).astype(BF16)
        n_two[l] = n2
        cq = dot_nn(n2, weights(l, c_cq, c_ck)).astype(BF16)
        cq_s[l] = cq
        ckv = ckv_s[l]
        ck = ckv[:, :inner]
        cv = ckv[:, inner:]
        e = jnp.exp(
            dot_nt(spread_heads(cq, masks), ck) + jnp.concatenate([cmask] * heads, axis=0)
        )
        prob = e * (1.0 / jnp.sum(e, axis=-1, keepdims=True))
        pc_s[l] = prob
        co_s[l] = join_heads(dot_nn(prob.astype(BF16), cv), masks).astype(BF16)

        def make_two(part):
            return dot_nt(co_s[l, part * half : (part + 1) * half], weights(l, c_co, c_end))

        def cover_two():
            poll(l, 2)
            issue_after(l, 2)

        x2 = x1 + all_sum(3 * l + 1, make_two, None, cover_two)
        r_two[l] = x2
        n3 = (x2 * norm_scale(x2) * gains_s[l, 2:3]).astype(BF16)
        n_three[l] = n3
        gu = dot_nn(n3, weights(l, 0, 2 * ff))
        gu_s[l] = gu
        value, _ = gelu_parts(gu[:, :ff])
        hid_s[l] = (value * gu[:, ff:]).astype(BF16)
        poll(l, 3)
        issue_after(l, 3)

        @pl.when(l < layers - 1)
        def _():
            x_in[l + 1] = (x2 + all_sum(3 * l + 2, make_result(l))).astype(BF16)

        return carry

    lax.fori_loop(0, layers, forward, 0)
    last = 3 * layers - 1
    sum_start(last, make_result(layers - 1))
    g_in[...] = up_ref[p]

    def attend_back(grad, query, keys, values, attended, prob):
        gs = spread_heads(grad, masks)
        qs = spread_heads(query, masks)
        delta = jnp.sum(
            gs.astype(F32) * jnp.concatenate([attended.astype(F32)] * heads, axis=0),
            axis=-1,
            keepdims=True,
        )
        ds = prob * (dot_nt(gs, values) - delta)
        dsb = ds.astype(BF16)
        grad_query = join_heads(dot_nn(dsb, keys), masks).astype(BF16)
        return grad_query, ds, dsb, gs, qs

    def keep(l, r, value):
        width = summed[r][1] // 2
        for side in range(2):
            grad_s[l, side, :, :, offsets[r] : offsets[r] + width] = (
                value[:, side * width : (side + 1) * width].astype(BF16).reshape(dp, chunk, width)
            )

    def columns(r):
        return pl.ds(offsets[r], summed[r][1] // 2)

    def swap_copy(l, r):
        return copy_to(
            grad_s.at[l, o, :, :, columns(r)],
            swap_s.at[l, :, :, columns(r)],
            sem_sw_send.at[l, r],
            sem_sw_recv.at[l, r],
            {"pipe": o},
        )

    def slot_of(source, owner):
        return lax.rem(source - owner + dp, dp) - 1

    def piece_copy(l, r, s):
        return copy_to(
            grad_s.at[l, p, s, :, columns(r)],
            part_s.at[l, slot_of(g, s), :, columns(r)],
            sem_g_send.at[l, r, s],
            sem_g_recv.at[l, r, g],
            {"dp": s},
        )

    def relay_copy(l, r, s):
        return copy_to(
            grad_s.at[l, p, s, :, columns(r)],
            relay_s.at[l, :, columns(r)],
            sem_g_send.at[l, r, s],
            sem_r_recv.at[l, r],
            {"dp": g + 1 - 2 * (g // 2)},
        )

    def piece_arrival(l, r, s):
        return copy_to(
            grad_s.at[l, p, g, :, columns(r)],
            part_s.at[l, slot_of(s, g), :, columns(r)],
            sem_g_send.at[l, r, s],
            sem_g_recv.at[l, r, s],
            {"dp": s},
        )

    def is_inside():
        return (g == 1) | (g == 2)

    def send_pieces(l, r):
        swap_copy(l, r).wait_recv()

        def merge(s):
            grad_s[l, p, s, :, columns(r)] = (
                grad_s[l, p, s, :, columns(r)].astype(F32)
                + swap_s[l, s, :, columns(r)].astype(F32)
            ).astype(BF16)

        each(0, dp, merge)

        def start(k):
            s = other(dp - k)
            if not line:
                piece_copy(l, r, s).start()
                return

            @pl.when(far_apart(g, s))
            def _():
                relay_copy(l, r, s).start()

            @pl.when(jnp.abs(g - s) == 1)
            def _():
                piece_copy(l, r, s).start()

            @pl.when((jnp.abs(g - s) == 2) & jnp.logical_not(is_inside()))
            def _():
                piece_copy(l, r, s).start()

        each(1, dp, start)

    def pass_on(l, r):
        if not line:
            return

        @pl.when(is_inside())
        def _():
            s = lax.rem(g + 2, dp)
            relay_copy(l, r, s).wait_recv()
            grad_s[l, p, s, :, columns(r)] = (
                grad_s[l, p, s, :, columns(r)].astype(F32) + relay_s[l, :, columns(r)].astype(F32)
            ).astype(BF16)
            piece_copy(l, r, s).start()

    def total_of(l, r):
        total_s[l, :, columns(r)] = grad_s[l, p, g, :, columns(r)].astype(F32)

        def add(k):
            s = other(k)

            def run():
                piece_arrival(l, r, s).wait_recv()
                total_s[l, :, columns(r)] = total_s[l, :, columns(r)] + part_s[
                    l, slot_of(s, g), :, columns(r)
                ].astype(F32)

            unless_relayed(s, run)

        each(1, dp, add)

    def backward(step, carry):
        l = layers - 1 - step
        base = 3 * layers + 3 * step
        g3 = g_in[...]
        gf = g3.astype(F32)
        gu = gu_s[l]
        value, slope = gelu_parts(gu[:, :ff])
        dh = dot_nn(g3, weights(l, 2 * ff, 3 * ff))
        dgu = jnp.concatenate(
            [(dh * gu[:, ff:] * slope).astype(BF16), (dh * value).astype(BF16)], axis=1
        )

        def make_three(part):
            return dot_nt(dgu[part * half : (part + 1) * half], weights(l, 0, 2 * ff))

        def cover_three():
            keep(
                l, 0, jnp.concatenate([dot_tn(n_three[l], dgu), dot_tn(g3, hid_s[l])], axis=1)
            )
            swap_copy(l, 0).start()

            @pl.when(step == 0)
            def _():
                sum_middle(last)

            @pl.when(step > 0)
            def _():
                pass_on(l + 1, 1)

        dn = all_sum(base, make_three, cover_three, lambda: send_pieces(l, 0))
        back, gain_three = norm_back(r_two[l], gains_s[l, 2:3], dn)
        g2 = gf + back
        g2b = g2.astype(BF16)
        dc = dot_nn(g2b, weights(l, c_co, c_end)).astype(BF16)
        ckv = ckv_s[l]
        co = co_s[l]
        pc = pc_s[l]
        dcq, _, dsb, gs, qs = attend_back(dc, cq_s[l], ckv[:, :inner], ckv[:, inner:], co, pc)

        def make_two(part):
            return dot_nt(dcq[part * half : (part + 1) * half], weights(l, c_cq, c_ck))

        def cover_two():
            dck = dot_tn(dsb, qs).astype(BF16)
            dcv = dot_tn(pc.astype(BF16), gs).astype(BF16)
            dckv = jnp.concatenate([dck, dcv], axis=1)
            blocks = inner // chunk
            for k in range(D // inner):
                owner = t if k == 0 else peers[k - 1]
                rows_of = w_ref[l, pl.ds(owner * blocks, blocks), :, c_ck:c_co]
                part = dot_nt(dckv, rows_of.reshape(inner, 2 * inner))
                if k == 0:
                    enc_own[l] = part
                else:
                    enc_send[l, k - 1] = part.astype(BF16)
                    enc_copy(l, k - 1).start()
            keep(
                l,
                1,
                jnp.concatenate(
                    [dot_tn(n_two[l], dcq), dot_tn(enc, dckv), dot_tn(g2b, co)], axis=1
                ),
            )
            swap_copy(l, 1).start()

            @pl.when(step == 0)
            def _():
                x_in[layers] = (r_two[layers - 1] + sum_end(last)).astype(BF16)

            @pl.when(step > 0)
            def _():
                pass_on(l + 1, 2)

        dn = all_sum(base + 1, make_two, cover_two, lambda: send_pieces(l, 1))
        back, gain_two = norm_back(r_one[l], gains_s[l, 1:2], dn)
        g1 = g2 + back
        g1b = g1.astype(BF16)
        dself = dot_nn(g1b, weights(l, c_so, c_cq)).astype(BF16)
        qkv = qkv_s[l]
        so = so_s[l]
        ps = p_s[l]
        dq, ds, dsb, gs, qs = attend_back(
            dself, qkv[:, :inner], qkv[:, inner : 2 * inner], qkv[:, 2 * inner :], so, ps
        )
        dk = dot_tn(dsb, qs).astype(BF16)
        dv = dot_tn(ps.astype(BF16), gs).astype(BF16)
        dqkv = jnp.concatenate([dq, dk, dv], axis=1)

        def make_one(part):
            return dot_nt(dqkv[part * half : (part + 1) * half], weights(l, c_q, c_so))

        def cover_one():
            keep(l, 2, jnp.concatenate([dot_tn(n_one[l], dqkv), dot_tn(g1b, so)], axis=1))
            swap_copy(l, 2).start()

        def later_one():
            send_pieces(l, 2)
            pass_on(l, 0)
            buckets = bmap_s[...]
            for h in range(heads):
                ds_h = ds[h * rows : (h + 1) * rows]
                for b in range(BUCKETS):
                    table_s[h, b : b + 1] = jnp.sum(
                        jnp.where(buckets == float(b), ds_h, 0.0), axis=0, keepdims=True
                    )

        dn = all_sum(base + 2, make_one, cover_one, later_one)
        back, gain_one = norm_back(x_in[l].astype(F32), gains_s[l, 0:1], dn)
        gin = g1 + back
        ingrad_s[l] = gin
        g_in[...] = gin.astype(BF16)
        small_g[l] = jnp.zeros(small_g.shape[1:], F32)
        table = jnp.concatenate(
            [jnp.sum(table_s[h], axis=1, keepdims=True) for h in range(heads)], axis=1
        )
        for s in range(dp):
            for n, value in enumerate((gain_one, gain_two, gain_three)):
                small_g[l, s, n : n + 1, 0:chunk] = value[:, s * chunk : (s + 1) * chunk]
            small_g[l, s, 8 : 8 + table_rows, 0:heads] = table[
                s * table_rows : (s + 1) * table_rows
            ]
        return carry

    def enc_copy(l, k):
        return copy_to(
            enc_send.at[l, k],
            enc_recv.at[l, k],
            sem_enc_send.at[l, k],
            sem_enc_recv.at[l, k],
            {"tensor": peers[k]},
        )

    lax.fori_loop(0, layers, backward, 0)

    def grad_small_copy(l, s, src_p, src_g, ids):
        return copy_to(
            small_g.at[l, s],
            small_out.at[src_p, src_g],
            sem_sg_send.at[l, s],
            sem_sg_recv.at[src_p, src_g],
            ids,
        )

    small_out[p, g] = small_g[p, g]
    grad_small_copy(o, g, p, g, {"pipe": o}).start()

    def grad_small_start(k):
        s = other(k)
        grad_small_copy(p, s, p, g, {"dp": s}).start()
        grad_small_copy(o, s, p, g, {"dp": s, "pipe": o}).start()

    each(1, dp, grad_small_start)
    pass_on(0, 1)
    pass_on(0, 2)

    for l in range(layers):
        total = enc_own[l]
        for k in range(3):
            enc_copy(l, k).wait()
            total = total + enc_recv[l, k].astype(F32)
        enc_own[l] = total

    moved = (
        (x_in.at[o + 1], sect_out.at[p]),
        (ingrad_s.at[o], ingrad_out.at[p]),
        (enc_own.at[o], enc_out.at[p]),
    )

    def moved_copy(n):
        src, dst = moved[n]
        return copy_to(src, dst, sem_o_send.at[n], sem_o_recv.at[n], {"pipe": o})

    for n in range(3):
        moved_copy(n).start()
    sect_out[p] = x_in[p + 1]
    ingrad_out[p] = ingrad_s[p]
    enc_out[p] = enc_own[p]

    def final_copy(r):
        return copy_to(
            total_s.at[o, :, columns(r)],
            sum_out.at[p, :, columns(r)],
            sem_f_send.at[r],
            sem_f_recv.at[r],
            {"pipe": o},
        )

    for r in range(3):
        for l in reversed(range(layers)):
            total_of(l, r)
        sum_out[p, :, columns(r)] = total_s[p, :, columns(r)]
        final_copy(r).start()

    def arrival(view, sem):
        copy_to(view, view, sem, sem, {"pipe": o}).wait_recv()

    for r in range(3):
        final_copy(r).wait_send()
        arrival(sum_out.at[o, :, columns(r)], sem_f_recv.at[r])
    for n in range(3):
        moved_copy(n).wait_send()
        arrival(moved[n][1], sem_o_recv.at[n])
    grad_small_copy(o, g, p, g, {"pipe": o}).wait_send()
    grad_small_copy(o, g, o, g, {"pipe": o}).wait_recv()

    def grad_small_end(k):
        s = other(k)
        grad_small_copy(p, s, p, g, {"dp": s}).wait_send()
        grad_small_copy(o, s, p, g, {"dp": s}).wait_send()
        grad_small_copy(p, s, p, s, {"dp": s}).wait_recv()
        grad_small_copy(o, s, o, s, {"dp": s}).wait_recv()

    each(1, dp, grad_small_end)
    small_copy({"pipe": o}, p, g, 0, 1).wait_send()

    def small_end(k):
        small_copy({"dp": other(k)}, p, g, k, 0).wait_send()
        small_copy({"dp": other(k)}, p, g, k, 1).wait_send()

    each(1, dp, small_end)
    for c in range(4):
        own_copy(c).wait_send()

    def layer_end(l, carry):
        for c in range(4):

            def sent_end(k):
                s = other(k)
                unless_relayed(s, lambda: z_copy(l, c, g, s, s).wait_send())
                relays(s, lambda: z_copy(l, c, s, dp - 1 - s, g).wait_send())
                p_copy(l, c, s, p).wait_send()

            each(1, dp, sent_end)
        for r in range(3):
            swap_copy(l, r).wait_send()
            each(1, dp, lambda k: piece_copy(l, r, other(k)).wait_send())
        return carry

    lax.fori_loop(0, layers, layer_end, 0)


def run_main(inputs, layers, dp):
    h, enc, wq, gate, table = inputs[0], inputs[1], inputs[6], inputs[14], inputs[18]
    rows, enc_rows = h.shape[1], enc.shape[1]
    chunk, inner, ff = wq.shape[0], wq.shape[1], gate.shape[1]
    heads, table_rows = inner // HEAD, table.shape[0]
    half = rows // 2
    slots = 6 * layers
    width = 3 * ff + 8 * inner
    small = (16, -(-chunk // 128) * 128)
    vm = pltpu.VMEM
    dma = pltpu.SemaphoreType.DMA
    dims = (layers, dp, rows, inner, ff, heads, chunk, table_rows)
    return pl.pallas_call(
        functools.partial(main_kernel, dims),
        out_shape=(
            jax.ShapeDtypeStruct((2, chunk, width // 2), F32),
            jax.ShapeDtypeStruct((2, rows, D), BF16),
            jax.ShapeDtypeStruct((2, rows, D), F32),
            jax.ShapeDtypeStruct((2, enc_rows, inner), F32),
            jax.ShapeDtypeStruct((2, dp) + small, F32),
        ),
        in_specs=[pl.BlockSpec(memory_space=pltpu.VMEM)] * 19,
        out_specs=(pl.BlockSpec(memory_space=pltpu.VMEM),) * 5,
        scratch_shapes=[
            vm((layers, dp, chunk, width), BF16),
            vm((layers, dp) + small, F32),
            vm((layers, 8, D), F32),
            vm((layers, heads * rows, rows), F32),
            vm((rows, rows), F32),
            vm((layers + 1, rows, D), BF16),
            vm((rows, D), BF16),
            vm((layers, rows, D), F32),
            vm((layers, rows, D), F32),
            vm((layers, rows, D), BF16),
            vm((layers, rows, D), BF16),
            vm((layers, rows, D), BF16),
            vm((layers, rows, 3 * inner), BF16),
            vm((layers, rows, inner), BF16),
            vm((layers, heads * rows, rows), F32),
            vm((layers, rows, inner), BF16),
            vm((layers, enc_rows, 2 * inner), BF16),
            vm((layers, rows, inner), BF16),
            vm((layers, heads * rows, enc_rows), F32),
            vm((layers, rows, 2 * ff), F32),
            vm((layers, rows, ff), BF16),
            vm((slots, 2, half, D), BF16),
            vm((slots, 2, half, D), BF16),
            vm((slots, 2, half, D), BF16),
            vm((slots, 2, half, D), BF16),
            vm((layers, 3, enc_rows, inner), BF16),
            vm((layers, enc_rows, inner), F32),
            vm((layers, 3, enc_rows, inner), BF16),
            vm((layers, 2, dp, chunk, width // 2), BF16),
            vm((layers, dp, chunk, width // 2), BF16),
            vm((layers, dp - 1, chunk, width // 2), BF16),
            vm((layers, chunk, width // 2), BF16),
            vm((layers, chunk, width // 2), F32),
            vm((layers, rows, D), F32),
            vm((heads, BUCKETS, rows), F32),
            vm((layers, dp) + small, F32),
            dma((slots, 4)),
            dma((slots, 4)),
            dma((layers, 3)),
            dma((layers, 3)),
            dma((4,)),
            dma((4,)),
            dma((layers, 4, dp)),
            dma((layers, 4, dp)),
            dma((layers, 4, dp)),
            dma((layers, 4, dp)),
            dma((layers, 3)),
            dma((layers, 3)),
            dma((layers, 3, dp)),
            dma((layers, 3, dp)),
            dma((layers, 3)),
            dma((3,)),
            dma((3,)),
            dma((3,)),
            dma((3,)),
            dma((2, dp)),
            dma((2, dp)),
            dma((2, dp)),
            dma((2, dp)),
        ],
        compiler_params=pltpu.CompilerParams(
            collective_id=0, has_side_effects=True, vmem_limit_bytes=60 * 1024 * 1024
        ),
    )(*inputs)


def finish_kernel(dims, *refs):
    inner, ff, heads, chunk, table_rows = dims
    sum_ref, sect_ref, ingrad_ref, enc_ref, small_ref = refs[:5]
    (sect_out, ingrad_out, enc_out, q_out, k_out, v_out, o_out, cq_out, ck_out, cv_out) = refs[5:15]
    co_out, gate_out, up_out, down_out, gain_out, tab_out = refs[15:]
    _, summed = layout(inner, ff)

    def take(a, n):
        offset = 0
        for start, width in summed:
            if start <= a < start + width:
                pieces = []
                for side in range(2):
                    low = max(a, start + side * (width // 2))
                    high = min(a + n, start + (side + 1) * (width // 2))
                    if low < high:
                        at = offset + low - start - side * (width // 2)
                        pieces.append(sum_ref[side, :, at : at + high - low])
                return pieces[0] if len(pieces) == 1 else jnp.concatenate(pieces, axis=1)
            offset += width // 2

    sect_out[...] = sect_ref[...]
    ingrad_out[...] = ingrad_ref[...]
    enc_out[...] = enc_ref[...]
    c = 3 * ff
    for n, out in enumerate((q_out, k_out, v_out, o_out, cq_out, ck_out, cv_out, co_out)):
        value = take(c + n * inner, inner)
        out[...] = value.T if n % 4 == 3 else value
    gate_out[...] = take(0, ff)
    up_out[...] = take(ff, ff)
    down_out[...] = take(2 * ff, ff).T
    small = jnp.sum(small_ref[...], axis=(0, 1))
    gain_out[...] = small[0:3, 0:chunk]
    tab_out[...] = small[8 : 8 + table_rows, 0:heads]


def run_finish(parts, inner, ff, chunk, table_rows):
    heads = inner // HEAD
    _, sect, ingrad, enc, _ = parts
    into, outer = (chunk, inner), (inner, chunk)
    shapes = [sect.shape, ingrad.shape, enc.shape]
    shapes += [into, into, into, outer] * 2
    shapes += [(chunk, ff), (chunk, ff), (ff, chunk), (3, chunk), (table_rows, heads)]
    types = [BF16] + [F32] * 15
    return pl.pallas_call(
        functools.partial(finish_kernel, (inner, ff, heads, chunk, table_rows)),
        out_shape=tuple(jax.ShapeDtypeStruct(s, d) for s, d in zip(shapes, types)),
        in_specs=[pl.BlockSpec(memory_space=pltpu.VMEM)] * 5,
        out_specs=(pl.BlockSpec(memory_space=pltpu.VMEM),) * 16,
        compiler_params=pltpu.CompilerParams(vmem_limit_bytes=32 * 1024 * 1024),
    )(*parts)


def body(*args):
    layers = lax.axis_size("pipe")
    dp = lax.axis_size("dp")
    inputs = list(args[:5]) + [args[5].reshape(1, -1)] + [value[0] for value in args[6:]]
    chunk, inner = inputs[6].shape
    ff, table_rows = inputs[14].shape[1], inputs[18].shape[0]
    parts = run_main(inputs, layers, dp)
    outs = run_finish(parts, inner, ff, chunk, table_rows)
    return tuple(value[None] for value in outs)


def solution(mesh):
    inner_spec = P("pipe", "dp", "tensor")
    outer_spec = P("pipe", "tensor", "dp")
    placed = (
        P(None, "dp", None),
        P(None, "dp", None),
        P(None, "dp", None),
        P(None, "dp"),
        P(None, "dp"),
        P(),
        inner_spec,
        inner_spec,
        inner_spec,
        outer_spec,
        inner_spec,
        inner_spec,
        inner_spec,
        outer_spec,
        inner_spec,
        inner_spec,
        outer_spec,
        P("pipe", None, "dp"),
        inner_spec,
    )
    return jax.shard_map(
        body,
        mesh=mesh,
        in_specs=placed,
        out_specs=(
            P("pipe", None, "dp", None),
            P("pipe", None, "dp", None),
            P("pipe", None, "dp", "tensor"),
            inner_spec,
            inner_spec,
            inner_spec,
            outer_spec,
            inner_spec,
            inner_spec,
            inner_spec,
            outer_spec,
            inner_spec,
            inner_spec,
            outer_spec,
            P("pipe", None, "dp"),
            inner_spec,
        ),
        check_vma=False,
    )
```

```python
import functools

import jax
import jax.numpy as jnp
from jax import lax
from jax.experimental import pallas as pl
from jax.experimental.pallas import tpu as pltpu
from jax.sharding import PartitionSpec as P

D = 768
HEAD = 64
BUCKETS = 32
MAXD = 128
EPS = 1e-06
AHEAD = 2
RELAY_WEIGHTS = True
RELAY_GRADS = True

F32 = jnp.float32
BF16 = jnp.bfloat16
MESH = pl.DeviceIdType.MESH


def dot_nn(a, b):
    return lax.dot_general(a, b, (((1,), (0,)), ((), ())), preferred_element_type=F32)


def dot_nt(a, b):
    return lax.dot_general(a, b, (((1,), (1,)), ((), ())), preferred_element_type=F32)


def dot_tn(a, b):
    return lax.dot_general(a, b, (((0,), (0,)), ((), ())), preferred_element_type=F32)


def norm_scale(values):
    return lax.rsqrt(jnp.mean(values * values, axis=-1, keepdims=True) + EPS)


def norm_back(values, gain, cotangent):
    scale = norm_scale(values)
    scaled = cotangent * gain
    inner = jnp.mean(scaled * values, axis=-1, keepdims=True)
    back = scale * scaled - values * (scale * scale * scale * inner)
    gain_grad = jnp.sum(cotangent * values * scale, axis=0, keepdims=True)
    return back, gain_grad


def gelu_parts(u):
    root = 0.7978845608028654
    cube = 0.044715
    t = jnp.tanh(root * (u + cube * u * u * u))
    value = 0.5 * u * (1.0 + t)
    slope = 0.5 * (1.0 + t) + 0.5 * u * (1.0 - t * t) * (root * (1.0 + 3.0 * cube * u * u))
    return value, slope


def head_masks(heads):
    lane = lax.broadcasted_iota(jnp.int32, (1, heads * HEAD), 1)
    return [
        ((lane >= h * HEAD) & (lane < (h + 1) * HEAD)).astype(F32).astype(BF16)
        for h in range(heads)
    ]


def spread_heads(values, masks):
    return jnp.concatenate([values * m for m in masks], axis=0)


def join_heads(values, masks):
    rows = values.shape[0] // len(masks)
    total = None
    for h, m in enumerate(masks):
        term = values[h * rows : (h + 1) * rows] * m.astype(F32)
        total = term if total is None else total + term
    return total


def each(low, high, run):
    if high - low <= 4:
        for k in range(low, high):
            run(k)
    else:
        lax.fori_loop(low, high, lambda k, c: (run(k), c)[1], 0)


def layout(inner, ff):
    sa, ca = 3 * ff, 3 * ff + 4 * inner
    sent = ((sa, 4 * inner), (ca, 4 * inner), (0, 2 * ff), (2 * ff, ff))
    summed = ((0, 3 * ff), (ca, 4 * inner), (sa, 4 * inner))
    return sent, summed


def main_kernel(
    dims,
    h_ref,
    enc_ref,
    up_ref,
    dec_ref,
    seg_ref,
    buck_ref,
    wq_ref,
    wk_ref,
    wv_ref,
    wo_ref,
    cq_ref,
    ck_ref,
    cv_ref,
    co_ref,
    gate_ref,
    upw_ref,
    down_ref,
    gain_ref,
    tab_ref,
    sum_out,
    sect_out,
    ingrad_out,
    enc_out,
    small_out,
    w_ref,
    small_w,
    gains_s,
    bias_s,
    bmap_s,
    x_in,
    g_in,
    r_one,
    r_two,
    n_one,
    n_two,
    n_three,
    qkv_s,
    so_s,
    p_s,
    cq_s,
    ckv_s,
    co_s,
    pc_s,
    gu_s,
    hid_s,
    send_one,
    recv_one,
    send_two,
    recv_two,
    enc_send,
    enc_own,
    enc_recv,
    grad_s,
    swap_s,
    part_s,
    relay_s,
    total_s,
    ingrad_s,
    table_s,
    small_g,
    sem_send,
    sem_recv,
    sem_enc_send,
    sem_enc_recv,
    sem_own_send,
    sem_own_recv,
    sem_z_send,
    sem_z_recv,
    sem_p_send,
    sem_p_recv,
    sem_sw_send,
    sem_sw_recv,
    sem_g_send,
    sem_g_recv,
    sem_r_recv,
    sem_f_send,
    sem_f_recv,
    sem_o_send,
    sem_o_recv,
    sem_sm_send,
    sem_sm_recv,
    sem_sg_send,
    sem_sg_recv,
):
    layers, dp, rows, inner, ff, heads, chunk, table_rows = dims
    half = rows // 2
    p = lax.axis_index("pipe")
    o = 1 - p
    g = lax.axis_index("dp")
    t = lax.axis_index("tensor")
    near = t + 1 - 2 * (t % 2)
    far = t + 2 - 4 * ((t // 2) % 2)
    both = far + 1 - 2 * (far % 2)
    peers = (near, far, both)
    way = 1 - 2 * (g // ((dp + 1) // 2))
    line = dp == 4 and RELAY_WEIGHTS
    line_back = dp == 4 and RELAY_GRADS
    masks = head_masks(heads)
    c_q = 3 * ff
    c_so = c_q + 3 * inner
    c_cq = c_q + 4 * inner
    c_ck = c_q + 5 * inner
    c_cv = c_q + 6 * inner
    c_co = c_q + 7 * inner
    c_end = c_q + 8 * inner
    sent, summed = layout(inner, ff)
    offsets = (0, summed[0][1] // 2, (summed[0][1] + summed[1][1]) // 2)

    barrier = pltpu.get_barrier_semaphore()

    def greet(ids):
        pl.semaphore_signal(barrier, inc=1, device_id=ids, device_id_type=MESH)

    for peer in peers:
        greet({"tensor": peer})
    greet({"pipe": o})

    def greet_group(k):
        s = lax.rem(g + k, dp)
        greet({"dp": s})
        greet({"dp": s, "pipe": o})

    each(1, dp, greet_group)

    def copy_to(src, dst, sem_a, sem_b, ids):
        return pltpu.make_async_remote_copy(
            src_ref=src,
            dst_ref=dst,
            send_sem=sem_a,
            recv_sem=sem_b,
            device_id=ids,
            device_id_type=MESH,
        )

    def other(k):
        return lax.rem(g + dp + way * k, dp)

    def pack(c, value):
        a, n = sent[c]
        w_ref[p, g, :, a : a + n] = value

    small_w[p, g] = jnp.zeros(small_w.shape[2:], F32)
    small_w[p, g, 0:3, 0:chunk] = gain_ref[...].astype(F32)
    small_w[p, g, 8 : 8 + heads, 0:table_rows] = tab_ref[...].astype(F32)
    pack(
        0, jnp.concatenate([wq_ref[...], wk_ref[...], wv_ref[...], wo_ref[...].T], axis=1)
    )
    pl.semaphore_wait(barrier, 3 + 1 + 2 * (dp - 1))

    def small_copy(ids, src_p, src_g, k, way_p):
        view = small_w.at[src_p, src_g]
        return copy_to(
            view, view, sem_sm_send.at[way_p, k], sem_sm_recv.at[src_p, src_g], ids
        )

    small_copy({"pipe": o}, p, g, 0, 1).start()

    def small_start(k):
        small_copy({"dp": other(k)}, p, g, k, 0).start()
        small_copy({"dp": other(k), "pipe": o}, p, g, k, 1).start()

    each(1, dp, small_start)

    def own_copy(c):
        a, n = sent[c]
        return copy_to(
            w_ref.at[p, g, :, a : a + n],
            w_ref.at[p, g, :, a : a + n],
            sem_own_send.at[c],
            sem_own_recv.at[c],
            {"pipe": o},
        )

    def own_arrival(c):
        a, n = sent[c]
        view = w_ref.at[o, g, :, a : a + n]
        copy_to(view, view, sem_own_send.at[c], sem_own_recv.at[c], {"pipe": o}).wait_recv()

    def view_of(l, c, s, side):
        a, n = sent[c]
        width = n // 2
        return w_ref.at[l, s, :, pl.ds(pl.multiple_of(a + side * width, 128), width)]

    def z_copy(l, c, s, target, sem):
        view = view_of(l, c, s, p)
        return copy_to(
            view, view, sem_z_send.at[l, c, sem], sem_z_recv.at[l, c, s], {"dp": target}
        )

    def p_copy(l, c, s, side):
        view = view_of(l, c, s, side)
        return copy_to(view, view, sem_p_send.at[l, c, s], sem_p_recv.at[l, c, s], {"pipe": o})

    def far_apart(a, b):
        return jnp.abs(a - b) == dp - 1

    def unless_relayed(s, run, relayed=line):
        if relayed:
            pl.when(jnp.logical_not(far_apart(g, s)))(run)
        else:
            run()

    def issue(l, c):
        @pl.when(l != p)
        def _():
            own_arrival(c)

        def start(k):
            s = other(dp - k)
            unless_relayed(s, lambda: z_copy(l, c, g, s, s).start())

        each(1, dp, start)

    def relays(s, run):
        if line:
            inside = (g == 1) | (g == 2)
            pl.when(inside & (s == lax.rem(g + 2, dp)))(run)

    def poll(l, c):
        def arrive(k):
            s = other(k)
            z_copy(l, c, s, s, s).wait_recv()
            relays(s, lambda: z_copy(l, c, s, dp - 1 - s, g).start())
            p_copy(l, c, s, p).start()

        each(1, dp, arrive)
        each(1, dp, lambda k: p_copy(l, c, other(k), o).wait_recv())

    own_copy(0).start()
    pack(
        1, jnp.concatenate([cq_ref[...], ck_ref[...], cv_ref[...], co_ref[...].T], axis=1)
    )
    own_copy(1).start()
    issue(0, 0)
    pack(2, jnp.concatenate([gate_ref[...], upw_ref[...]], axis=1))
    own_copy(2).start()
    pack(3, down_ref[...])
    own_copy(3).start()
    for c in range(1, AHEAD):
        issue(0, c)

    def issue_after(l, c):
        nl, nc = l + (c + AHEAD) // 4, (c + AHEAD) % 4
        if nc == c + AHEAD:
            issue(nl, nc)
        else:

            @pl.when(nl < layers)
            def _():
                issue(nl, nc)

    ri = lax.broadcasted_iota(jnp.int32, (rows, rows), 0)
    ci = lax.broadcasted_iota(jnp.int32, (rows, rows), 1)
    dec_row = dec_ref[pl.ds(p, 1), :].astype(F32)
    enc_row = seg_ref[pl.ds(p, 1), :].astype(F32)
    dec_col = jnp.sum(jnp.where(ri == ci, dec_row, 0.0), axis=1, keepdims=True)
    allowed = (dec_col == dec_row) & (ci <= ri)
    cmask = jnp.where(dec_col == enc_row, 0.0, -1e30)
    bi = lax.broadcasted_iota(jnp.int32, (BUCKETS, MAXD), 0)
    starts = jnp.sum(jnp.where(buck_ref[...] < bi, 1.0, 0.0), axis=1, keepdims=True)
    dist = jnp.clip(ri - ci, 0, MAXD - 1).astype(F32)
    bmap = jnp.zeros((rows, rows), F32)
    for b in range(1, BUCKETS):
        bmap = bmap + jnp.where(dist >= starts[b : b + 1], 1.0, 0.0)
    bmap_s[...] = bmap

    def small_arrive(k):
        s = other(k)
        small_copy({"dp": s}, p, s, k, 0).wait_recv()
        small_copy({"dp": s}, o, s, k, 0).wait_recv()

    each(1, dp, small_arrive)
    small_copy({"pipe": o}, o, g, 0, 1).wait_recv()
    for l in range(layers):
        for n in range(3):
            gains_s[l, n : n + 1] = jnp.concatenate(
                [small_w[l, s, n : n + 1, 0:chunk] for s in range(dp)], axis=1
            )
        for h in range(heads):
            bias = jnp.zeros((rows, rows), F32)
            for b in range(BUCKETS):
                at = b % table_rows
                value = small_w[l, b // table_rows, 8 + h : 9 + h, at : at + 1]
                bias = jnp.where(bmap == float(b), value, bias)
            bias_s[l, h * rows : (h + 1) * rows] = jnp.where(allowed, bias, -1e30)

    def weights(l, a, b):
        return w_ref[l, :, :, a:b].reshape(D, b - a)

    def first_copy(slot, part):
        return copy_to(
            send_one.at[slot, part],
            recv_one.at[slot, part],
            sem_send.at[slot, part],
            sem_recv.at[slot, part],
            {"tensor": near if part == 0 else far},
        )

    def second_copy(slot, part):
        return copy_to(
            send_two.at[slot, part],
            recv_two.at[slot, part],
            sem_send.at[slot, part + 2],
            sem_recv.at[slot, part + 2],
            {"tensor": far if part == 0 else near},
        )

    def sum_start(slot, make_half):
        for part in range(2):
            send_one[slot, part] = make_half(part).astype(BF16)
            first_copy(slot, part).start()

    def sum_middle(slot):
        for part in range(2):
            first_copy(slot, part).wait()
            value = send_one[slot, part].astype(F32) + recv_one[slot, part].astype(F32)
            send_two[slot, part] = value.astype(BF16)
            second_copy(slot, part).start()

    def sum_end(slot):
        pieces = []
        for part in range(2):
            second_copy(slot, part).wait()
            pieces.append(send_two[slot, part].astype(F32) + recv_two[slot, part].astype(F32))
        return jnp.concatenate(pieces, axis=0)

    def all_sum(slot, make_half, cover=None, later=None):
        sum_start(slot, make_half)
        if cover is not None:
            cover()
        sum_middle(slot)
        if later is not None:
            later()
        return sum_end(slot)

    x_in[0] = h_ref[p]
    enc = enc_ref[p]

    def make_result(l):
        def make_three(part):
            return dot_nt(
                hid_s[l, part * half : (part + 1) * half], weights(l, 2 * ff, 3 * ff)
            )

        return make_three

    def forward(l, carry):
        poll(l, 0)
        issue_after(l, 0)
        x0 = x_in[l].astype(F32)
        n1 = (x0 * norm_scale(x0) * gains_s[l, 0:1]).astype(BF16)
        n_one[l] = n1
        qkv = dot_nn(n1, weights(l, c_q, c_so)).astype(BF16)
        qkv_s[l] = qkv
        q = qkv[:, :inner]
        k = qkv[:, inner : 2 * inner]
        v = qkv[:, 2 * inner :]
        e = jnp.exp(dot_nt(spread_heads(q, masks), k) + bias_s[l])
        prob = e * (1.0 / jnp.sum(e, axis=-1, keepdims=True))
        p_s[l] = prob
        so_s[l] = join_heads(dot_nn(prob.astype(BF16), v), masks).astype(BF16)

        def make_one(part):
            return dot_nt(so_s[l, part * half : (part + 1) * half], weights(l, c_so, c_cq))

        def cover_one():
            poll(l, 1)
            issue_after(l, 1)
            ckv_s[l] = dot_nn(enc, weights(l, c_ck, c_co)).astype(BF16)

        x1 = x0 + all_sum(3 * l, make_one, cover_one)
        r_one[l] = x1
        n2 = (x1 * norm_scale(x1) * gains_s[l, 1:2]).astype(BF16)
        n_two[l] = n2
        cq = dot_nn(n2, weights(l, c_cq, c_ck)).astype(BF16)
        cq_s[l] = cq
        ckv = ckv_s[l]
        ck = ckv[:, :inner]
        cv = ckv[:, inner:]
        e = jnp.exp(
            dot_nt(spread_heads(cq, masks), ck) + jnp.concatenate([cmask] * heads, axis=0)
        )
        prob = e * (1.0 / jnp.sum(e, axis=-1, keepdims=True))
        pc_s[l] = prob
        co_s[l] = join_heads(dot_nn(prob.astype(BF16), cv), masks).astype(BF16)

        def make_two(part):
            return dot_nt(co_s[l, part * half : (part + 1) * half], weights(l, c_co, c_end))

        def cover_two():
            poll(l, 2)
            issue_after(l, 2)

        x2 = x1 + all_sum(3 * l + 1, make_two, None, cover_two)
        r_two[l] = x2
        n3 = (x2 * norm_scale(x2) * gains_s[l, 2:3]).astype(BF16)
        n_three[l] = n3
        gu = dot_nn(n3, weights(l, 0, 2 * ff))
        gu_s[l] = gu
        value, _ = gelu_parts(gu[:, :ff])
        hid_s[l] = (value * gu[:, ff:]).astype(BF16)
        poll(l, 3)
        issue_after(l, 3)

        @pl.when(l < layers - 1)
        def _():
            x_in[l + 1] = (x2 + all_sum(3 * l + 2, make_result(l))).astype(BF16)

        return carry

    lax.fori_loop(0, layers, forward, 0)
    last = 3 * layers - 1
    sum_start(last, make_result(layers - 1))
    g_in[...] = up_ref[p]

    def attend_back(grad, query, keys, values, attended, prob):
        gs = spread_heads(grad, masks)
        qs = spread_heads(query, masks)
        delta = jnp.sum(
            gs.astype(F32) * jnp.concatenate([attended.astype(F32)] * heads, axis=0),
            axis=-1,
            keepdims=True,
        )
        ds = prob * (dot_nt(gs, values) - delta)
        dsb = ds.astype(BF16)
        grad_query = join_heads(dot_nn(dsb, keys), masks).astype(BF16)
        return grad_query, ds, dsb, gs, qs

    def keep(l, r, value):
        width = summed[r][1] // 2
        for side in range(2):
            grad_s[l, side, :, :, offsets[r] : offsets[r] + width] = (
                value[:, side * width : (side + 1) * width].astype(BF16).reshape(dp, chunk, width)
            )

    def columns(r):
        return pl.ds(offsets[r], summed[r][1] // 2)

    def swap_copy(l, r):
        return copy_to(
            grad_s.at[l, o, :, :, columns(r)],
            swap_s.at[l, :, :, columns(r)],
            sem_sw_send.at[l, r],
            sem_sw_recv.at[l, r],
            {"pipe": o},
        )

    def slot_of(source, owner):
        return lax.rem(source - owner + dp, dp) - 1

    def piece_copy(l, r, s):
        return copy_to(
            grad_s.at[l, p, s, :, columns(r)],
            part_s.at[l, slot_of(g, s), :, columns(r)],
            sem_g_send.at[l, r, s],
            sem_g_recv.at[l, r, g],
            {"dp": s},
        )

    def relay_copy(l, r, s):
        return copy_to(
            grad_s.at[l, p, s, :, columns(r)],
            relay_s.at[l, :, columns(r)],
            sem_g_send.at[l, r, s],
            sem_r_recv.at[l, r],
            {"dp": g + 1 - 2 * (g // 2)},
        )

    def piece_arrival(l, r, s):
        return copy_to(
            grad_s.at[l, p, g, :, columns(r)],
            part_s.at[l, slot_of(s, g), :, columns(r)],
            sem_g_send.at[l, r, s],
            sem_g_recv.at[l, r, s],
            {"dp": s},
        )

    def is_inside():
        return (g == 1) | (g == 2)

    def send_pieces(l, r):
        swap_copy(l, r).wait_recv()

        def merge(s):
            grad_s[l, p, s, :, columns(r)] = (
                grad_s[l, p, s, :, columns(r)].astype(F32)
                + swap_s[l, s, :, columns(r)].astype(F32)
            ).astype(BF16)

        each(0, dp, merge)

        def start(k):
            s = other(dp - k)
            if not line_back:
                piece_copy(l, r, s).start()
                return

            @pl.when(far_apart(g, s))
            def _():
                relay_copy(l, r, s).start()

            @pl.when(jnp.abs(g - s) == 1)
            def _():
                piece_copy(l, r, s).start()

            @pl.when((jnp.abs(g - s) == 2) & jnp.logical_not(is_inside()))
            def _():
                piece_copy(l, r, s).start()

        each(1, dp, start)

    def pass_on(l, r):
        if not line_back:
            return

        @pl.when(is_inside())
        def _():
            s = lax.rem(g + 2, dp)
            relay_copy(l, r, s).wait_recv()
            grad_s[l, p, s, :, columns(r)] = (
                grad_s[l, p, s, :, columns(r)].astype(F32) + relay_s[l, :, columns(r)].astype(F32)
            ).astype(BF16)
            piece_copy(l, r, s).start()

    def total_of(l, r):
        total_s[l, :, columns(r)] = grad_s[l, p, g, :, columns(r)].astype(F32)

        def add(k):
            s = other(k)

            def run():
                piece_arrival(l, r, s).wait_recv()
                total_s[l, :, columns(r)] = total_s[l, :, columns(r)] + part_s[
                    l, slot_of(s, g), :, columns(r)
                ].astype(F32)

            unless_relayed(s, run, line_back)

        each(1, dp, add)

    def backward(step, carry):
        l = layers - 1 - step
        base = 3 * layers + 3 * step
        g3 = g_in[...]
        gf = g3.astype(F32)
        gu = gu_s[l]
        value, slope = gelu_parts(gu[:, :ff])
        dh = dot_nn(g3, weights(l, 2 * ff, 3 * ff))
        dgu = jnp.concatenate(
            [(dh * gu[:, ff:] * slope).astype(BF16), (dh * value).astype(BF16)], axis=1
        )

        def make_three(part):
            return dot_nt(dgu[part * half : (part + 1) * half], weights(l, 0, 2 * ff))

        def cover_three():
            keep(
                l, 0, jnp.concatenate([dot_tn(n_three[l], dgu), dot_tn(g3, hid_s[l])], axis=1)
            )
            swap_copy(l, 0).start()

            @pl.when(step == 0)
            def _():
                sum_middle(last)

            @pl.when(step > 0)
            def _():
                pass_on(l + 1, 1)

        dn = all_sum(base, make_three, cover_three, lambda: send_pieces(l, 0))
        back, gain_three = norm_back(r_two[l], gains_s[l, 2:3], dn)
        g2 = gf + back
        g2b = g2.astype(BF16)
        dc = dot_nn(g2b, weights(l, c_co, c_end)).astype(BF16)
        ckv = ckv_s[l]
        co = co_s[l]
        pc = pc_s[l]
        dcq, _, dsb, gs, qs = attend_back(dc, cq_s[l], ckv[:, :inner], ckv[:, inner:], co, pc)

        def make_two(part):
            return dot_nt(dcq[part * half : (part + 1) * half], weights(l, c_cq, c_ck))

        def cover_two():
            dck = dot_tn(dsb, qs).astype(BF16)
            dcv = dot_tn(pc.astype(BF16), gs).astype(BF16)
            dckv = jnp.concatenate([dck, dcv], axis=1)
            blocks = inner // chunk
            for k in range(D // inner):
                owner = t if k == 0 else peers[k - 1]
                rows_of = w_ref[l, pl.ds(owner * blocks, blocks), :, c_ck:c_co]
                part = dot_nt(rows_of.reshape(inner, 2 * inner), dckv)
                if k == 0:
                    enc_own[l] = part
                else:
                    enc_send[l, k - 1] = part.astype(BF16)
                    enc_copy(l, k - 1).start()
            keep(
                l,
                1,
                jnp.concatenate(
                    [dot_tn(n_two[l], dcq), dot_tn(enc, dckv), dot_tn(g2b, co)], axis=1
                ),
            )
            swap_copy(l, 1).start()

            @pl.when(step == 0)
            def _():
                x_in[layers] = (r_two[layers - 1] + sum_end(last)).astype(BF16)

            @pl.when(step > 0)
            def _():
                pass_on(l + 1, 2)

        dn = all_sum(base + 1, make_two, cover_two, lambda: send_pieces(l, 1))
        back, gain_two = norm_back(r_one[l], gains_s[l, 1:2], dn)
        g1 = g2 + back
        g1b = g1.astype(BF16)
        dself = dot_nn(g1b, weights(l, c_so, c_cq)).astype(BF16)
        qkv = qkv_s[l]
        so = so_s[l]
        ps = p_s[l]
        dq, ds, dsb, gs, qs = attend_back(
            dself, qkv[:, :inner], qkv[:, inner : 2 * inner], qkv[:, 2 * inner :], so, ps
        )
        dk = dot_tn(dsb, qs).astype(BF16)
        dv = dot_tn(ps.astype(BF16), gs).astype(BF16)
        dqkv = jnp.concatenate([dq, dk, dv], axis=1)

        def make_one(part):
            return dot_nt(dqkv[part * half : (part + 1) * half], weights(l, c_q, c_so))

        def cover_one():
            keep(l, 2, jnp.concatenate([dot_tn(n_one[l], dqkv), dot_tn(g1b, so)], axis=1))
            swap_copy(l, 2).start()

        def later_one():
            send_pieces(l, 2)
            pass_on(l, 0)
            buckets = bmap_s[...]
            for h in range(heads):
                ds_h = ds[h * rows : (h + 1) * rows]
                for b in range(BUCKETS):
                    table_s[h, b : b + 1] = jnp.sum(
                        jnp.where(buckets == float(b), ds_h, 0.0), axis=0, keepdims=True
                    )

        dn = all_sum(base + 2, make_one, cover_one, later_one)
        back, gain_one = norm_back(x_in[l].astype(F32), gains_s[l, 0:1], dn)
        gin = g1 + back
        ingrad_s[l] = gin
        g_in[...] = gin.astype(BF16)
        small_g[l] = jnp.zeros(small_g.shape[1:], F32)
        table = jnp.sum(table_s[...], axis=2)
        for s in range(dp):
            for n, value in enumerate((gain_one, gain_two, gain_three)):
                small_g[l, s, n : n + 1, 0:chunk] = value[:, s * chunk : (s + 1) * chunk]
            for h in range(heads):
                small_g[l, s, 8 + h : 9 + h, 0:table_rows] = table[
                    h : h + 1, s * table_rows : (s + 1) * table_rows
                ]
        return carry

    def enc_copy(l, k):
        return copy_to(
            enc_send.at[l, k],
            enc_recv.at[l, k],
            sem_enc_send.at[l, k],
            sem_enc_recv.at[l, k],
            {"tensor": peers[k]},
        )

    lax.fori_loop(0, layers, backward, 0)

    def grad_small_copy(l, s, src_p, src_g, ids):
        return copy_to(
            small_g.at[l, s],
            small_out.at[src_p, src_g],
            sem_sg_send.at[l, s],
            sem_sg_recv.at[src_p, src_g],
            ids,
        )

    small_out[p, g] = small_g[p, g]
    grad_small_copy(o, g, p, g, {"pipe": o}).start()

    def grad_small_start(k):
        s = other(k)
        grad_small_copy(p, s, p, g, {"dp": s}).start()
        grad_small_copy(o, s, p, g, {"dp": s, "pipe": o}).start()

    each(1, dp, grad_small_start)
    pass_on(0, 1)
    pass_on(0, 2)

    for l in range(layers):
        total = enc_own[l]
        for k in range(3):
            enc_copy(l, k).wait()
            total = total + enc_recv[l, k].astype(F32)
        enc_own[l] = total

    moved = (
        (x_in.at[o + 1], sect_out.at[p]),
        (ingrad_s.at[o], ingrad_out.at[p]),
        (enc_own.at[o], enc_out.at[p]),
    )

    def moved_copy(n):
        src, dst = moved[n]
        return copy_to(src, dst, sem_o_send.at[n], sem_o_recv.at[n], {"pipe": o})

    for n in range(3):
        moved_copy(n).start()
    sect_out[p] = x_in[p + 1]
    ingrad_out[p] = ingrad_s[p]
    enc_out[p] = enc_own[p]

    def final_copy(r):
        return copy_to(
            total_s.at[o, :, columns(r)],
            sum_out.at[p, :, columns(r)],
            sem_f_send.at[r],
            sem_f_recv.at[r],
            {"pipe": o},
        )

    for r in range(3):
        for l in reversed(range(layers)):
            total_of(l, r)
        sum_out[p, :, columns(r)] = total_s[p, :, columns(r)]
        final_copy(r).start()

    def arrival(view, sem):
        copy_to(view, view, sem, sem, {"pipe": o}).wait_recv()

    for r in range(3):
        final_copy(r).wait_send()
        arrival(sum_out.at[o, :, columns(r)], sem_f_recv.at[r])
    for n in range(3):
        moved_copy(n).wait_send()
        arrival(moved[n][1], sem_o_recv.at[n])
    grad_small_copy(o, g, p, g, {"pipe": o}).wait_send()
    grad_small_copy(o, g, o, g, {"pipe": o}).wait_recv()

    def grad_small_end(k):
        s = other(k)
        grad_small_copy(p, s, p, g, {"dp": s}).wait_send()
        grad_small_copy(o, s, p, g, {"dp": s}).wait_send()
        grad_small_copy(p, s, p, s, {"dp": s}).wait_recv()
        grad_small_copy(o, s, o, s, {"dp": s}).wait_recv()

    each(1, dp, grad_small_end)
    small_copy({"pipe": o}, p, g, 0, 1).wait_send()

    def small_end(k):
        small_copy({"dp": other(k)}, p, g, k, 0).wait_send()
        small_copy({"dp": other(k)}, p, g, k, 1).wait_send()

    each(1, dp, small_end)
    for c in range(4):
        own_copy(c).wait_send()

    def layer_end(l, carry):
        for c in range(4):

            def sent_end(k):
                s = other(k)
                unless_relayed(s, lambda: z_copy(l, c, g, s, s).wait_send())
                relays(s, lambda: z_copy(l, c, s, dp - 1 - s, g).wait_send())
                p_copy(l, c, s, p).wait_send()

            each(1, dp, sent_end)
        for r in range(3):
            swap_copy(l, r).wait_send()
            each(1, dp, lambda k: piece_copy(l, r, other(k)).wait_send())
        return carry

    lax.fori_loop(0, layers, layer_end, 0)


def run_main(inputs, layers, dp):
    h, enc, wq, gate, table = inputs[0], inputs[1], inputs[6], inputs[14], inputs[18]
    rows, enc_rows = h.shape[1], enc.shape[1]
    chunk, inner, ff = wq.shape[0], wq.shape[1], gate.shape[1]
    heads, table_rows = inner // HEAD, table.shape[1]
    half = rows // 2
    slots = 6 * layers
    width = 3 * ff + 8 * inner
    small = (16, -(-chunk // 128) * 128)
    vm = pltpu.VMEM
    dma = pltpu.SemaphoreType.DMA
    dims = (layers, dp, rows, inner, ff, heads, chunk, table_rows)
    return pl.pallas_call(
        functools.partial(main_kernel, dims),
        out_shape=(
            jax.ShapeDtypeStruct((2, chunk, width // 2), F32),
            jax.ShapeDtypeStruct((2, rows, D), BF16),
            jax.ShapeDtypeStruct((2, rows, D), F32),
            jax.ShapeDtypeStruct((2, inner, enc_rows), F32),
            jax.ShapeDtypeStruct((2, dp) + small, F32),
        ),
        in_specs=[pl.BlockSpec(memory_space=pltpu.VMEM)] * 19,
        out_specs=(pl.BlockSpec(memory_space=pltpu.VMEM),) * 5,
        scratch_shapes=[
            vm((layers, dp, chunk, width), BF16),
            vm((layers, dp) + small, F32),
            vm((layers, 8, D), F32),
            vm((layers, heads * rows, rows), F32),
            vm((rows, rows), F32),
            vm((layers + 1, rows, D), BF16),
            vm((rows, D), BF16),
            vm((layers, rows, D), F32),
            vm((layers, rows, D), F32),
            vm((layers, rows, D), BF16),
            vm((layers, rows, D), BF16),
            vm((layers, rows, D), BF16),
            vm((layers, rows, 3 * inner), BF16),
            vm((layers, rows, inner), BF16),
            vm((layers, heads * rows, rows), F32),
            vm((layers, rows, inner), BF16),
            vm((layers, enc_rows, 2 * inner), BF16),
            vm((layers, rows, inner), BF16),
            vm((layers, heads * rows, enc_rows), F32),
            vm((layers, rows, 2 * ff), F32),
            vm((layers, rows, ff), BF16),
            vm((slots, 2, half, D), BF16),
            vm((slots, 2, half, D), BF16),
            vm((slots, 2, half, D), BF16),
            vm((slots, 2, half, D), BF16),
            vm((layers, 3, inner, enc_rows), BF16),
            vm((layers, inner, enc_rows), F32),
            vm((layers, 3, inner, enc_rows), BF16),
            vm((layers, 2, dp, chunk, width // 2), BF16),
            vm((layers, dp, chunk, width // 2), BF16),
            vm((layers, dp - 1, chunk, width // 2), BF16),
            vm((layers, chunk, width // 2), BF16),
            vm((layers, chunk, width // 2), F32),
            vm((layers, rows, D), F32),
            vm((heads, BUCKETS, rows), F32),
            vm((layers, dp) + small, F32),
            dma((slots, 4)),
            dma((slots, 4)),
            dma((layers, 3)),
            dma((layers, 3)),
            dma((4,)),
            dma((4,)),
            dma((layers, 4, dp)),
            dma((layers, 4, dp)),
            dma((layers, 4, dp)),
            dma((layers, 4, dp)),
            dma((layers, 3)),
            dma((layers, 3)),
            dma((layers, 3, dp)),
            dma((layers, 3, dp)),
            dma((layers, 3)),
            dma((3,)),
            dma((3,)),
            dma((3,)),
            dma((3,)),
            dma((2, dp)),
            dma((2, dp)),
            dma((2, dp)),
            dma((2, dp)),
        ],
        compiler_params=pltpu.CompilerParams(
            collective_id=0, has_side_effects=True, vmem_limit_bytes=60 * 1024 * 1024
        ),
    )(*inputs)


def finish_kernel(dims, *refs):
    inner, ff, heads, chunk, table_rows = dims
    sum_hbm, sect_ref, ingrad_ref, enc_ref, small_hbm = refs[:5]
    (sect_out, ingrad_out, enc_out, q_out, k_out, v_out, o_out, cq_out, ck_out, cv_out) = refs[5:15]
    co_out, gate_out, up_out, down_out, gain_out, tab_out = refs[15:21]
    sum_ref, small_ref, sem = refs[21:]
    _, summed = layout(inner, ff)

    def take(a, n):
        offset = 0
        for start, width in summed:
            if start <= a < start + width:
                pieces = []
                for side in range(2):
                    low = max(a, start + side * (width // 2))
                    high = min(a + n, start + (side + 1) * (width // 2))
                    if low < high:
                        at = offset + low - start - side * (width // 2)
                        pieces.append(sum_ref[side, :, at : at + high - low])
                return pieces[0] if len(pieces) == 1 else jnp.concatenate(pieces, axis=1)
            offset += width // 2

    copies = [
        pltpu.make_async_copy(src, dst, sem.at[n])
        for n, (src, dst) in enumerate(
            ((sum_hbm, sum_ref), (small_hbm, small_ref), (sect_ref, sect_out))
            + ((ingrad_ref, ingrad_out), (enc_ref, enc_out))
        )
    ]
    for copy in copies:
        copy.start()
    copies[1].wait()
    small = jnp.sum(small_ref[...], axis=(0, 1))
    for n in range(3):
        gain_out[n] = small[n : n + 1, 0:chunk]
    for h in range(heads):
        tab_out[h] = small[8 + h : 9 + h, 0:table_rows]
    copies[0].wait()
    c = 3 * ff
    for n, out in enumerate((q_out, k_out, v_out, o_out, cq_out, ck_out, cv_out, co_out)):
        value = take(c + n * inner, inner)
        out[...] = value.T if n % 4 == 3 else value
    gate_out[...] = take(0, ff)
    up_out[...] = take(ff, ff)
    down_out[...] = take(2 * ff, ff)
    for copy in copies[2:]:
        copy.wait()


def run_finish(parts, inner, ff, chunk, table_rows):
    heads = inner // HEAD
    total, sect, ingrad, enc, small = parts
    into, outer = (chunk, inner), (inner, chunk)
    shapes = [sect.shape, ingrad.shape, enc.shape]
    shapes += [into, into, into, outer] * 2
    shapes += [(chunk, ff), (chunk, ff), (chunk, ff), (3, 1, chunk), (heads, 1, table_rows)]
    types = [BF16] + [F32] * 15
    return pl.pallas_call(
        functools.partial(finish_kernel, (inner, ff, heads, chunk, table_rows)),
        out_shape=tuple(jax.ShapeDtypeStruct(s, d) for s, d in zip(shapes, types)),
        in_specs=[pl.BlockSpec(memory_space=pltpu.HBM)] * 5,
        out_specs=(pl.BlockSpec(memory_space=pltpu.VMEM),) * 16,
        scratch_shapes=[
            pltpu.VMEM(total.shape, F32),
            pltpu.VMEM(small.shape, F32),
            pltpu.SemaphoreType.DMA((5,)),
        ],
        compiler_params=pltpu.CompilerParams(vmem_limit_bytes=60 * 1024 * 1024),
    )(*parts)


def body(*args):
    layers = lax.axis_size("pipe")
    dp = lax.axis_size("dp")
    inputs = list(args[:5]) + [args[5].reshape(1, -1)] + [value[0] for value in args[6:]]
    inputs[16], inputs[18] = inputs[16].T, inputs[18].T
    chunk, inner = inputs[6].shape
    ff, table_rows = inputs[14].shape[1], inputs[18].shape[1]
    parts = run_main(inputs, layers, dp)
    outs = run_finish(parts, inner, ff, chunk, table_rows)
    outs = list(outs)
    outs[2] = outs[2].transpose(0, 2, 1)
    outs[13] = outs[13].T
    gain, table = outs[14].transpose(1, 0, 2), outs[15].transpose(1, 2, 0)
    return tuple(value[None] for value in outs[:14]) + (gain, table)


def solution(mesh):
    inner_spec = P("pipe", "dp", "tensor")
    outer_spec = P("pipe", "tensor", "dp")
    placed = (
        P(None, "dp", None),
        P(None, "dp", None),
        P(None, "dp", None),
        P(None, "dp"),
        P(None, "dp"),
        P(),
        inner_spec,
        inner_spec,
        inner_spec,
        outer_spec,
        inner_spec,
        inner_spec,
        inner_spec,
        outer_spec,
        inner_spec,
        inner_spec,
        outer_spec,
        P("pipe", None, "dp"),
        inner_spec,
    )
    return jax.shard_map(
        body,
        mesh=mesh,
        in_specs=placed,
        out_specs=(
            P("pipe", None, "dp", None),
            P("pipe", None, "dp", None),
            P("pipe", None, "dp", "tensor"),
            inner_spec,
            inner_spec,
            inner_spec,
            outer_spec,
            inner_spec,
            inner_spec,
            inner_spec,
            outer_spec,
            inner_spec,
            inner_spec,
            outer_spec,
            P("pipe", None, "dp"),
            inner_spec,
        ),
        check_vma=False,
    )
```

```python
import functools

import jax
import jax.numpy as jnp
from jax import lax
from jax.experimental import pallas as pl
from jax.experimental.pallas import tpu as pltpu
from jax.sharding import PartitionSpec as P

D = 768
HEAD = 64
BUCKETS = 32
MAXD = 128
EPS = 1e-06
AHEAD = 3
AHEAD_END = 2
RELAY_WEIGHTS = True
RELAY_GRADS = True

F32 = jnp.float32
BF16 = jnp.bfloat16
MESH = pl.DeviceIdType.MESH


def dot_nn(a, b):
    return lax.dot_general(a, b, (((1,), (0,)), ((), ())), preferred_element_type=F32)


def dot_nt(a, b):
    return lax.dot_general(a, b, (((1,), (1,)), ((), ())), preferred_element_type=F32)


def dot_tn(a, b):
    return lax.dot_general(a, b, (((0,), (0,)), ((), ())), preferred_element_type=F32)


def norm_scale(values):
    return lax.rsqrt(jnp.mean(values * values, axis=-1, keepdims=True) + EPS)


def norm_back(values, gain, cotangent):
    scale = norm_scale(values)
    scaled = cotangent * gain
    inner = jnp.mean(scaled * values, axis=-1, keepdims=True)
    back = scale * scaled - values * (scale * scale * scale * inner)
    gain_grad = jnp.sum(cotangent * values * scale, axis=0, keepdims=True)
    return back, gain_grad


def gelu_parts(u):
    root = 0.7978845608028654
    cube = 0.044715
    t = jnp.tanh(root * (u + cube * u * u * u))
    value = 0.5 * u * (1.0 + t)
    slope = 0.5 * (1.0 + t) + 0.5 * u * (1.0 - t * t) * (root * (1.0 + 3.0 * cube * u * u))
    return value, slope


def head_masks(heads):
    lane = lax.broadcasted_iota(jnp.int32, (1, heads * HEAD), 1)
    return [
        ((lane >= h * HEAD) & (lane < (h + 1) * HEAD)).astype(F32).astype(BF16)
        for h in range(heads)
    ]


def spread_heads(values, masks):
    return jnp.concatenate([values * m for m in masks], axis=0)


def join_heads(values, masks):
    rows = values.shape[0] // len(masks)
    total = None
    for h, m in enumerate(masks):
        term = values[h * rows : (h + 1) * rows] * m.astype(F32)
        total = term if total is None else total + term
    return total


def each(low, high, run):
    if high - low <= 4:
        for k in range(low, high):
            run(k)
    else:
        lax.fori_loop(low, high, lambda k, c: (run(k), c)[1], 0)


def layout(inner, ff):
    sa, ca = 3 * ff, 3 * ff + 4 * inner
    sent = ((sa, 4 * inner), (ca, 4 * inner), (0, 2 * ff), (2 * ff, ff))
    summed = ((2 * ff, ff), (0, 2 * ff), (ca, 4 * inner), (sa, 4 * inner))
    return sent, summed


def main_kernel(
    dims,
    h_ref,
    enc_ref,
    up_ref,
    dec_ref,
    seg_ref,
    buck_ref,
    wq_ref,
    wk_ref,
    wv_ref,
    wo_ref,
    cq_ref,
    ck_ref,
    cv_ref,
    co_ref,
    gate_ref,
    upw_ref,
    down_ref,
    gain_ref,
    tab_ref,
    sum_out,
    sect_out,
    ingrad_out,
    enc_out,
    small_out,
    w_ref,
    small_w,
    gains_s,
    bias_s,
    bmap_s,
    x_in,
    g_in,
    r_one,
    r_two,
    n_one,
    n_two,
    n_three,
    qkv_s,
    so_s,
    p_s,
    cq_s,
    ckv_s,
    co_s,
    pc_s,
    gu_s,
    hid_s,
    send_one,
    recv_one,
    send_two,
    recv_two,
    enc_send,
    enc_own,
    enc_recv,
    grad_s,
    swap_s,
    part_s,
    relay_s,
    total_s,
    ingrad_s,
    table_s,
    small_g,
    sem_send,
    sem_recv,
    sem_enc_send,
    sem_enc_recv,
    sem_own_send,
    sem_own_recv,
    sem_z_send,
    sem_z_recv,
    sem_p_send,
    sem_p_recv,
    sem_sw_send,
    sem_sw_recv,
    sem_g_send,
    sem_g_recv,
    sem_r_recv,
    sem_f_send,
    sem_f_recv,
    sem_o_send,
    sem_o_recv,
    sem_sm_send,
    sem_sm_recv,
    sem_sg_send,
    sem_sg_recv,
):
    layers, dp, rows, inner, ff, heads, chunk, table_rows = dims
    half = rows // 2
    p = lax.axis_index("pipe")
    o = 1 - p
    g = lax.axis_index("dp")
    t = lax.axis_index("tensor")
    near = t + 1 - 2 * (t % 2)
    far = t + 2 - 4 * ((t // 2) % 2)
    both = far + 1 - 2 * (far % 2)
    peers = (near, far, both)
    way = 1 - 2 * (g // ((dp + 1) // 2))
    line = dp == 4 and RELAY_WEIGHTS
    line_back = dp == 4 and RELAY_GRADS
    masks = head_masks(heads)
    c_q = 3 * ff
    c_so = c_q + 3 * inner
    c_cq = c_q + 4 * inner
    c_ck = c_q + 5 * inner
    c_cv = c_q + 6 * inner
    c_co = c_q + 7 * inner
    c_end = c_q + 8 * inner
    sent, summed = layout(inner, ff)
    parts = len(summed)
    offsets = [sum(n for _, n in summed[:r]) // 2 for r in range(parts)]

    barrier = pltpu.get_barrier_semaphore()

    def greet(ids):
        pl.semaphore_signal(barrier, inc=1, device_id=ids, device_id_type=MESH)

    for peer in peers:
        greet({"tensor": peer})
    greet({"pipe": o})

    def greet_group(k):
        s = lax.rem(g + k, dp)
        greet({"dp": s})
        greet({"dp": s, "pipe": o})

    each(1, dp, greet_group)

    def copy_to(src, dst, sem_a, sem_b, ids):
        return pltpu.make_async_remote_copy(
            src_ref=src,
            dst_ref=dst,
            send_sem=sem_a,
            recv_sem=sem_b,
            device_id=ids,
            device_id_type=MESH,
        )

    def other(k):
        return lax.rem(g + dp + way * k, dp)

    def pack(c, value):
        a, n = sent[c]
        w_ref[p, g, :, a : a + n] = value

    small_w[p, g] = jnp.zeros(small_w.shape[2:], F32)
    small_w[p, g, 0:3, 0:chunk] = gain_ref[...].astype(F32)
    small_w[p, g, 8 : 8 + heads, 0:table_rows] = tab_ref[...].astype(F32)
    pack(
        0, jnp.concatenate([wq_ref[...], wk_ref[...], wv_ref[...], wo_ref[...].T], axis=1)
    )
    pl.semaphore_wait(barrier, 3 + 1 + 2 * (dp - 1))

    def small_copy(ids, src_p, src_g, k, way_p):
        view = small_w.at[src_p, src_g]
        return copy_to(
            view, view, sem_sm_send.at[way_p, k], sem_sm_recv.at[src_p, src_g], ids
        )

    small_copy({"pipe": o}, p, g, 0, 1).start()

    def small_start(k):
        small_copy({"dp": other(k)}, p, g, k, 0).start()
        small_copy({"dp": other(k), "pipe": o}, p, g, k, 1).start()

    each(1, dp, small_start)

    def own_copy(c):
        a, n = sent[c]
        return copy_to(
            w_ref.at[p, g, :, a : a + n],
            w_ref.at[p, g, :, a : a + n],
            sem_own_send.at[c],
            sem_own_recv.at[c],
            {"pipe": o},
        )

    def own_arrival(c):
        a, n = sent[c]
        view = w_ref.at[o, g, :, a : a + n]
        copy_to(view, view, sem_own_send.at[c], sem_own_recv.at[c], {"pipe": o}).wait_recv()

    def view_of(l, c, s, side):
        a, n = sent[c]
        width = n // 2
        return w_ref.at[l, s, :, pl.ds(pl.multiple_of(a + side * width, 128), width)]

    def z_copy(l, c, s, target, sem):
        view = view_of(l, c, s, p)
        return copy_to(
            view, view, sem_z_send.at[l, c, sem], sem_z_recv.at[l, c, s], {"dp": target}
        )

    def p_copy(l, c, s, side):
        view = view_of(l, c, s, side)
        return copy_to(view, view, sem_p_send.at[l, c, s], sem_p_recv.at[l, c, s], {"pipe": o})

    def far_apart(a, b):
        return jnp.abs(a - b) == dp - 1

    def unless_relayed(s, run, relayed=line):
        if relayed:
            pl.when(jnp.logical_not(far_apart(g, s)))(run)
        else:
            run()

    def issue(l, c):
        @pl.when(l != p)
        def _():
            own_arrival(c)

        def start(k):
            s = other(dp - k)
            unless_relayed(s, lambda: z_copy(l, c, g, s, s).start())

        each(1, dp, start)

    def relays(s, run):
        if line:
            inside = (g == 1) | (g == 2)
            pl.when(inside & (s == lax.rem(g + 2, dp)))(run)

    def poll(l, c):
        def arrive(k):
            s = other(k)
            z_copy(l, c, s, s, s).wait_recv()
            relays(s, lambda: z_copy(l, c, s, dp - 1 - s, g).start())
            p_copy(l, c, s, p).start()

        each(1, dp, arrive)
        each(1, dp, lambda k: p_copy(l, c, other(k), o).wait_recv())

    own_copy(0).start()
    pack(
        1, jnp.concatenate([cq_ref[...], ck_ref[...], cv_ref[...], co_ref[...].T], axis=1)
    )
    own_copy(1).start()
    issue(0, 0)
    pack(2, jnp.concatenate([gate_ref[...], upw_ref[...]], axis=1))
    own_copy(2).start()
    pack(3, down_ref[...])
    own_copy(3).start()
    inner_group = (g > 0) & (g < dp - 1)
    paces = ((inner_group, AHEAD), (jnp.logical_not(inner_group), AHEAD_END))

    for mine, ahead in paces:

        @pl.when(mine)
        def _():
            for c in range(1, ahead):
                issue(0, c)

    def issue_after(l, c):
        for mine, ahead in paces:
            nl, nc = l + (c + ahead) // 4, (c + ahead) % 4

            @pl.when(mine & (nl < layers))
            def _():
                issue(nl, nc)

    ri = lax.broadcasted_iota(jnp.int32, (rows, rows), 0)
    ci = lax.broadcasted_iota(jnp.int32, (rows, rows), 1)
    dec_row = dec_ref[pl.ds(p, 1), :].astype(F32)
    enc_row = seg_ref[pl.ds(p, 1), :].astype(F32)
    dec_col = jnp.sum(jnp.where(ri == ci, dec_row, 0.0), axis=1, keepdims=True)
    allowed = (dec_col == dec_row) & (ci <= ri)
    cmask = jnp.where(dec_col == enc_row, 0.0, -1e30)
    bi = lax.broadcasted_iota(jnp.int32, (BUCKETS, MAXD), 0)
    starts = jnp.sum(jnp.where(buck_ref[...] < bi, 1.0, 0.0), axis=1, keepdims=True)
    dist = jnp.clip(ri - ci, 0, MAXD - 1).astype(F32)
    bmap = jnp.zeros((rows, rows), F32)
    for b in range(1, BUCKETS):
        bmap = bmap + jnp.where(dist >= starts[b : b + 1], 1.0, 0.0)
    bmap_s[...] = bmap

    def small_arrive(k):
        s = other(k)
        small_copy({"dp": s}, p, s, k, 0).wait_recv()
        small_copy({"dp": s}, o, s, k, 0).wait_recv()

    each(1, dp, small_arrive)
    small_copy({"pipe": o}, o, g, 0, 1).wait_recv()
    for l in range(layers):
        for n in range(3):
            gains_s[l, n : n + 1] = jnp.concatenate(
                [small_w[l, s, n : n + 1, 0:chunk] for s in range(dp)], axis=1
            )
        for h in range(heads):
            bias = jnp.zeros((rows, rows), F32)
            for b in range(BUCKETS):
                at = b % table_rows
                value = small_w[l, b // table_rows, 8 + h : 9 + h, at : at + 1]
                bias = jnp.where(bmap == float(b), value, bias)
            bias_s[l, h * rows : (h + 1) * rows] = jnp.where(allowed, bias, -1e30)

    def weights(l, a, b):
        return w_ref[l, :, :, a:b].reshape(D, b - a)

    def first_copy(slot, part):
        return copy_to(
            send_one.at[slot, part],
            recv_one.at[slot, part],
            sem_send.at[slot, part],
            sem_recv.at[slot, part],
            {"tensor": near if part == 0 else far},
        )

    def second_copy(slot, part):
        return copy_to(
            send_two.at[slot, part],
            recv_two.at[slot, part],
            sem_send.at[slot, part + 2],
            sem_recv.at[slot, part + 2],
            {"tensor": far if part == 0 else near},
        )

    def sum_start(slot, make_half):
        for part in range(2):
            send_one[slot, part] = make_half(part).astype(BF16)
            first_copy(slot, part).start()

    def sum_middle(slot):
        for part in range(2):
            first_copy(slot, part).wait()
            value = send_one[slot, part].astype(F32) + recv_one[slot, part].astype(F32)
            send_two[slot, part] = value.astype(BF16)
            second_copy(slot, part).start()

    def sum_end(slot):
        pieces = []
        for part in range(2):
            second_copy(slot, part).wait()
            pieces.append(send_two[slot, part].astype(F32) + recv_two[slot, part].astype(F32))
        return jnp.concatenate(pieces, axis=0)

    def all_sum(slot, make_half, cover=None, later=None):
        sum_start(slot, make_half)
        if cover is not None:
            cover()
        sum_middle(slot)
        if later is not None:
            later()
        return sum_end(slot)

    def keep(l, r, value):
        width = summed[r][1] // 2
        for side in range(2):
            grad_s[l, side, :, :, offsets[r] : offsets[r] + width] = (
                value[:, side * width : (side + 1) * width].astype(BF16).reshape(dp, chunk, width)
            )

    def columns(r):
        return pl.ds(offsets[r], summed[r][1] // 2)

    def swap_copy(l, r):
        return copy_to(
            grad_s.at[l, o, :, :, columns(r)],
            swap_s.at[l, :, :, columns(r)],
            sem_sw_send.at[l, r],
            sem_sw_recv.at[l, r],
            {"pipe": o},
        )

    def slot_of(source, owner):
        return lax.rem(source - owner + dp, dp) - 1

    def piece_copy(l, r, s):
        return copy_to(
            grad_s.at[l, p, s, :, columns(r)],
            part_s.at[l, slot_of(g, s), :, columns(r)],
            sem_g_send.at[l, r, s],
            sem_g_recv.at[l, r, g],
            {"dp": s},
        )

    def relay_copy(l, r, s):
        return copy_to(
            grad_s.at[l, p, s, :, columns(r)],
            relay_s.at[l, :, columns(r)],
            sem_g_send.at[l, r, s],
            sem_r_recv.at[l, r],
            {"dp": g + 1 - 2 * (g // 2)},
        )

    def piece_arrival(l, r, s):
        return copy_to(
            grad_s.at[l, p, g, :, columns(r)],
            part_s.at[l, slot_of(s, g), :, columns(r)],
            sem_g_send.at[l, r, s],
            sem_g_recv.at[l, r, s],
            {"dp": s},
        )

    def is_inside():
        return (g == 1) | (g == 2)

    def send_pieces(l, r):
        swap_copy(l, r).wait_recv()

        def merge(s):
            grad_s[l, p, s, :, columns(r)] = (
                grad_s[l, p, s, :, columns(r)].astype(F32)
                + swap_s[l, s, :, columns(r)].astype(F32)
            ).astype(BF16)

        each(0, dp, merge)

        def start(k):
            s = other(dp - k)
            if not line_back:
                piece_copy(l, r, s).start()
                return

            @pl.when(far_apart(g, s))
            def _():
                relay_copy(l, r, s).start()

            @pl.when(jnp.abs(g - s) == 1)
            def _():
                piece_copy(l, r, s).start()

            @pl.when((jnp.abs(g - s) == 2) & jnp.logical_not(is_inside()))
            def _():
                piece_copy(l, r, s).start()

        each(1, dp, start)

    def pass_on(l, r):
        if not line_back:
            return

        @pl.when(is_inside())
        def _():
            s = lax.rem(g + 2, dp)
            relay_copy(l, r, s).wait_recv()
            grad_s[l, p, s, :, columns(r)] = (
                grad_s[l, p, s, :, columns(r)].astype(F32) + relay_s[l, :, columns(r)].astype(F32)
            ).astype(BF16)
            piece_copy(l, r, s).start()

    def total_of(l, r):
        total_s[l, :, columns(r)] = grad_s[l, p, g, :, columns(r)].astype(F32)

        def add(k):
            s = other(k)

            def run():
                piece_arrival(l, r, s).wait_recv()
                total_s[l, :, columns(r)] = total_s[l, :, columns(r)] + part_s[
                    l, slot_of(s, g), :, columns(r)
                ].astype(F32)

            unless_relayed(s, run, line_back)

        each(1, dp, add)

    x_in[0] = h_ref[p]
    enc = enc_ref[p]

    def make_result(l):
        def make_three(part):
            return dot_nt(
                hid_s[l, part * half : (part + 1) * half], weights(l, 2 * ff, 3 * ff)
            )

        return make_three

    def forward(l, carry):
        poll(l, 0)
        issue_after(l, 0)
        x0 = x_in[l].astype(F32)
        n1 = (x0 * norm_scale(x0) * gains_s[l, 0:1]).astype(BF16)
        n_one[l] = n1
        qkv = dot_nn(n1, weights(l, c_q, c_so)).astype(BF16)
        qkv_s[l] = qkv
        q = qkv[:, :inner]
        k = qkv[:, inner : 2 * inner]
        v = qkv[:, 2 * inner :]
        e = jnp.exp(dot_nt(spread_heads(q, masks), k) + bias_s[l])
        prob = e * (1.0 / jnp.sum(e, axis=-1, keepdims=True))
        p_s[l] = prob
        so_s[l] = join_heads(dot_nn(prob.astype(BF16), v), masks).astype(BF16)

        def make_one(part):
            return dot_nt(so_s[l, part * half : (part + 1) * half], weights(l, c_so, c_cq))

        def cover_one():
            poll(l, 1)
            issue_after(l, 1)
            ckv_s[l] = dot_nn(enc, weights(l, c_ck, c_co)).astype(BF16)

        x1 = x0 + all_sum(3 * l, make_one, cover_one)
        r_one[l] = x1
        n2 = (x1 * norm_scale(x1) * gains_s[l, 1:2]).astype(BF16)
        n_two[l] = n2
        cq = dot_nn(n2, weights(l, c_cq, c_ck)).astype(BF16)
        cq_s[l] = cq
        ckv = ckv_s[l]
        ck = ckv[:, :inner]
        cv = ckv[:, inner:]
        e = jnp.exp(
            dot_nt(spread_heads(cq, masks), ck) + jnp.concatenate([cmask] * heads, axis=0)
        )
        prob = e * (1.0 / jnp.sum(e, axis=-1, keepdims=True))
        pc_s[l] = prob
        co_s[l] = join_heads(dot_nn(prob.astype(BF16), cv), masks).astype(BF16)

        def make_two(part):
            return dot_nt(co_s[l, part * half : (part + 1) * half], weights(l, c_co, c_end))

        def cover_two():
            poll(l, 2)
            issue_after(l, 2)

        x2 = x1 + all_sum(3 * l + 1, make_two, None, cover_two)
        r_two[l] = x2
        n3 = (x2 * norm_scale(x2) * gains_s[l, 2:3]).astype(BF16)
        n_three[l] = n3
        gu = dot_nn(n3, weights(l, 0, 2 * ff))
        gu_s[l] = gu
        value, _ = gelu_parts(gu[:, :ff])
        hid_s[l] = (value * gu[:, ff:]).astype(BF16)

        @pl.when(l == layers - 1)
        def _():
            keep(l, 0, dot_tn(up_ref[p], hid_s[l]))
            swap_copy(l, 0).start()
            send_pieces(l, 0)

        poll(l, 3)
        issue_after(l, 3)

        @pl.when(l < layers - 1)
        def _():
            x_in[l + 1] = (x2 + all_sum(3 * l + 2, make_result(l))).astype(BF16)

        return carry

    lax.fori_loop(0, layers, forward, 0)
    last = 3 * layers - 1
    sum_start(last, make_result(layers - 1))
    g_in[...] = up_ref[p]

    def attend_back(grad, query, keys, values, attended, prob):
        gs = spread_heads(grad, masks)
        qs = spread_heads(query, masks)
        delta = jnp.sum(
            gs.astype(F32) * jnp.concatenate([attended.astype(F32)] * heads, axis=0),
            axis=-1,
            keepdims=True,
        )
        ds = prob * (dot_nt(gs, values) - delta)
        dsb = ds.astype(BF16)
        grad_query = join_heads(dot_nn(dsb, keys), masks).astype(BF16)
        return grad_query, ds, dsb, gs, qs

    def backward(step, carry):
        l = layers - 1 - step
        base = 3 * layers + 3 * step
        g3 = g_in[...]
        gf = g3.astype(F32)
        gu = gu_s[l]
        value, slope = gelu_parts(gu[:, :ff])
        dh = dot_nn(g3, weights(l, 2 * ff, 3 * ff))
        dgu = jnp.concatenate(
            [(dh * gu[:, ff:] * slope).astype(BF16), (dh * value).astype(BF16)], axis=1
        )

        def make_three(part):
            return dot_nt(dgu[part * half : (part + 1) * half], weights(l, 0, 2 * ff))

        def cover_three():
            @pl.when(step > 0)
            def _():
                keep(l, 0, dot_tn(g3, hid_s[l]))
                swap_copy(l, 0).start()

            keep(l, 1, dot_tn(n_three[l], dgu))
            swap_copy(l, 1).start()

            @pl.when(step == 0)
            def _():
                sum_middle(last)

            @pl.when(step > 0)
            def _():
                pass_on(l + 1, 3)

        def later_three():
            @pl.when(step > 0)
            def _():
                send_pieces(l, 0)

            send_pieces(l, 1)

        dn = all_sum(base, make_three, cover_three, later_three)
        back, gain_three = norm_back(r_two[l], gains_s[l, 2:3], dn)
        g2 = gf + back
        g2b = g2.astype(BF16)
        dc = dot_nn(g2b, weights(l, c_co, c_end)).astype(BF16)
        ckv = ckv_s[l]
        co = co_s[l]
        pc = pc_s[l]
        dcq, _, dsb, gs, qs = attend_back(dc, cq_s[l], ckv[:, :inner], ckv[:, inner:], co, pc)

        def make_two(part):
            return dot_nt(dcq[part * half : (part + 1) * half], weights(l, c_cq, c_ck))

        def cover_two():
            dck = dot_tn(dsb, qs).astype(BF16)
            dcv = dot_tn(pc.astype(BF16), gs).astype(BF16)
            dckv = jnp.concatenate([dck, dcv], axis=1)
            blocks = inner // chunk
            for k in range(D // inner):
                owner = t if k == 0 else peers[k - 1]
                rows_of = w_ref[l, pl.ds(owner * blocks, blocks), :, c_ck:c_co]
                part = dot_nt(rows_of.reshape(inner, 2 * inner), dckv)
                if k == 0:
                    enc_own[l] = part
                else:
                    enc_send[l, k - 1] = part.astype(BF16)
                    enc_copy(l, k - 1).start()
            keep(
                l,
                2,
                jnp.concatenate(
                    [dot_tn(n_two[l], dcq), dot_tn(enc, dckv), dot_tn(g2b, co)], axis=1
                ),
            )
            swap_copy(l, 2).start()

            @pl.when(step == 0)
            def _():
                x_in[layers] = (r_two[layers - 1] + sum_end(last)).astype(BF16)

        def later_two():
            send_pieces(l, 2)
            pass_on(l, 0)
            pass_on(l, 1)

        dn = all_sum(base + 1, make_two, cover_two, later_two)
        back, gain_two = norm_back(r_one[l], gains_s[l, 1:2], dn)
        g1 = g2 + back
        g1b = g1.astype(BF16)
        dself = dot_nn(g1b, weights(l, c_so, c_cq)).astype(BF16)
        qkv = qkv_s[l]
        so = so_s[l]
        ps = p_s[l]
        dq, ds, dsb, gs, qs = attend_back(
            dself, qkv[:, :inner], qkv[:, inner : 2 * inner], qkv[:, 2 * inner :], so, ps
        )
        dk = dot_tn(dsb, qs).astype(BF16)
        dv = dot_tn(ps.astype(BF16), gs).astype(BF16)
        dqkv = jnp.concatenate([dq, dk, dv], axis=1)

        def make_one(part):
            return dot_nt(dqkv[part * half : (part + 1) * half], weights(l, c_q, c_so))

        def cover_one():
            keep(l, 3, jnp.concatenate([dot_tn(n_one[l], dqkv), dot_tn(g1b, so)], axis=1))
            swap_copy(l, 3).start()

        def later_one():
            send_pieces(l, 3)
            pass_on(l, 2)
            buckets = bmap_s[...]
            for h in range(heads):
                ds_h = ds[h * rows : (h + 1) * rows]
                for b in range(BUCKETS):
                    table_s[h, b : b + 1] = jnp.sum(
                        jnp.where(buckets == float(b), ds_h, 0.0), axis=0, keepdims=True
                    )

        dn = all_sum(base + 2, make_one, cover_one, later_one)
        back, gain_one = norm_back(x_in[l].astype(F32), gains_s[l, 0:1], dn)
        gin = g1 + back
        ingrad_s[l] = gin
        g_in[...] = gin.astype(BF16)
        small_g[l] = jnp.zeros(small_g.shape[1:], F32)
        table = jnp.sum(table_s[...], axis=2)
        for s in range(dp):
            for n, value in enumerate((gain_one, gain_two, gain_three)):
                small_g[l, s, n : n + 1, 0:chunk] = value[:, s * chunk : (s + 1) * chunk]
            for h in range(heads):
                small_g[l, s, 8 + h : 9 + h, 0:table_rows] = table[
                    h : h + 1, s * table_rows : (s + 1) * table_rows
                ]
        return carry

    def enc_copy(l, k):
        return copy_to(
            enc_send.at[l, k],
            enc_recv.at[l, k],
            sem_enc_send.at[l, k],
            sem_enc_recv.at[l, k],
            {"tensor": peers[k]},
        )

    lax.fori_loop(0, layers, backward, 0)

    def grad_small_copy(l, s, src_p, src_g, ids):
        return copy_to(
            small_g.at[l, s],
            small_out.at[src_p, src_g],
            sem_sg_send.at[l, s],
            sem_sg_recv.at[src_p, src_g],
            ids,
        )

    small_out[p, g] = small_g[p, g]
    grad_small_copy(o, g, p, g, {"pipe": o}).start()

    def grad_small_start(k):
        s = other(k)
        grad_small_copy(p, s, p, g, {"dp": s}).start()
        grad_small_copy(o, s, p, g, {"dp": s, "pipe": o}).start()

    each(1, dp, grad_small_start)
    pass_on(0, 3)

    for l in range(layers):
        total = enc_own[l]
        for k in range(3):
            enc_copy(l, k).wait()
            total = total + enc_recv[l, k].astype(F32)
        enc_own[l] = total

    moved = (
        (x_in.at[o + 1], sect_out.at[p]),
        (ingrad_s.at[o], ingrad_out.at[p]),
        (enc_own.at[o], enc_out.at[p]),
    )

    def moved_copy(n):
        src, dst = moved[n]
        return copy_to(src, dst, sem_o_send.at[n], sem_o_recv.at[n], {"pipe": o})

    for n in range(3):
        moved_copy(n).start()
    sect_out[p] = x_in[p + 1]
    ingrad_out[p] = ingrad_s[p]
    enc_out[p] = enc_own[p]

    def final_copy(r):
        return copy_to(
            total_s.at[o, :, columns(r)],
            sum_out.at[p, :, columns(r)],
            sem_f_send.at[r],
            sem_f_recv.at[r],
            {"pipe": o},
        )

    for r in range(parts):
        for l in reversed(range(layers)):
            total_of(l, r)
        sum_out[p, :, columns(r)] = total_s[p, :, columns(r)]
        final_copy(r).start()

    def arrival(view, sem):
        copy_to(view, view, sem, sem, {"pipe": o}).wait_recv()

    for r in range(parts):
        final_copy(r).wait_send()
        arrival(sum_out.at[o, :, columns(r)], sem_f_recv.at[r])
    for n in range(3):
        moved_copy(n).wait_send()
        arrival(moved[n][1], sem_o_recv.at[n])
    grad_small_copy(o, g, p, g, {"pipe": o}).wait_send()
    grad_small_copy(o, g, o, g, {"pipe": o}).wait_recv()

    def grad_small_end(k):
        s = other(k)
        grad_small_copy(p, s, p, g, {"dp": s}).wait_send()
        grad_small_copy(o, s, p, g, {"dp": s}).wait_send()
        grad_small_copy(p, s, p, s, {"dp": s}).wait_recv()
        grad_small_copy(o, s, o, s, {"dp": s}).wait_recv()

    each(1, dp, grad_small_end)
    small_copy({"pipe": o}, p, g, 0, 1).wait_send()

    def small_end(k):
        small_copy({"dp": other(k)}, p, g, k, 0).wait_send()
        small_copy({"dp": other(k)}, p, g, k, 1).wait_send()

    each(1, dp, small_end)
    for c in range(4):
        own_copy(c).wait_send()

    def layer_end(l, carry):
        for c in range(4):

            def sent_end(k):
                s = other(k)
                unless_relayed(s, lambda: z_copy(l, c, g, s, s).wait_send())
                relays(s, lambda: z_copy(l, c, s, dp - 1 - s, g).wait_send())
                p_copy(l, c, s, p).wait_send()

            each(1, dp, sent_end)
        for r in range(parts):
            swap_copy(l, r).wait_send()
            each(1, dp, lambda k: piece_copy(l, r, other(k)).wait_send())
        return carry

    lax.fori_loop(0, layers, layer_end, 0)


def run_main(inputs, layers, dp):
    h, enc, wq, gate, table = inputs[0], inputs[1], inputs[6], inputs[14], inputs[18]
    rows, enc_rows = h.shape[1], enc.shape[1]
    chunk, inner, ff = wq.shape[0], wq.shape[1], gate.shape[1]
    heads, table_rows = inner // HEAD, table.shape[1]
    half = rows // 2
    slots = 6 * layers
    width = 3 * ff + 8 * inner
    small = (16, -(-chunk // 128) * 128)
    vm = pltpu.VMEM
    dma = pltpu.SemaphoreType.DMA
    dims = (layers, dp, rows, inner, ff, heads, chunk, table_rows)
    return pl.pallas_call(
        functools.partial(main_kernel, dims),
        out_shape=(
            jax.ShapeDtypeStruct((2, chunk, width // 2), F32),
            jax.ShapeDtypeStruct((2, rows, D), BF16),
            jax.ShapeDtypeStruct((2, rows, D), F32),
            jax.ShapeDtypeStruct((2, inner, enc_rows), F32),
            jax.ShapeDtypeStruct((2, dp) + small, F32),
        ),
        in_specs=[pl.BlockSpec(memory_space=pltpu.VMEM)] * 19,
        out_specs=(pl.BlockSpec(memory_space=pltpu.VMEM),) * 5,
        scratch_shapes=[
            vm((layers, dp, chunk, width), BF16),
            vm((layers, dp) + small, F32),
            vm((layers, 8, D), F32),
            vm((layers, heads * rows, rows), F32),
            vm((rows, rows), F32),
            vm((layers + 1, rows, D), BF16),
            vm((rows, D), BF16),
            vm((layers, rows, D), F32),
            vm((layers, rows, D), F32),
            vm((layers, rows, D), BF16),
            vm((layers, rows, D), BF16),
            vm((layers, rows, D), BF16),
            vm((layers, rows, 3 * inner), BF16),
            vm((layers, rows, inner), BF16),
            vm((layers, heads * rows, rows), F32),
            vm((layers, rows, inner), BF16),
            vm((layers, enc_rows, 2 * inner), BF16),
            vm((layers, rows, inner), BF16),
            vm((layers, heads * rows, enc_rows), F32),
            vm((layers, rows, 2 * ff), F32),
            vm((layers, rows, ff), BF16),
            vm((slots, 2, half, D), BF16),
            vm((slots, 2, half, D), BF16),
            vm((slots, 2, half, D), BF16),
            vm((slots, 2, half, D), BF16),
            vm((layers, 3, inner, enc_rows), BF16),
            vm((layers, inner, enc_rows), F32),
            vm((layers, 3, inner, enc_rows), BF16),
            vm((layers, 2, dp, chunk, width // 2), BF16),
            vm((layers, dp, chunk, width // 2), BF16),
            vm((layers, dp - 1, chunk, width // 2), BF16),
            vm((layers, chunk, width // 2), BF16),
            vm((layers, chunk, width // 2), F32),
            vm((layers, rows, D), F32),
            vm((heads, BUCKETS, rows), F32),
            vm((layers, dp) + small, F32),
            dma((slots, 4)),
            dma((slots, 4)),
            dma((layers, 3)),
            dma((layers, 3)),
            dma((4,)),
            dma((4,)),
            dma((layers, 4, dp)),
            dma((layers, 4, dp)),
            dma((layers, 4, dp)),
            dma((layers, 4, dp)),
            dma((layers, 4)),
            dma((layers, 4)),
            dma((layers, 4, dp)),
            dma((layers, 4, dp)),
            dma((layers, 4)),
            dma((4,)),
            dma((4,)),
            dma((3,)),
            dma((3,)),
            dma((2, dp)),
            dma((2, dp)),
            dma((2, dp)),
            dma((2, dp)),
        ],
        compiler_params=pltpu.CompilerParams(
            collective_id=0, has_side_effects=True, vmem_limit_bytes=60 * 1024 * 1024
        ),
    )(*inputs)


def finish_kernel(dims, *refs):
    inner, ff, heads, chunk, table_rows = dims
    sum_hbm, sect_ref, ingrad_ref, enc_ref, small_hbm = refs[:5]
    (sect_out, ingrad_out, enc_out, q_out, k_out, v_out, o_out, cq_out, ck_out, cv_out) = refs[5:15]
    co_out, gate_out, up_out, down_out, gain_out, tab_out = refs[15:21]
    sum_ref, small_ref, sem = refs[21:]
    _, summed = layout(inner, ff)

    def take(a, n):
        offset = 0
        for start, width in summed:
            if start <= a < start + width:
                pieces = []
                for side in range(2):
                    low = max(a, start + side * (width // 2))
                    high = min(a + n, start + (side + 1) * (width // 2))
                    if low < high:
                        at = offset + low - start - side * (width // 2)
                        pieces.append(sum_ref[side, :, at : at + high - low])
                return pieces[0] if len(pieces) == 1 else jnp.concatenate(pieces, axis=1)
            offset += width // 2

    copies = [
        pltpu.make_async_copy(src, dst, sem.at[n])
        for n, (src, dst) in enumerate(
            ((sum_hbm, sum_ref), (small_hbm, small_ref), (sect_ref, sect_out))
            + ((ingrad_ref, ingrad_out), (enc_ref, enc_out))
        )
    ]
    for copy in copies:
        copy.start()
    copies[1].wait()
    small = jnp.sum(small_ref[...], axis=(0, 1))
    for n in range(3):
        gain_out[n] = small[n : n + 1, 0:chunk]
    for h in range(heads):
        tab_out[h] = small[8 + h : 9 + h, 0:table_rows]
    copies[0].wait()
    c = 3 * ff
    for n, out in enumerate((q_out, k_out, v_out, o_out, cq_out, ck_out, cv_out, co_out)):
        value = take(c + n * inner, inner)
        out[...] = value.T if n % 4 == 3 else value
    gate_out[...] = take(0, ff)
    up_out[...] = take(ff, ff)
    down_out[...] = take(2 * ff, ff)
    for copy in copies[2:]:
        copy.wait()


def run_finish(parts, inner, ff, chunk, table_rows):
    heads = inner // HEAD
    total, sect, ingrad, enc, small = parts
    into, outer = (chunk, inner), (inner, chunk)
    shapes = [sect.shape, ingrad.shape, enc.shape]
    shapes += [into, into, into, outer] * 2
    shapes += [(chunk, ff), (chunk, ff), (chunk, ff), (3, 1, chunk), (heads, 1, table_rows)]
    types = [BF16] + [F32] * 15
    return pl.pallas_call(
        functools.partial(finish_kernel, (inner, ff, heads, chunk, table_rows)),
        out_shape=tuple(jax.ShapeDtypeStruct(s, d) for s, d in zip(shapes, types)),
        in_specs=[pl.BlockSpec(memory_space=pltpu.HBM)] * 5,
        out_specs=(pl.BlockSpec(memory_space=pltpu.VMEM),) * 16,
        scratch_shapes=[
            pltpu.VMEM(total.shape, F32),
            pltpu.VMEM(small.shape, F32),
            pltpu.SemaphoreType.DMA((5,)),
        ],
        compiler_params=pltpu.CompilerParams(vmem_limit_bytes=60 * 1024 * 1024),
    )(*parts)


def body(*args):
    layers = lax.axis_size("pipe")
    dp = lax.axis_size("dp")
    inputs = list(args[:5]) + [args[5].reshape(1, -1)] + [value[0] for value in args[6:]]
    inputs[16], inputs[18] = inputs[16].T, inputs[18].T
    chunk, inner = inputs[6].shape
    ff, table_rows = inputs[14].shape[1], inputs[18].shape[1]
    parts = run_main(inputs, layers, dp)
    outs = run_finish(parts, inner, ff, chunk, table_rows)
    outs = list(outs)
    outs[2] = outs[2].transpose(0, 2, 1)
    outs[13] = outs[13].T
    gain, table = outs[14].transpose(1, 0, 2), outs[15].transpose(1, 2, 0)
    return tuple(value[None] for value in outs[:14]) + (gain, table)


def solution(mesh):
    inner_spec = P("pipe", "dp", "tensor")
    outer_spec = P("pipe", "tensor", "dp")
    placed = (
        P(None, "dp", None),
        P(None, "dp", None),
        P(None, "dp", None),
        P(None, "dp"),
        P(None, "dp"),
        P(),
        inner_spec,
        inner_spec,
        inner_spec,
        outer_spec,
        inner_spec,
        inner_spec,
        inner_spec,
        outer_spec,
        inner_spec,
        inner_spec,
        outer_spec,
        P("pipe", None, "dp"),
        inner_spec,
    )
    return jax.shard_map(
        body,
        mesh=mesh,
        in_specs=placed,
        out_specs=(
            P("pipe", None, "dp", None),
            P("pipe", None, "dp", None),
            P("pipe", None, "dp", "tensor"),
            inner_spec,
            inner_spec,
            inner_spec,
            outer_spec,
            inner_spec,
            inner_spec,
            inner_spec,
            outer_spec,
            inner_spec,
            inner_spec,
            outer_spec,
            P("pipe", None, "dp"),
            inner_spec,
        ),
        check_vma=False,
    )
```

```python
import functools

import jax
import jax.numpy as jnp
from jax import lax
from jax.experimental import pallas as pl
from jax.experimental.pallas import tpu as pltpu
from jax.sharding import PartitionSpec as P

D = 768
HEAD = 64
BUCKETS = 32
MAXD = 128
EPS = 1e-06
AHEAD = 3
AHEAD_END = 2
RELAY_WEIGHTS = True
RELAY_GRADS = True

F32 = jnp.float32
BF16 = jnp.bfloat16
MESH = pl.DeviceIdType.MESH


def dot_nn(a, b):
    return lax.dot_general(a, b, (((1,), (0,)), ((), ())), preferred_element_type=F32)


def dot_nt(a, b):
    return lax.dot_general(a, b, (((1,), (1,)), ((), ())), preferred_element_type=F32)


def dot_tn(a, b):
    return lax.dot_general(a, b, (((0,), (0,)), ((), ())), preferred_element_type=F32)


def norm_scale(values):
    return lax.rsqrt(jnp.mean(values * values, axis=-1, keepdims=True) + EPS)


def norm_back(values, gain, cotangent):
    scale = norm_scale(values)
    scaled = cotangent * gain
    inner = jnp.mean(scaled * values, axis=-1, keepdims=True)
    back = scale * scaled - values * (scale * scale * scale * inner)
    gain_grad = jnp.sum(cotangent * values * scale, axis=0, keepdims=True)
    return back, gain_grad


def gelu_parts(u):
    root = 0.7978845608028654
    cube = 0.044715
    t = jnp.tanh(root * (u + cube * u * u * u))
    value = 0.5 * u * (1.0 + t)
    slope = 0.5 * (1.0 + t) + 0.5 * u * (1.0 - t * t) * (root * (1.0 + 3.0 * cube * u * u))
    return value, slope


def head_masks(heads):
    lane = lax.broadcasted_iota(jnp.int32, (1, heads * HEAD), 1)
    return [
        ((lane >= h * HEAD) & (lane < (h + 1) * HEAD)).astype(F32).astype(BF16)
        for h in range(heads)
    ]


def spread_heads(values, masks):
    return jnp.concatenate([values * m for m in masks], axis=0)


def join_heads(values, masks):
    rows = values.shape[0] // len(masks)
    total = None
    for h, m in enumerate(masks):
        term = values[h * rows : (h + 1) * rows] * m.astype(F32)
        total = term if total is None else total + term
    return total


def each(low, high, run):
    if high - low <= 4:
        for k in range(low, high):
            run(k)
    else:
        lax.fori_loop(low, high, lambda k, c: (run(k), c)[1], 0)


def layout(inner, ff):
    sa, ca = 3 * ff, 3 * ff + 4 * inner
    sent = ((sa, 4 * inner), (ca, 4 * inner), (0, 2 * ff), (2 * ff, ff))
    summed = ((2 * ff, ff), (0, 2 * ff), (ca, 4 * inner), (sa, 4 * inner))
    return sent, summed


def main_kernel(
    dims,
    h_ref,
    enc_ref,
    up_ref,
    dec_ref,
    seg_ref,
    buck_ref,
    wq_ref,
    wk_ref,
    wv_ref,
    wo_ref,
    cq_ref,
    ck_ref,
    cv_ref,
    co_ref,
    gate_ref,
    upw_ref,
    down_ref,
    gain_ref,
    tab_ref,
    sum_out,
    sect_out,
    ingrad_out,
    enc_out,
    small_out,
    w_ref,
    small_w,
    gains_s,
    bias_s,
    bmap_s,
    x_in,
    g_in,
    r_one,
    r_two,
    n_one,
    n_two,
    n_three,
    qkv_s,
    so_s,
    p_s,
    cq_s,
    ckv_s,
    co_s,
    pc_s,
    gu_s,
    hid_s,
    send_one,
    recv_one,
    send_two,
    recv_two,
    enc_send,
    enc_own,
    enc_recv,
    grad_s,
    swap_s,
    part_s,
    relay_s,
    total_s,
    ingrad_s,
    table_s,
    small_g,
    sem_send,
    sem_recv,
    sem_enc_send,
    sem_enc_recv,
    sem_own_send,
    sem_own_recv,
    sem_z_send,
    sem_z_recv,
    sem_p_send,
    sem_p_recv,
    sem_sw_send,
    sem_sw_recv,
    sem_g_send,
    sem_g_recv,
    sem_r_recv,
    sem_f_send,
    sem_f_recv,
    sem_o_send,
    sem_o_recv,
    sem_sm_send,
    sem_sm_recv,
    sem_sg_send,
    sem_sg_recv,
    sem_local,
):
    layers, dp, rows, inner, ff, heads, chunk, table_rows = dims
    half = rows // 2
    p = lax.axis_index("pipe")
    o = 1 - p
    g = lax.axis_index("dp")
    t = lax.axis_index("tensor")
    near = t + 1 - 2 * (t % 2)
    far = t + 2 - 4 * ((t // 2) % 2)
    both = far + 1 - 2 * (far % 2)
    peers = (near, far, both)
    way = 1 - 2 * (g // ((dp + 1) // 2))
    line = dp == 4 and RELAY_WEIGHTS
    line_back = dp == 4 and RELAY_GRADS
    masks = head_masks(heads)
    c_q = 3 * ff
    c_so = c_q + 3 * inner
    c_cq = c_q + 4 * inner
    c_ck = c_q + 5 * inner
    c_cv = c_q + 6 * inner
    c_co = c_q + 7 * inner
    c_end = c_q + 8 * inner
    sent, summed = layout(inner, ff)
    parts = len(summed)
    offsets = [sum(n for _, n in summed[:r]) // 2 for r in range(parts)]

    barrier = pltpu.get_barrier_semaphore()

    def greet(ids):
        pl.semaphore_signal(barrier, inc=1, device_id=ids, device_id_type=MESH)

    for peer in peers:
        greet({"tensor": peer})
    greet({"pipe": o})

    def greet_group(k):
        s = lax.rem(g + k, dp)
        greet({"dp": s})
        greet({"dp": s, "pipe": o})

    each(1, dp, greet_group)

    def copy_to(src, dst, sem_a, sem_b, ids):
        return pltpu.make_async_remote_copy(
            src_ref=src,
            dst_ref=dst,
            send_sem=sem_a,
            recv_sem=sem_b,
            device_id=ids,
            device_id_type=MESH,
        )

    def other(k):
        return lax.rem(g + dp + way * k, dp)

    def pack(c, value):
        a, n = sent[c]
        w_ref[p, g, :, a : a + n] = value

    small_w[p, g] = jnp.zeros(small_w.shape[2:], F32)
    small_w[p, g, 0:3, 0:chunk] = gain_ref[...].astype(F32)
    small_w[p, g, 8 : 8 + heads, 0:table_rows] = tab_ref[...].astype(F32)
    pack(
        0, jnp.concatenate([wq_ref[...], wk_ref[...], wv_ref[...], wo_ref[...].T], axis=1)
    )
    pl.semaphore_wait(barrier, 3 + 1 + 2 * (dp - 1))

    def small_copy(ids, src_p, src_g, k, way_p):
        view = small_w.at[src_p, src_g]
        return copy_to(
            view, view, sem_sm_send.at[way_p, k], sem_sm_recv.at[src_p, src_g], ids
        )

    small_copy({"pipe": o}, p, g, 0, 1).start()

    def small_start(k):
        small_copy({"dp": other(k)}, p, g, k, 0).start()
        small_copy({"dp": other(k), "pipe": o}, p, g, k, 1).start()

    each(1, dp, small_start)

    def own_copy(c):
        a, n = sent[c]
        return copy_to(
            w_ref.at[p, g, :, a : a + n],
            w_ref.at[p, g, :, a : a + n],
            sem_own_send.at[c],
            sem_own_recv.at[c],
            {"pipe": o},
        )

    def own_arrival(c):
        a, n = sent[c]
        view = w_ref.at[o, g, :, a : a + n]
        copy_to(view, view, sem_own_send.at[c], sem_own_recv.at[c], {"pipe": o}).wait_recv()

    def view_of(l, c, s, side):
        a, n = sent[c]
        width = n // 2
        return w_ref.at[l, s, :, pl.ds(pl.multiple_of(a + side * width, 128), width)]

    def z_copy(l, c, s, target, sem):
        view = view_of(l, c, s, p)
        return copy_to(
            view, view, sem_z_send.at[l, c, sem], sem_z_recv.at[l, c, s], {"dp": target}
        )

    def p_copy(l, c, s, side):
        view = view_of(l, c, s, side)
        return copy_to(view, view, sem_p_send.at[l, c, s], sem_p_recv.at[l, c, s], {"pipe": o})

    def far_apart(a, b):
        return jnp.abs(a - b) == dp - 1

    def unless_relayed(s, run, relayed=line):
        if relayed:
            pl.when(jnp.logical_not(far_apart(g, s)))(run)
        else:
            run()

    def issue(l, c):
        @pl.when(l != p)
        def _():
            own_arrival(c)

        def start(k):
            s = other(dp - k)
            unless_relayed(s, lambda: z_copy(l, c, g, s, s).start())

        each(1, dp, start)

    def relays(s, run):
        if line:
            inside = (g == 1) | (g == 2)
            pl.when(inside & (s == lax.rem(g + 2, dp)))(run)

    def poll(l, c):
        def arrive(k):
            s = other(k)
            z_copy(l, c, s, s, s).wait_recv()
            relays(s, lambda: z_copy(l, c, s, dp - 1 - s, g).start())
            p_copy(l, c, s, p).start()

        each(1, dp, arrive)
        each(1, dp, lambda k: p_copy(l, c, other(k), o).wait_recv())

    own_copy(0).start()
    pack(
        1, jnp.concatenate([cq_ref[...], ck_ref[...], cv_ref[...], co_ref[...].T], axis=1)
    )
    own_copy(1).start()
    issue(0, 0)
    pack(2, jnp.concatenate([gate_ref[...], upw_ref[...]], axis=1))
    own_copy(2).start()
    pack(3, down_ref[...])
    own_copy(3).start()
    inner_group = (g > 0) & (g < dp - 1)
    paces = ((inner_group, AHEAD), (jnp.logical_not(inner_group), AHEAD_END))

    for mine, ahead in paces:

        @pl.when(mine)
        def _():
            for c in range(1, ahead):
                issue(0, c)

    def issue_after(l, c):
        for mine, ahead in paces:
            nl, nc = l + (c + ahead) // 4, (c + ahead) % 4

            @pl.when(mine & (nl < layers))
            def _():
                issue(nl, nc)

    ri = lax.broadcasted_iota(jnp.int32, (rows, rows), 0)
    ci = lax.broadcasted_iota(jnp.int32, (rows, rows), 1)
    dec_row = dec_ref[pl.ds(p, 1), :].astype(F32)
    enc_row = seg_ref[pl.ds(p, 1), :].astype(F32)
    dec_col = jnp.sum(jnp.where(ri == ci, dec_row, 0.0), axis=1, keepdims=True)
    allowed = (dec_col == dec_row) & (ci <= ri)
    cmask = jnp.where(dec_col == enc_row, 0.0, -1e30)
    bi = lax.broadcasted_iota(jnp.int32, (BUCKETS, MAXD), 0)
    starts = jnp.sum(jnp.where(buck_ref[...] < bi, 1.0, 0.0), axis=1, keepdims=True)
    dist = jnp.clip(ri - ci, 0, MAXD - 1).astype(F32)
    bmap = jnp.zeros((rows, rows), F32)
    for b in range(1, BUCKETS):
        bmap = bmap + jnp.where(dist >= starts[b : b + 1], 1.0, 0.0)
    bmap_s[...] = bmap

    def small_arrive(k):
        s = other(k)
        small_copy({"dp": s}, p, s, k, 0).wait_recv()
        small_copy({"dp": s}, o, s, k, 0).wait_recv()

    each(1, dp, small_arrive)
    small_copy({"pipe": o}, o, g, 0, 1).wait_recv()
    for l in range(layers):
        for n in range(3):
            gains_s[l, n : n + 1] = jnp.concatenate(
                [small_w[l, s, n : n + 1, 0:chunk] for s in range(dp)], axis=1
            )
        for h in range(heads):
            bias = jnp.zeros((rows, rows), F32)
            for b in range(BUCKETS):
                at = b % table_rows
                value = small_w[l, b // table_rows, 8 + h : 9 + h, at : at + 1]
                bias = jnp.where(bmap == float(b), value, bias)
            bias_s[l, h * rows : (h + 1) * rows] = jnp.where(allowed, bias, -1e30)

    def weights(l, a, b):
        return w_ref[l, :, :, a:b].reshape(D, b - a)

    def first_copy(slot, part):
        return copy_to(
            send_one.at[slot, part],
            recv_one.at[slot, part],
            sem_send.at[slot, part],
            sem_recv.at[slot, part],
            {"tensor": near if part == 0 else far},
        )

    def second_copy(slot, part):
        return copy_to(
            send_two.at[slot, part],
            recv_two.at[slot, part],
            sem_send.at[slot, part + 2],
            sem_recv.at[slot, part + 2],
            {"tensor": far if part == 0 else near},
        )

    def sum_start(slot, make_half):
        for part in range(2):
            send_one[slot, part] = make_half(part).astype(BF16)
            first_copy(slot, part).start()

    def sum_middle(slot):
        for part in range(2):
            first_copy(slot, part).wait()
            value = send_one[slot, part].astype(F32) + recv_one[slot, part].astype(F32)
            send_two[slot, part] = value.astype(BF16)
            second_copy(slot, part).start()

    def sum_end(slot):
        pieces = []
        for part in range(2):
            second_copy(slot, part).wait()
            pieces.append(send_two[slot, part].astype(F32) + recv_two[slot, part].astype(F32))
        return jnp.concatenate(pieces, axis=0)

    def all_sum(slot, make_half, cover=None, later=None):
        sum_start(slot, make_half)
        if cover is not None:
            cover()
        sum_middle(slot)
        if later is not None:
            later()
        return sum_end(slot)

    def keep(l, r, value):
        width = summed[r][1] // 2
        for side in range(2):
            grad_s[l, side, :, :, offsets[r] : offsets[r] + width] = (
                value[:, side * width : (side + 1) * width].astype(BF16).reshape(dp, chunk, width)
            )

    def columns(r):
        return pl.ds(offsets[r], summed[r][1] // 2)

    def swap_copy(l, r):
        return copy_to(
            grad_s.at[l, o, :, :, columns(r)],
            swap_s.at[l, :, :, columns(r)],
            sem_sw_send.at[l, r],
            sem_sw_recv.at[l, r],
            {"pipe": o},
        )

    def slot_of(source, owner):
        return lax.rem(source - owner + dp, dp) - 1

    def piece_copy(l, r, s):
        return copy_to(
            grad_s.at[l, p, s, :, columns(r)],
            part_s.at[l, slot_of(g, s), :, columns(r)],
            sem_g_send.at[l, r, s],
            sem_g_recv.at[l, r, g],
            {"dp": s},
        )

    def relay_copy(l, r, s):
        return copy_to(
            grad_s.at[l, p, s, :, columns(r)],
            relay_s.at[l, :, columns(r)],
            sem_g_send.at[l, r, s],
            sem_r_recv.at[l, r],
            {"dp": g + 1 - 2 * (g // 2)},
        )

    def piece_arrival(l, r, s):
        return copy_to(
            grad_s.at[l, p, g, :, columns(r)],
            part_s.at[l, slot_of(s, g), :, columns(r)],
            sem_g_send.at[l, r, s],
            sem_g_recv.at[l, r, s],
            {"dp": s},
        )

    def is_inside():
        return (g == 1) | (g == 2)

    def send_pieces(l, r):
        swap_copy(l, r).wait_recv()

        def merge(s):
            grad_s[l, p, s, :, columns(r)] = (
                grad_s[l, p, s, :, columns(r)].astype(F32)
                + swap_s[l, s, :, columns(r)].astype(F32)
            ).astype(BF16)

        each(0, dp, merge)

        def start(k):
            s = other(dp - k)
            if not line_back:
                piece_copy(l, r, s).start()
                return

            @pl.when(far_apart(g, s))
            def _():
                relay_copy(l, r, s).start()

            @pl.when(jnp.abs(g - s) == 1)
            def _():
                piece_copy(l, r, s).start()

            @pl.when((jnp.abs(g - s) == 2) & jnp.logical_not(is_inside()))
            def _():
                piece_copy(l, r, s).start()

        each(1, dp, start)

    def pass_on(l, r):
        if not line_back:
            return

        @pl.when(is_inside())
        def _():
            s = lax.rem(g + 2, dp)
            relay_copy(l, r, s).wait_recv()
            grad_s[l, p, s, :, columns(r)] = (
                grad_s[l, p, s, :, columns(r)].astype(F32) + relay_s[l, :, columns(r)].astype(F32)
            ).astype(BF16)
            piece_copy(l, r, s).start()

    def total_of(l, r):
        total_s[l, :, columns(r)] = grad_s[l, p, g, :, columns(r)].astype(F32)

        def add(k):
            s = other(k)

            def run():
                piece_arrival(l, r, s).wait_recv()
                total_s[l, :, columns(r)] = total_s[l, :, columns(r)] + part_s[
                    l, slot_of(s, g), :, columns(r)
                ].astype(F32)

            unless_relayed(s, run, line_back)

        each(1, dp, add)

    x_in[0] = h_ref[p]
    enc = enc_ref[p]

    def make_result(l):
        def make_three(part):
            return dot_nt(
                hid_s[l, part * half : (part + 1) * half], weights(l, 2 * ff, 3 * ff)
            )

        return make_three

    def forward(l, carry):
        poll(l, 0)
        issue_after(l, 0)
        x0 = x_in[l].astype(F32)
        n1 = (x0 * norm_scale(x0) * gains_s[l, 0:1]).astype(BF16)
        n_one[l] = n1
        qkv = dot_nn(n1, weights(l, c_q, c_so)).astype(BF16)
        qkv_s[l] = qkv
        q = qkv[:, :inner]
        k = qkv[:, inner : 2 * inner]
        v = qkv[:, 2 * inner :]
        e = jnp.exp(dot_nt(spread_heads(q, masks), k) + bias_s[l])
        prob = e * (1.0 / jnp.sum(e, axis=-1, keepdims=True))
        p_s[l] = prob
        so_s[l] = join_heads(dot_nn(prob.astype(BF16), v), masks).astype(BF16)

        def make_one(part):
            return dot_nt(so_s[l, part * half : (part + 1) * half], weights(l, c_so, c_cq))

        def cover_one():
            poll(l, 1)
            issue_after(l, 1)
            ckv_s[l] = dot_nn(enc, weights(l, c_ck, c_co)).astype(BF16)

        x1 = x0 + all_sum(3 * l, make_one, cover_one)
        r_one[l] = x1
        n2 = (x1 * norm_scale(x1) * gains_s[l, 1:2]).astype(BF16)
        n_two[l] = n2
        cq = dot_nn(n2, weights(l, c_cq, c_ck)).astype(BF16)
        cq_s[l] = cq
        ckv = ckv_s[l]
        ck = ckv[:, :inner]
        cv = ckv[:, inner:]
        e = jnp.exp(
            dot_nt(spread_heads(cq, masks), ck) + jnp.concatenate([cmask] * heads, axis=0)
        )
        prob = e * (1.0 / jnp.sum(e, axis=-1, keepdims=True))
        pc_s[l] = prob
        co_s[l] = join_heads(dot_nn(prob.astype(BF16), cv), masks).astype(BF16)

        def make_two(part):
            return dot_nt(co_s[l, part * half : (part + 1) * half], weights(l, c_co, c_end))

        def cover_two():
            poll(l, 2)
            issue_after(l, 2)

        x2 = x1 + all_sum(3 * l + 1, make_two, None, cover_two)
        r_two[l] = x2
        n3 = (x2 * norm_scale(x2) * gains_s[l, 2:3]).astype(BF16)
        n_three[l] = n3
        gu = dot_nn(n3, weights(l, 0, 2 * ff))
        gu_s[l] = gu
        value, _ = gelu_parts(gu[:, :ff])
        hid_s[l] = (value * gu[:, ff:]).astype(BF16)

        @pl.when(l == layers - 1)
        def _():
            keep(l, 0, dot_tn(up_ref[p], hid_s[l]))
            swap_copy(l, 0).start()
            send_pieces(l, 0)

        poll(l, 3)
        issue_after(l, 3)

        @pl.when(l < layers - 1)
        def _():
            x_in[l + 1] = (x2 + all_sum(3 * l + 2, make_result(l))).astype(BF16)

        return carry

    lax.fori_loop(0, layers, forward, 0)
    last = 3 * layers - 1
    sum_start(last, make_result(layers - 1))
    g_in[...] = up_ref[p]

    def attend_back(grad, query, keys, values, attended, prob):
        gs = spread_heads(grad, masks)
        qs = spread_heads(query, masks)
        delta = jnp.sum(
            gs.astype(F32) * jnp.concatenate([attended.astype(F32)] * heads, axis=0),
            axis=-1,
            keepdims=True,
        )
        ds = prob * (dot_nt(gs, values) - delta)
        dsb = ds.astype(BF16)
        grad_query = join_heads(dot_nn(dsb, keys), masks).astype(BF16)
        return grad_query, ds, dsb, gs, qs

    def backward(step, carry):
        l = layers - 1 - step
        base = 3 * layers + 3 * step
        g3 = g_in[...]
        gf = g3.astype(F32)
        gu = gu_s[l]
        value, slope = gelu_parts(gu[:, :ff])
        dh = dot_nn(g3, weights(l, 2 * ff, 3 * ff))
        dgu = jnp.concatenate(
            [(dh * gu[:, ff:] * slope).astype(BF16), (dh * value).astype(BF16)], axis=1
        )

        def make_three(part):
            return dot_nt(dgu[part * half : (part + 1) * half], weights(l, 0, 2 * ff))

        def cover_three():
            @pl.when(step > 0)
            def _():
                keep(l, 0, dot_tn(g3, hid_s[l]))
                swap_copy(l, 0).start()

            keep(l, 1, dot_tn(n_three[l], dgu))
            swap_copy(l, 1).start()

            @pl.when(step == 0)
            def _():
                sum_middle(last)

        def later_three():
            @pl.when(step > 0)
            def _():
                send_pieces(l, 0)

            send_pieces(l, 1)

            @pl.when(step == 0)
            def _():
                pass_on(l, 0)

            @pl.when(step > 0)
            def _():
                pass_on(l + 1, 3)

        dn = all_sum(base, make_three, cover_three, later_three)
        back, gain_three = norm_back(r_two[l], gains_s[l, 2:3], dn)
        g2 = gf + back
        g2b = g2.astype(BF16)
        dc = dot_nn(g2b, weights(l, c_co, c_end)).astype(BF16)
        ckv = ckv_s[l]
        co = co_s[l]
        pc = pc_s[l]
        dcq, _, dsb, gs, qs = attend_back(dc, cq_s[l], ckv[:, :inner], ckv[:, inner:], co, pc)

        def make_two(part):
            return dot_nt(dcq[part * half : (part + 1) * half], weights(l, c_cq, c_ck))

        def cover_two():
            dck = dot_tn(dsb, qs).astype(BF16)
            dcv = dot_tn(pc.astype(BF16), gs).astype(BF16)
            dckv = jnp.concatenate([dck, dcv], axis=1)
            blocks = inner // chunk
            for k in range(D // inner):
                owner = t if k == 0 else peers[k - 1]
                rows_of = w_ref[l, pl.ds(owner * blocks, blocks), :, c_ck:c_co]
                part = dot_nt(rows_of.reshape(inner, 2 * inner), dckv)
                if k == 0:
                    enc_own[l] = part
                else:
                    enc_send[l, k - 1] = part.astype(BF16)
                    enc_copy(l, k - 1).start()
            keep(
                l,
                2,
                jnp.concatenate(
                    [dot_tn(n_two[l], dcq), dot_tn(enc, dckv), dot_tn(g2b, co)], axis=1
                ),
            )
            swap_copy(l, 2).start()

            @pl.when(step == 0)
            def _():
                x_in[layers] = (r_two[layers - 1] + sum_end(last)).astype(BF16)

        def later_two():
            send_pieces(l, 2)

            @pl.when(step > 0)
            def _():
                pass_on(l, 0)

            pass_on(l, 1)

        dn = all_sum(base + 1, make_two, cover_two, later_two)
        back, gain_two = norm_back(r_one[l], gains_s[l, 1:2], dn)
        g1 = g2 + back
        g1b = g1.astype(BF16)
        dself = dot_nn(g1b, weights(l, c_so, c_cq)).astype(BF16)
        qkv = qkv_s[l]
        so = so_s[l]
        ps = p_s[l]
        dq, ds, dsb, gs, qs = attend_back(
            dself, qkv[:, :inner], qkv[:, inner : 2 * inner], qkv[:, 2 * inner :], so, ps
        )
        dk = dot_tn(dsb, qs).astype(BF16)
        dv = dot_tn(ps.astype(BF16), gs).astype(BF16)
        dqkv = jnp.concatenate([dq, dk, dv], axis=1)

        def make_one(part):
            return dot_nt(dqkv[part * half : (part + 1) * half], weights(l, c_q, c_so))

        def cover_one():
            keep(l, 3, jnp.concatenate([dot_tn(n_one[l], dqkv), dot_tn(g1b, so)], axis=1))
            swap_copy(l, 3).start()

        def later_one():
            send_pieces(l, 3)
            pass_on(l, 2)
            buckets = bmap_s[...]
            for h in range(heads):
                ds_h = ds[h * rows : (h + 1) * rows]
                for b in range(BUCKETS):
                    table_s[h, b : b + 1] = jnp.sum(
                        jnp.where(buckets == float(b), ds_h, 0.0), axis=0, keepdims=True
                    )

        dn = all_sum(base + 2, make_one, cover_one, later_one)
        back, gain_one = norm_back(x_in[l].astype(F32), gains_s[l, 0:1], dn)
        gin = g1 + back
        ingrad_s[l] = gin
        g_in[...] = gin.astype(BF16)
        small_g[l] = jnp.zeros(small_g.shape[1:], F32)
        table = jnp.sum(table_s[...], axis=2)
        for s in range(dp):
            for n, value in enumerate((gain_one, gain_two, gain_three)):
                small_g[l, s, n : n + 1, 0:chunk] = value[:, s * chunk : (s + 1) * chunk]
            for h in range(heads):
                small_g[l, s, 8 + h : 9 + h, 0:table_rows] = table[
                    h : h + 1, s * table_rows : (s + 1) * table_rows
                ]
        return carry

    def enc_copy(l, k):
        return copy_to(
            enc_send.at[l, k],
            enc_recv.at[l, k],
            sem_enc_send.at[l, k],
            sem_enc_recv.at[l, k],
            {"tensor": peers[k]},
        )

    lax.fori_loop(0, layers, backward, 0)

    def grad_small_copy(l, s, src_p, src_g, ids):
        return copy_to(
            small_g.at[l, s],
            small_out.at[src_p, src_g],
            sem_sg_send.at[l, s],
            sem_sg_recv.at[src_p, src_g],
            ids,
        )

    def local_copy(n, src, dst):
        return pltpu.make_async_copy(src, dst, sem_local.at[n])

    def own_small():
        return local_copy(3, small_g.at[p, g], small_out.at[p, g])

    own_small().start()
    grad_small_copy(o, g, p, g, {"pipe": o}).start()

    def grad_small_start(k):
        s = other(k)
        grad_small_copy(p, s, p, g, {"dp": s}).start()
        grad_small_copy(o, s, p, g, {"dp": s, "pipe": o}).start()

    each(1, dp, grad_small_start)
    for l in range(layers):
        total = enc_own[l]
        for k in range(3):
            enc_copy(l, k).wait()
            total = total + enc_recv[l, k].astype(F32)
        enc_own[l] = total

    moved = (
        (x_in.at[o + 1], sect_out.at[p]),
        (ingrad_s.at[o], ingrad_out.at[p]),
        (enc_own.at[o], enc_out.at[p]),
    )

    away = (sect_out.at[o], ingrad_out.at[o], enc_out.at[o])

    def moved_copy(n):
        src, dst = moved[n]
        return copy_to(src, dst, sem_o_send.at[n], sem_o_recv.at[n], {"pipe": o})

    kept = (x_in.at[p + 1], ingrad_s.at[p], enc_own.at[p])

    def kept_copy(n):
        return local_copy(n, kept[n], moved[n][1])

    for n in range(3):
        moved_copy(n).start()
        kept_copy(n).start()

    def final_copy(r):
        return copy_to(
            total_s.at[o, :, columns(r)],
            sum_out.at[p, :, columns(r)],
            sem_f_send.at[r],
            sem_f_recv.at[r],
            {"pipe": o},
        )

    def own_total(r):
        return local_copy(4 + r, total_s.at[p, :, columns(r)], sum_out.at[p, :, columns(r)])

    for r in range(parts):
        if r == parts - 1:
            pass_on(0, r)
        for l in reversed(range(layers)):
            total_of(l, r)
        final_copy(r).start()
        own_total(r).start()

    def arrival(view, sem):
        copy_to(view, view, sem, sem, {"pipe": o}).wait_recv()

    for n in range(3):
        moved_copy(n).wait_send()
        kept_copy(n).wait()
        arrival(away[n], sem_o_recv.at[n])
    for r in range(parts):
        final_copy(r).wait_send()
        own_total(r).wait()
        arrival(sum_out.at[o, :, columns(r)], sem_f_recv.at[r])
    own_small().wait()
    grad_small_copy(o, g, p, g, {"pipe": o}).wait_send()
    grad_small_copy(o, g, o, g, {"pipe": o}).wait_recv()

    def grad_small_end(k):
        s = other(k)
        grad_small_copy(p, s, p, g, {"dp": s}).wait_send()
        grad_small_copy(o, s, p, g, {"dp": s}).wait_send()
        grad_small_copy(p, s, p, s, {"dp": s}).wait_recv()
        grad_small_copy(o, s, o, s, {"dp": s}).wait_recv()

    each(1, dp, grad_small_end)
    small_copy({"pipe": o}, p, g, 0, 1).wait_send()

    def small_end(k):
        small_copy({"dp": other(k)}, p, g, k, 0).wait_send()
        small_copy({"dp": other(k)}, p, g, k, 1).wait_send()

    each(1, dp, small_end)
    for c in range(4):
        own_copy(c).wait_send()

    def layer_end(l, carry):
        for c in range(4):

            def sent_end(k):
                s = other(k)
                unless_relayed(s, lambda: z_copy(l, c, g, s, s).wait_send())
                relays(s, lambda: z_copy(l, c, s, dp - 1 - s, g).wait_send())
                p_copy(l, c, s, p).wait_send()

            each(1, dp, sent_end)
        for r in range(parts):
            swap_copy(l, r).wait_send()
            each(1, dp, lambda k: piece_copy(l, r, other(k)).wait_send())
        return carry

    lax.fori_loop(0, layers, layer_end, 0)


def run_main(inputs, layers, dp):
    h, enc, wq, gate, table = inputs[0], inputs[1], inputs[6], inputs[14], inputs[18]
    rows, enc_rows = h.shape[1], enc.shape[1]
    chunk, inner, ff = wq.shape[0], wq.shape[1], gate.shape[1]
    heads, table_rows = inner // HEAD, table.shape[1]
    half = rows // 2
    slots = 6 * layers
    width = 3 * ff + 8 * inner
    small = (16, -(-chunk // 128) * 128)
    vm = pltpu.VMEM
    dma = pltpu.SemaphoreType.DMA
    dims = (layers, dp, rows, inner, ff, heads, chunk, table_rows)
    return pl.pallas_call(
        functools.partial(main_kernel, dims),
        out_shape=(
            jax.ShapeDtypeStruct((2, chunk, width // 2), F32),
            jax.ShapeDtypeStruct((2, rows, D), BF16),
            jax.ShapeDtypeStruct((2, rows, D), F32),
            jax.ShapeDtypeStruct((2, inner, enc_rows), F32),
            jax.ShapeDtypeStruct((2, dp) + small, F32),
        ),
        in_specs=[pl.BlockSpec(memory_space=pltpu.VMEM)] * 19,
        out_specs=(pl.BlockSpec(memory_space=pltpu.HBM),) * 5,
        scratch_shapes=[
            vm((layers, dp, chunk, width), BF16),
            vm((layers, dp) + small, F32),
            vm((layers, 8, D), F32),
            vm((layers, heads * rows, rows), F32),
            vm((rows, rows), F32),
            vm((layers + 1, rows, D), BF16),
            vm((rows, D), BF16),
            vm((layers, rows, D), F32),
            vm((layers, rows, D), F32),
            vm((layers, rows, D), BF16),
            vm((layers, rows, D), BF16),
            vm((layers, rows, D), BF16),
            vm((layers, rows, 3 * inner), BF16),
            vm((layers, rows, inner), BF16),
            vm((layers, heads * rows, rows), F32),
            vm((layers, rows, inner), BF16),
            vm((layers, enc_rows, 2 * inner), BF16),
            vm((layers, rows, inner), BF16),
            vm((layers, heads * rows, enc_rows), F32),
            vm((layers, rows, 2 * ff), F32),
            vm((layers, rows, ff), BF16),
            vm((slots, 2, half, D), BF16),
            vm((slots, 2, half, D), BF16),
            vm((slots, 2, half, D), BF16),
            vm((slots, 2, half, D), BF16),
            vm((layers, 3, inner, enc_rows), BF16),
            vm((layers, inner, enc_rows), F32),
            vm((layers, 3, inner, enc_rows), BF16),
            vm((layers, 2, dp, chunk, width // 2), BF16),
            vm((layers, dp, chunk, width // 2), BF16),
            vm((layers, dp - 1, chunk, width // 2), BF16),
            vm((layers, chunk, width // 2), BF16),
            vm((layers, chunk, width // 2), F32),
            vm((layers, rows, D), F32),
            vm((heads, BUCKETS, rows), F32),
            vm((layers, dp) + small, F32),
            dma((slots, 4)),
            dma((slots, 4)),
            dma((layers, 3)),
            dma((layers, 3)),
            dma((4,)),
            dma((4,)),
            dma((layers, 4, dp)),
            dma((layers, 4, dp)),
            dma((layers, 4, dp)),
            dma((layers, 4, dp)),
            dma((layers, 4)),
            dma((layers, 4)),
            dma((layers, 4, dp)),
            dma((layers, 4, dp)),
            dma((layers, 4)),
            dma((4,)),
            dma((4,)),
            dma((3,)),
            dma((3,)),
            dma((2, dp)),
            dma((2, dp)),
            dma((2, dp)),
            dma((2, dp)),
            dma((8,)),
        ],
        compiler_params=pltpu.CompilerParams(
            collective_id=0, has_side_effects=True, vmem_limit_bytes=60 * 1024 * 1024
        ),
    )(*inputs)


def finish_kernel(dims, *refs):
    inner, ff, heads, chunk, table_rows = dims
    sum_hbm, sect_ref, ingrad_ref, enc_ref, small_hbm = refs[:5]
    (sect_out, ingrad_out, enc_out, q_out, k_out, v_out, o_out, cq_out, ck_out, cv_out) = refs[5:15]
    co_out, gate_out, up_out, down_out, gain_out, tab_out = refs[15:21]
    sum_ref, small_ref, sem = refs[21:]
    _, summed = layout(inner, ff)

    def take(a, n):
        offset = 0
        for start, width in summed:
            if start <= a < start + width:
                pieces = []
                for side in range(2):
                    low = max(a, start + side * (width // 2))
                    high = min(a + n, start + (side + 1) * (width // 2))
                    if low < high:
                        at = offset + low - start - side * (width // 2)
                        pieces.append(sum_ref[side, :, at : at + high - low])
                return pieces[0] if len(pieces) == 1 else jnp.concatenate(pieces, axis=1)
            offset += width // 2

    copies = [
        pltpu.make_async_copy(src, dst, sem.at[n])
        for n, (src, dst) in enumerate(
            ((sum_hbm, sum_ref), (small_hbm, small_ref), (sect_ref, sect_out))
            + ((ingrad_ref, ingrad_out), (enc_ref, enc_out))
        )
    ]
    for copy in copies:
        copy.start()
    copies[1].wait()
    small = jnp.sum(small_ref[...], axis=(0, 1))
    for n in range(3):
        gain_out[n] = small[n : n + 1, 0:chunk]
    for h in range(heads):
        tab_out[h] = small[8 + h : 9 + h, 0:table_rows]
    copies[0].wait()
    c = 3 * ff
    for n, out in enumerate((q_out, k_out, v_out, o_out, cq_out, ck_out, cv_out, co_out)):
        value = take(c + n * inner, inner)
        out[...] = value.T if n % 4 == 3 else value
    gate_out[...] = take(0, ff)
    up_out[...] = take(ff, ff)
    down_out[...] = take(2 * ff, ff)
    for copy in copies[2:]:
        copy.wait()


def run_finish(parts, inner, ff, chunk, table_rows):
    heads = inner // HEAD
    total, sect, ingrad, enc, small = parts
    into, outer = (chunk, inner), (inner, chunk)
    shapes = [sect.shape, ingrad.shape, enc.shape]
    shapes += [into, into, into, outer] * 2
    shapes += [(chunk, ff), (chunk, ff), (chunk, ff), (3, 1, chunk), (heads, 1, table_rows)]
    types = [BF16] + [F32] * 15
    return pl.pallas_call(
        functools.partial(finish_kernel, (inner, ff, heads, chunk, table_rows)),
        out_shape=tuple(jax.ShapeDtypeStruct(s, d) for s, d in zip(shapes, types)),
        in_specs=[pl.BlockSpec(memory_space=pltpu.HBM)] * 5,
        out_specs=(pl.BlockSpec(memory_space=pltpu.VMEM),) * 16,
        scratch_shapes=[
            pltpu.VMEM(total.shape, F32),
            pltpu.VMEM(small.shape, F32),
            pltpu.SemaphoreType.DMA((5,)),
        ],
        compiler_params=pltpu.CompilerParams(vmem_limit_bytes=60 * 1024 * 1024),
    )(*parts)


def body(*args):
    layers = lax.axis_size("pipe")
    dp = lax.axis_size("dp")
    inputs = list(args[:5]) + [args[5].reshape(1, -1)] + [value[0] for value in args[6:]]
    inputs[16], inputs[18] = inputs[16].T, inputs[18].T
    chunk, inner = inputs[6].shape
    ff, table_rows = inputs[14].shape[1], inputs[18].shape[1]
    parts = run_main(inputs, layers, dp)
    outs = run_finish(parts, inner, ff, chunk, table_rows)
    outs = list(outs)
    outs[2] = outs[2].transpose(0, 2, 1)
    outs[13] = outs[13].T
    gain, table = outs[14].transpose(1, 0, 2), outs[15].transpose(1, 2, 0)
    return tuple(value[None] for value in outs[:14]) + (gain, table)


def solution(mesh):
    inner_spec = P("pipe", "dp", "tensor")
    outer_spec = P("pipe", "tensor", "dp")
    placed = (
        P(None, "dp", None),
        P(None, "dp", None),
        P(None, "dp", None),
        P(None, "dp"),
        P(None, "dp"),
        P(),
        inner_spec,
        inner_spec,
        inner_spec,
        outer_spec,
        inner_spec,
        inner_spec,
        inner_spec,
        outer_spec,
        inner_spec,
        inner_spec,
        outer_spec,
        P("pipe", None, "dp"),
        inner_spec,
    )
    return jax.shard_map(
        body,
        mesh=mesh,
        in_specs=placed,
        out_specs=(
            P("pipe", None, "dp", None),
            P("pipe", None, "dp", None),
            P("pipe", None, "dp", "tensor"),
            inner_spec,
            inner_spec,
            inner_spec,
            outer_spec,
            inner_spec,
            inner_spec,
            inner_spec,
            outer_spec,
            inner_spec,
            inner_spec,
            outer_spec,
            P("pipe", None, "dp"),
            inner_spec,
        ),
        check_vma=False,
    )
```

```python
import functools

import jax
import jax.numpy as jnp
from jax import lax
from jax.experimental import pallas as pl
from jax.experimental.pallas import tpu as pltpu
from jax.sharding import PartitionSpec as P

D = 768
HEAD = 64
BUCKETS = 32
MAXD = 128
EPS = 1e-06
AHEAD = 3
AHEAD_END = 2
RELAY_WEIGHTS = True
RELAY_GRADS = True

F32 = jnp.float32
BF16 = jnp.bfloat16
MESH = pl.DeviceIdType.MESH


def dot_nn(a, b):
    return lax.dot_general(a, b, (((1,), (0,)), ((), ())), preferred_element_type=F32)


def dot_nt(a, b):
    return lax.dot_general(a, b, (((1,), (1,)), ((), ())), preferred_element_type=F32)


def dot_tn(a, b):
    return lax.dot_general(a, b, (((0,), (0,)), ((), ())), preferred_element_type=F32)


def norm_scale(values):
    return lax.rsqrt(jnp.mean(values * values, axis=-1, keepdims=True) + EPS)


def norm_back(values, gain, cotangent):
    scale = norm_scale(values)
    scaled = cotangent * gain
    inner = jnp.mean(scaled * values, axis=-1, keepdims=True)
    back = scale * scaled - values * (scale * scale * scale * inner)
    gain_grad = jnp.sum(cotangent * values * scale, axis=0, keepdims=True)
    return back, gain_grad


def gelu_parts(u):
    root = 0.7978845608028654
    cube = 0.044715
    t = jnp.tanh(root * (u + cube * u * u * u))
    value = 0.5 * u * (1.0 + t)
    slope = 0.5 * (1.0 + t) + 0.5 * u * (1.0 - t * t) * (root * (1.0 + 3.0 * cube * u * u))
    return value, slope


def head_masks(heads):
    lane = lax.broadcasted_iota(jnp.int32, (1, heads * HEAD), 1)
    return [
        ((lane >= h * HEAD) & (lane < (h + 1) * HEAD)).astype(F32).astype(BF16)
        for h in range(heads)
    ]


def spread_heads(values, masks):
    return jnp.concatenate([values * m for m in masks], axis=0)


def join_heads(values, masks):
    rows = values.shape[0] // len(masks)
    total = None
    for h, m in enumerate(masks):
        term = values[h * rows : (h + 1) * rows] * m.astype(F32)
        total = term if total is None else total + term
    return total


def each(low, high, run):
    if high - low <= 4:
        for k in range(low, high):
            run(k)
    else:
        lax.fori_loop(low, high, lambda k, c: (run(k), c)[1], 0)


def layout(inner, ff):
    sa, ca = 3 * ff, 3 * ff + 4 * inner
    sent = ((sa, 4 * inner), (ca, 4 * inner), (0, 2 * ff), (2 * ff, ff))
    summed = ((2 * ff, ff), (0, 2 * ff), (ca, 4 * inner), (sa, 4 * inner))
    return sent, summed


def main_kernel(
    dims,
    h_ref,
    enc_ref,
    up_ref,
    dec_ref,
    seg_ref,
    buck_ref,
    wq_ref,
    wk_ref,
    wv_ref,
    wo_ref,
    cq_ref,
    ck_ref,
    cv_ref,
    co_ref,
    gate_ref,
    upw_ref,
    down_ref,
    gain_ref,
    tab_ref,
    sum_out,
    sect_out,
    ingrad_out,
    enc_out,
    small_out,
    w_ref,
    small_w,
    gains_s,
    bias_s,
    bmap_s,
    x_in,
    g_in,
    r_one,
    r_two,
    n_one,
    n_two,
    n_three,
    qkv_s,
    so_s,
    p_s,
    cq_s,
    ckv_s,
    co_s,
    pc_s,
    gu_s,
    hid_s,
    send_one,
    recv_one,
    send_two,
    recv_two,
    enc_send,
    enc_own,
    enc_recv,
    grad_s,
    swap_s,
    part_s,
    relay_s,
    total_s,
    ingrad_s,
    table_s,
    small_g,
    sem_send,
    sem_recv,
    sem_enc_send,
    sem_enc_recv,
    sem_own_send,
    sem_own_recv,
    sem_z_send,
    sem_z_recv,
    sem_p_send,
    sem_p_recv,
    sem_sw_send,
    sem_sw_recv,
    sem_g_send,
    sem_g_recv,
    sem_r_recv,
    sem_f_send,
    sem_f_recv,
    sem_o_send,
    sem_o_recv,
    sem_sm_send,
    sem_sm_recv,
    sem_sg_send,
    sem_sg_recv,
    sem_local,
):
    layers, dp, rows, inner, ff, heads, chunk, table_rows = dims
    half = rows // 2
    p = lax.axis_index("pipe")
    o = 1 - p
    g = lax.axis_index("dp")
    t = lax.axis_index("tensor")
    near = t + 1 - 2 * (t % 2)
    far = t + 2 - 4 * ((t // 2) % 2)
    both = far + 1 - 2 * (far % 2)
    peers = (near, far, both)
    way = 1 - 2 * (g // ((dp + 1) // 2))
    line = dp == 4 and RELAY_WEIGHTS
    line_back = dp == 4 and RELAY_GRADS
    masks = head_masks(heads)
    c_q = 3 * ff
    c_so = c_q + 3 * inner
    c_cq = c_q + 4 * inner
    c_ck = c_q + 5 * inner
    c_cv = c_q + 6 * inner
    c_co = c_q + 7 * inner
    c_end = c_q + 8 * inner
    sent, summed = layout(inner, ff)
    parts = len(summed)
    offsets = [sum(n for _, n in summed[:r]) // 2 for r in range(parts)]

    barrier = pltpu.get_barrier_semaphore()

    def greet(ids):
        pl.semaphore_signal(barrier, inc=1, device_id=ids, device_id_type=MESH)

    for peer in peers:
        greet({"tensor": peer})
    greet({"pipe": o})

    def greet_group(k):
        s = lax.rem(g + k, dp)
        greet({"dp": s})
        greet({"dp": s, "pipe": o})

    each(1, dp, greet_group)

    def copy_to(src, dst, sem_a, sem_b, ids):
        return pltpu.make_async_remote_copy(
            src_ref=src,
            dst_ref=dst,
            send_sem=sem_a,
            recv_sem=sem_b,
            device_id=ids,
            device_id_type=MESH,
        )

    def other(k):
        return lax.rem(g + dp + way * k, dp)

    def pack(c, value):
        a, n = sent[c]
        w_ref[p, g, :, a : a + n] = value

    small_w[p, g] = jnp.zeros(small_w.shape[2:], F32)
    small_w[p, g, 0:3, 0:chunk] = gain_ref[...].astype(F32)
    small_w[p, g, 8 : 8 + heads, 0:table_rows] = tab_ref[...].astype(F32)
    pack(
        0, jnp.concatenate([wq_ref[...], wk_ref[...], wv_ref[...], wo_ref[...].T], axis=1)
    )
    pl.semaphore_wait(barrier, 3 + 1 + 2 * (dp - 1))

    def small_copy(ids, src_p, src_g, k, way_p):
        view = small_w.at[src_p, src_g]
        return copy_to(
            view, view, sem_sm_send.at[way_p, k], sem_sm_recv.at[src_p, src_g], ids
        )

    small_copy({"pipe": o}, p, g, 0, 1).start()

    def small_start(k):
        small_copy({"dp": other(k)}, p, g, k, 0).start()
        small_copy({"dp": other(k), "pipe": o}, p, g, k, 1).start()

    each(1, dp, small_start)

    def own_copy(c):
        a, n = sent[c]
        return copy_to(
            w_ref.at[p, g, :, a : a + n],
            w_ref.at[p, g, :, a : a + n],
            sem_own_send.at[c],
            sem_own_recv.at[c],
            {"pipe": o},
        )

    def own_arrival(c):
        a, n = sent[c]
        view = w_ref.at[o, g, :, a : a + n]
        copy_to(view, view, sem_own_send.at[c], sem_own_recv.at[c], {"pipe": o}).wait_recv()

    def view_of(l, c, s, side):
        a, n = sent[c]
        width = n // 2
        return w_ref.at[l, s, :, pl.ds(pl.multiple_of(a + side * width, 128), width)]

    def z_copy(l, c, s, target, sem):
        view = view_of(l, c, s, p)
        return copy_to(
            view, view, sem_z_send.at[l, c, sem], sem_z_recv.at[l, c, s], {"dp": target}
        )

    def p_copy(l, c, s, side):
        view = view_of(l, c, s, side)
        return copy_to(view, view, sem_p_send.at[l, c, s], sem_p_recv.at[l, c, s], {"pipe": o})

    def unless_relayed(s, run):
        if line:
            to_end = (s == 0) | (s == dp - 1)
            pl.when(jnp.logical_not(to_end & (jnp.abs(g - s) >= 2)))(run)
        else:
            run()

    def issue(l, c):
        @pl.when(l != p)
        def _():
            own_arrival(c)

        def start(k):
            s = other(dp - k)
            unless_relayed(s, lambda: z_copy(l, c, g, s, s).start())

        each(1, dp, start)

    def relays(l, c, s, run):
        if line:
            away = lax.rem(g + 2, dp)
            beyond = (s == away) | (s == dp - 1 - g)
            sem = jnp.where(s == away, g, away)
            pl.when(((g == 1) | (g == 2)) & beyond)(
                lambda: run(z_copy(l, c, s, (g // 2) * (dp - 1), sem))
            )

    def poll(l, c):
        def arrive(k):
            s = other(k)
            z_copy(l, c, s, s, s).wait_recv()
            relays(l, c, s, lambda copy: copy.start())
            p_copy(l, c, s, p).start()

        each(1, dp, arrive)
        each(1, dp, lambda k: p_copy(l, c, other(k), o).wait_recv())

    own_copy(0).start()
    pack(
        1, jnp.concatenate([cq_ref[...], ck_ref[...], cv_ref[...], co_ref[...].T], axis=1)
    )
    own_copy(1).start()
    issue(0, 0)
    pack(2, jnp.concatenate([gate_ref[...], upw_ref[...]], axis=1))
    own_copy(2).start()
    pack(3, down_ref[...])
    own_copy(3).start()
    inner_group = (g > 0) & (g < dp - 1)
    paces = ((inner_group, AHEAD), (jnp.logical_not(inner_group), AHEAD_END))

    for mine, ahead in paces:

        @pl.when(mine)
        def _():
            for c in range(1, ahead):
                issue(0, c)

    def issue_after(l, c):
        for mine, ahead in paces:
            nl, nc = l + (c + ahead) // 4, (c + ahead) % 4

            @pl.when(mine & (nl < layers))
            def _():
                issue(nl, nc)

    ri = lax.broadcasted_iota(jnp.int32, (rows, rows), 0)
    ci = lax.broadcasted_iota(jnp.int32, (rows, rows), 1)
    dec_row = dec_ref[pl.ds(p, 1), :].astype(F32)
    enc_row = seg_ref[pl.ds(p, 1), :].astype(F32)
    dec_col = jnp.sum(jnp.where(ri == ci, dec_row, 0.0), axis=1, keepdims=True)
    allowed = (dec_col == dec_row) & (ci <= ri)
    cmask = jnp.where(dec_col == enc_row, 0.0, -1e30)
    bi = lax.broadcasted_iota(jnp.int32, (BUCKETS, MAXD), 0)
    starts = jnp.sum(jnp.where(buck_ref[...] < bi, 1.0, 0.0), axis=1, keepdims=True)
    dist = jnp.clip(ri - ci, 0, MAXD - 1).astype(F32)
    bmap = jnp.zeros((rows, rows), F32)
    for b in range(1, BUCKETS):
        bmap = bmap + jnp.where(dist >= starts[b : b + 1], 1.0, 0.0)
    bmap_s[...] = bmap

    def small_arrive(k):
        s = other(k)
        small_copy({"dp": s}, p, s, k, 0).wait_recv()
        small_copy({"dp": s}, o, s, k, 0).wait_recv()

    each(1, dp, small_arrive)
    small_copy({"pipe": o}, o, g, 0, 1).wait_recv()
    for l in range(layers):
        for n in range(3):
            gains_s[l, n : n + 1] = jnp.concatenate(
                [small_w[l, s, n : n + 1, 0:chunk] for s in range(dp)], axis=1
            )
        for h in range(heads):
            bias = jnp.zeros((rows, rows), F32)
            for b in range(BUCKETS):
                at = b % table_rows
                value = small_w[l, b // table_rows, 8 + h : 9 + h, at : at + 1]
                bias = jnp.where(bmap == float(b), value, bias)
            bias_s[l, h * rows : (h + 1) * rows] = jnp.where(allowed, bias, -1e30)

    def weights(l, a, b):
        return w_ref[l, :, :, a:b].reshape(D, b - a)

    def first_copy(slot, part):
        return copy_to(
            send_one.at[slot, part],
            recv_one.at[slot, part],
            sem_send.at[slot, part],
            sem_recv.at[slot, part],
            {"tensor": near if part == 0 else far},
        )

    def second_copy(slot, part):
        return copy_to(
            send_two.at[slot, part],
            recv_two.at[slot, part],
            sem_send.at[slot, part + 2],
            sem_recv.at[slot, part + 2],
            {"tensor": far if part == 0 else near},
        )

    def sum_start(slot, make_half):
        for part in range(2):
            send_one[slot, part] = make_half(part).astype(BF16)
            first_copy(slot, part).start()

    def sum_middle(slot):
        for part in range(2):
            first_copy(slot, part).wait()
            value = send_one[slot, part].astype(F32) + recv_one[slot, part].astype(F32)
            send_two[slot, part] = value.astype(BF16)
            second_copy(slot, part).start()

    def sum_end(slot):
        pieces = []
        for part in range(2):
            second_copy(slot, part).wait()
            pieces.append(send_two[slot, part].astype(F32) + recv_two[slot, part].astype(F32))
        return jnp.concatenate(pieces, axis=0)

    def all_sum(slot, make_half, cover=None, later=None):
        sum_start(slot, make_half)
        if cover is not None:
            cover()
        sum_middle(slot)
        if later is not None:
            later()
        return sum_end(slot)

    def keep(l, r, value):
        width = summed[r][1] // 2
        for side in range(2):
            grad_s[l, side, :, :, offsets[r] : offsets[r] + width] = (
                value[:, side * width : (side + 1) * width].astype(BF16).reshape(dp, chunk, width)
            )

    def columns(r):
        return pl.ds(offsets[r], summed[r][1] // 2)

    def swap_copy(l, r):
        return copy_to(
            grad_s.at[l, o, :, :, columns(r)],
            swap_s.at[l, :, :, columns(r)],
            sem_sw_send.at[l, r],
            sem_sw_recv.at[l, r],
            {"pipe": o},
        )

    def slot_of(source, owner):
        return lax.rem(source - owner + dp, dp) - 1

    def piece_copy(l, r, s):
        return copy_to(
            grad_s.at[l, p, s, :, columns(r)],
            part_s.at[l, slot_of(g, s), :, columns(r)],
            sem_g_send.at[l, r, s],
            sem_g_recv.at[l, r, g],
            {"dp": s},
        )

    def relay_copy(l, r, s, slot):
        return copy_to(
            grad_s.at[l, p, s, :, columns(r)],
            relay_s.at[l, slot, :, columns(r)],
            sem_g_send.at[l, r, s],
            sem_r_recv.at[l, r, slot],
            {"dp": g + 1 - 2 * (g // 2)},
        )

    def piece_arrival(l, r, s):
        return copy_to(
            grad_s.at[l, p, g, :, columns(r)],
            part_s.at[l, slot_of(s, g), :, columns(r)],
            sem_g_send.at[l, r, s],
            sem_g_recv.at[l, r, s],
            {"dp": s},
        )

    def inside(s):
        return (s == 1) | (s == 2)

    def is_inside():
        return inside(g)

    def send_pieces(l, r):
        swap_copy(l, r).wait_recv()

        def merge(s):
            grad_s[l, p, s, :, columns(r)] = (
                grad_s[l, p, s, :, columns(r)].astype(F32)
                + swap_s[l, s, :, columns(r)].astype(F32)
            ).astype(BF16)

        each(0, dp, merge)

        def start(k):
            s = other(dp - k)
            if not line_back:
                piece_copy(l, r, s).start()
                return

            for slot in range(2):

                @pl.when((jnp.abs(g - s) == 3 - slot) & jnp.logical_not(is_inside()))
                def _():
                    relay_copy(l, r, s, slot).start()

            @pl.when((jnp.abs(g - s) == 1) & jnp.logical_not(is_inside() & inside(s)))
            def _():
                piece_copy(l, r, s).start()

        each(1, dp, start)

    def pass_on(l, r):
        if not line_back:
            return

        @pl.when(is_inside())
        def _():
            for slot, s in enumerate((lax.rem(g + 2, dp), dp - 1 - g)):
                relay_copy(l, r, s, slot).wait_recv()
                grad_s[l, p, s, :, columns(r)] = (
                    grad_s[l, p, s, :, columns(r)].astype(F32)
                    + relay_s[l, slot, :, columns(r)].astype(F32)
                ).astype(BF16)
                piece_copy(l, r, s).start()

    def total_of(l, r):
        total_s[l, :, columns(r)] = grad_s[l, p, g, :, columns(r)].astype(F32)

        def add(k):
            s = other(k)

            def run():
                piece_arrival(l, r, s).wait_recv()
                total_s[l, :, columns(r)] = total_s[l, :, columns(r)] + part_s[
                    l, slot_of(s, g), :, columns(r)
                ].astype(F32)

            if line_back:
                pl.when(inside(s) | (jnp.abs(g - s) == 1))(run)
            else:
                run()

        each(1, dp, add)

    x_in[0] = h_ref[p]
    enc = enc_ref[p]

    def make_result(l):
        def make_three(part):
            return dot_nt(
                hid_s[l, part * half : (part + 1) * half], weights(l, 2 * ff, 3 * ff)
            )

        return make_three

    def forward(l, carry):
        poll(l, 0)
        issue_after(l, 0)
        x0 = x_in[l].astype(F32)
        n1 = (x0 * norm_scale(x0) * gains_s[l, 0:1]).astype(BF16)
        n_one[l] = n1
        qkv = dot_nn(n1, weights(l, c_q, c_so)).astype(BF16)
        qkv_s[l] = qkv
        q = qkv[:, :inner]
        k = qkv[:, inner : 2 * inner]
        v = qkv[:, 2 * inner :]
        e = jnp.exp(dot_nt(spread_heads(q, masks), k) + bias_s[l])
        prob = e * (1.0 / jnp.sum(e, axis=-1, keepdims=True))
        p_s[l] = prob
        so_s[l] = join_heads(dot_nn(prob.astype(BF16), v), masks).astype(BF16)

        def make_one(part):
            return dot_nt(so_s[l, part * half : (part + 1) * half], weights(l, c_so, c_cq))

        def cover_one():
            poll(l, 1)
            issue_after(l, 1)
            ckv_s[l] = dot_nn(enc, weights(l, c_ck, c_co)).astype(BF16)

        x1 = x0 + all_sum(3 * l, make_one, cover_one)
        r_one[l] = x1
        n2 = (x1 * norm_scale(x1) * gains_s[l, 1:2]).astype(BF16)
        n_two[l] = n2
        cq = dot_nn(n2, weights(l, c_cq, c_ck)).astype(BF16)
        cq_s[l] = cq
        ckv = ckv_s[l]
        ck = ckv[:, :inner]
        cv = ckv[:, inner:]
        e = jnp.exp(
            dot_nt(spread_heads(cq, masks), ck) + jnp.concatenate([cmask] * heads, axis=0)
        )
        prob = e * (1.0 / jnp.sum(e, axis=-1, keepdims=True))
        pc_s[l] = prob
        co_s[l] = join_heads(dot_nn(prob.astype(BF16), cv), masks).astype(BF16)

        def make_two(part):
            return dot_nt(co_s[l, part * half : (part + 1) * half], weights(l, c_co, c_end))

        def cover_two():
            poll(l, 2)
            issue_after(l, 2)

        x2 = x1 + all_sum(3 * l + 1, make_two, None, cover_two)
        r_two[l] = x2
        n3 = (x2 * norm_scale(x2) * gains_s[l, 2:3]).astype(BF16)
        n_three[l] = n3
        gu = dot_nn(n3, weights(l, 0, 2 * ff))
        gu_s[l] = gu
        value, _ = gelu_parts(gu[:, :ff])
        hid_s[l] = (value * gu[:, ff:]).astype(BF16)

        @pl.when(l == layers - 1)
        def _():
            keep(l, 0, dot_tn(up_ref[p], hid_s[l]))
            swap_copy(l, 0).start()
            send_pieces(l, 0)

        poll(l, 3)
        issue_after(l, 3)

        @pl.when(l < layers - 1)
        def _():
            x_in[l + 1] = (x2 + all_sum(3 * l + 2, make_result(l))).astype(BF16)

        return carry

    lax.fori_loop(0, layers, forward, 0)
    last = 3 * layers - 1
    sum_start(last, make_result(layers - 1))
    g_in[...] = up_ref[p]

    def attend_back(grad, query, keys, values, attended, prob):
        gs = spread_heads(grad, masks)
        qs = spread_heads(query, masks)
        delta = jnp.sum(
            gs.astype(F32) * jnp.concatenate([attended.astype(F32)] * heads, axis=0),
            axis=-1,
            keepdims=True,
        )
        ds = prob * (dot_nt(gs, values) - delta)
        dsb = ds.astype(BF16)
        grad_query = join_heads(dot_nn(dsb, keys), masks).astype(BF16)
        return grad_query, ds, dsb, gs, qs

    def backward(step, carry):
        l = layers - 1 - step
        base = 3 * layers + 3 * step
        g3 = g_in[...]
        gf = g3.astype(F32)
        gu = gu_s[l]
        value, slope = gelu_parts(gu[:, :ff])
        dh = dot_nn(g3, weights(l, 2 * ff, 3 * ff))
        dgu = jnp.concatenate(
            [(dh * gu[:, ff:] * slope).astype(BF16), (dh * value).astype(BF16)], axis=1
        )

        def make_three(part):
            return dot_nt(dgu[part * half : (part + 1) * half], weights(l, 0, 2 * ff))

        def cover_three():
            @pl.when(step > 0)
            def _():
                keep(l, 0, dot_tn(g3, hid_s[l]))
                swap_copy(l, 0).start()

            keep(l, 1, dot_tn(n_three[l], dgu))
            swap_copy(l, 1).start()

            @pl.when(step == 0)
            def _():
                sum_middle(last)

        def later_three():
            @pl.when(step > 0)
            def _():
                send_pieces(l, 0)

            send_pieces(l, 1)

            @pl.when(step == 0)
            def _():
                pass_on(l, 0)

            @pl.when(step > 0)
            def _():
                pass_on(l + 1, 3)

        dn = all_sum(base, make_three, cover_three, later_three)
        back, gain_three = norm_back(r_two[l], gains_s[l, 2:3], dn)
        g2 = gf + back
        g2b = g2.astype(BF16)
        dc = dot_nn(g2b, weights(l, c_co, c_end)).astype(BF16)
        ckv = ckv_s[l]
        co = co_s[l]
        pc = pc_s[l]
        dcq, _, dsb, gs, qs = attend_back(dc, cq_s[l], ckv[:, :inner], ckv[:, inner:], co, pc)

        def make_two(part):
            return dot_nt(dcq[part * half : (part + 1) * half], weights(l, c_cq, c_ck))

        def cover_two():
            dck = dot_tn(dsb, qs).astype(BF16)
            dcv = dot_tn(pc.astype(BF16), gs).astype(BF16)
            dckv = jnp.concatenate([dck, dcv], axis=1)
            blocks = inner // chunk
            for k in range(D // inner):
                owner = t if k == 0 else peers[k - 1]
                rows_of = w_ref[l, pl.ds(owner * blocks, blocks), :, c_ck:c_co]
                part = dot_nt(rows_of.reshape(inner, 2 * inner), dckv)
                if k == 0:
                    enc_own[l] = part
                else:
                    enc_send[l, k - 1] = part.astype(BF16)
                    enc_copy(l, k - 1).start()
            keep(
                l,
                2,
                jnp.concatenate(
                    [dot_tn(n_two[l], dcq), dot_tn(enc, dckv), dot_tn(g2b, co)], axis=1
                ),
            )
            swap_copy(l, 2).start()

            @pl.when(step == 0)
            def _():
                x_in[layers] = (r_two[layers - 1] + sum_end(last)).astype(BF16)

        def later_two():
            send_pieces(l, 2)

            @pl.when(step > 0)
            def _():
                pass_on(l, 0)

            pass_on(l, 1)

        dn = all_sum(base + 1, make_two, cover_two, later_two)
        back, gain_two = norm_back(r_one[l], gains_s[l, 1:2], dn)
        g1 = g2 + back
        g1b = g1.astype(BF16)
        dself = dot_nn(g1b, weights(l, c_so, c_cq)).astype(BF16)
        qkv = qkv_s[l]
        so = so_s[l]
        ps = p_s[l]
        dq, ds, dsb, gs, qs = attend_back(
            dself, qkv[:, :inner], qkv[:, inner : 2 * inner], qkv[:, 2 * inner :], so, ps
        )
        dk = dot_tn(dsb, qs).astype(BF16)
        dv = dot_tn(ps.astype(BF16), gs).astype(BF16)
        dqkv = jnp.concatenate([dq, dk, dv], axis=1)

        def make_one(part):
            return dot_nt(dqkv[part * half : (part + 1) * half], weights(l, c_q, c_so))

        def cover_one():
            keep(l, 3, jnp.concatenate([dot_tn(n_one[l], dqkv), dot_tn(g1b, so)], axis=1))
            swap_copy(l, 3).start()

        def later_one():
            send_pieces(l, 3)
            pass_on(l, 2)
            buckets = bmap_s[...]
            for h in range(heads):
                ds_h = ds[h * rows : (h + 1) * rows]
                for b in range(BUCKETS):
                    table_s[h, b : b + 1] = jnp.sum(
                        jnp.where(buckets == float(b), ds_h, 0.0), axis=0, keepdims=True
                    )

        dn = all_sum(base + 2, make_one, cover_one, later_one)
        back, gain_one = norm_back(x_in[l].astype(F32), gains_s[l, 0:1], dn)
        gin = g1 + back
        ingrad_s[l] = gin
        g_in[...] = gin.astype(BF16)
        small_g[l] = jnp.zeros(small_g.shape[1:], F32)
        table = jnp.sum(table_s[...], axis=2)
        for s in range(dp):
            for n, value in enumerate((gain_one, gain_two, gain_three)):
                small_g[l, s, n : n + 1, 0:chunk] = value[:, s * chunk : (s + 1) * chunk]
            for h in range(heads):
                small_g[l, s, 8 + h : 9 + h, 0:table_rows] = table[
                    h : h + 1, s * table_rows : (s + 1) * table_rows
                ]
        return carry

    def enc_copy(l, k):
        return copy_to(
            enc_send.at[l, k],
            enc_recv.at[l, k],
            sem_enc_send.at[l, k],
            sem_enc_recv.at[l, k],
            {"tensor": peers[k]},
        )

    lax.fori_loop(0, layers, backward, 0)

    def grad_small_copy(l, s, src_p, src_g, ids):
        return copy_to(
            small_g.at[l, s],
            small_out.at[src_p, src_g],
            sem_sg_send.at[l, s],
            sem_sg_recv.at[src_p, src_g],
            ids,
        )

    def local_copy(n, src, dst):
        return pltpu.make_async_copy(src, dst, sem_local.at[n])

    def own_small():
        return local_copy(3, small_g.at[p, g], small_out.at[p, g])

    own_small().start()
    grad_small_copy(o, g, p, g, {"pipe": o}).start()

    def grad_small_start(k):
        s = other(k)
        grad_small_copy(p, s, p, g, {"dp": s}).start()
        grad_small_copy(o, s, p, g, {"dp": s, "pipe": o}).start()

    each(1, dp, grad_small_start)
    for l in range(layers):
        total = enc_own[l]
        for k in range(3):
            enc_copy(l, k).wait()
            total = total + enc_recv[l, k].astype(F32)
        enc_own[l] = total

    moved = (
        (x_in.at[o + 1], sect_out.at[p]),
        (ingrad_s.at[o], ingrad_out.at[p]),
        (enc_own.at[o], enc_out.at[p]),
    )

    away = (sect_out.at[o], ingrad_out.at[o], enc_out.at[o])

    def moved_copy(n):
        src, dst = moved[n]
        return copy_to(src, dst, sem_o_send.at[n], sem_o_recv.at[n], {"pipe": o})

    kept = (x_in.at[p + 1], ingrad_s.at[p], enc_own.at[p])

    def kept_copy(n):
        return local_copy(n, kept[n], moved[n][1])

    for n in range(3):
        moved_copy(n).start()
        kept_copy(n).start()

    def final_copy(r):
        return copy_to(
            total_s.at[o, :, columns(r)],
            sum_out.at[p, :, columns(r)],
            sem_f_send.at[r],
            sem_f_recv.at[r],
            {"pipe": o},
        )

    def own_total(r):
        return local_copy(4 + r, total_s.at[p, :, columns(r)], sum_out.at[p, :, columns(r)])

    for r in range(parts):
        if r == parts - 1:
            pass_on(0, r)
        for l in reversed(range(layers)):
            total_of(l, r)
        final_copy(r).start()
        own_total(r).start()

    def arrival(view, sem):
        copy_to(view, view, sem, sem, {"pipe": o}).wait_recv()

    for n in range(3):
        moved_copy(n).wait_send()
        kept_copy(n).wait()
        arrival(away[n], sem_o_recv.at[n])
    for r in range(parts):
        final_copy(r).wait_send()
        own_total(r).wait()
        arrival(sum_out.at[o, :, columns(r)], sem_f_recv.at[r])
    own_small().wait()
    grad_small_copy(o, g, p, g, {"pipe": o}).wait_send()
    grad_small_copy(o, g, o, g, {"pipe": o}).wait_recv()

    def grad_small_end(k):
        s = other(k)
        grad_small_copy(p, s, p, g, {"dp": s}).wait_send()
        grad_small_copy(o, s, p, g, {"dp": s}).wait_send()
        grad_small_copy(p, s, p, s, {"dp": s}).wait_recv()
        grad_small_copy(o, s, o, s, {"dp": s}).wait_recv()

    each(1, dp, grad_small_end)
    small_copy({"pipe": o}, p, g, 0, 1).wait_send()

    def small_end(k):
        small_copy({"dp": other(k)}, p, g, k, 0).wait_send()
        small_copy({"dp": other(k)}, p, g, k, 1).wait_send()

    each(1, dp, small_end)
    for c in range(4):
        own_copy(c).wait_send()

    def layer_end(l, carry):
        for c in range(4):

            def sent_end(k):
                s = other(k)
                unless_relayed(s, lambda: z_copy(l, c, g, s, s).wait_send())
                relays(l, c, s, lambda copy: copy.wait_send())
                p_copy(l, c, s, p).wait_send()

            each(1, dp, sent_end)
        for r in range(parts):
            swap_copy(l, r).wait_send()
            each(1, dp, lambda k: piece_copy(l, r, other(k)).wait_send())
        return carry

    lax.fori_loop(0, layers, layer_end, 0)


def run_main(inputs, layers, dp):
    h, enc, wq, gate, table = inputs[0], inputs[1], inputs[6], inputs[14], inputs[18]
    rows, enc_rows = h.shape[1], enc.shape[1]
    chunk, inner, ff = wq.shape[0], wq.shape[1], gate.shape[1]
    heads, table_rows = inner // HEAD, table.shape[1]
    half = rows // 2
    slots = 6 * layers
    width = 3 * ff + 8 * inner
    small = (16, -(-chunk // 128) * 128)
    vm = pltpu.VMEM
    dma = pltpu.SemaphoreType.DMA
    dims = (layers, dp, rows, inner, ff, heads, chunk, table_rows)
    return pl.pallas_call(
        functools.partial(main_kernel, dims),
        out_shape=(
            jax.ShapeDtypeStruct((2, chunk, width // 2), F32),
            jax.ShapeDtypeStruct((2, rows, D), BF16),
            jax.ShapeDtypeStruct((2, rows, D), F32),
            jax.ShapeDtypeStruct((2, inner, enc_rows), F32),
            jax.ShapeDtypeStruct((2, dp) + small, F32),
        ),
        in_specs=[pl.BlockSpec(memory_space=pltpu.VMEM)] * 19,
        out_specs=(pl.BlockSpec(memory_space=pltpu.HBM),) * 5,
        scratch_shapes=[
            vm((layers, dp, chunk, width), BF16),
            vm((layers, dp) + small, F32),
            vm((layers, 8, D), F32),
            vm((layers, heads * rows, rows), F32),
            vm((rows, rows), F32),
            vm((layers + 1, rows, D), BF16),
            vm((rows, D), BF16),
            vm((layers, rows, D), F32),
            vm((layers, rows, D), F32),
            vm((layers, rows, D), BF16),
            vm((layers, rows, D), BF16),
            vm((layers, rows, D), BF16),
            vm((layers, rows, 3 * inner), BF16),
            vm((layers, rows, inner), BF16),
            vm((layers, heads * rows, rows), F32),
            vm((layers, rows, inner), BF16),
            vm((layers, enc_rows, 2 * inner), BF16),
            vm((layers, rows, inner), BF16),
            vm((layers, heads * rows, enc_rows), F32),
            vm((layers, rows, 2 * ff), F32),
            vm((layers, rows, ff), BF16),
            vm((slots, 2, half, D), BF16),
            vm((slots, 2, half, D), BF16),
            vm((slots, 2, half, D), BF16),
            vm((slots, 2, half, D), BF16),
            vm((layers, 3, inner, enc_rows), BF16),
            vm((layers, inner, enc_rows), F32),
            vm((layers, 3, inner, enc_rows), BF16),
            vm((layers, 2, dp, chunk, width // 2), BF16),
            vm((layers, dp, chunk, width // 2), BF16),
            vm((layers, dp - 1, chunk, width // 2), BF16),
            vm((layers, 2, chunk, width // 2), BF16),
            vm((layers, chunk, width // 2), F32),
            vm((layers, rows, D), F32),
            vm((heads, BUCKETS, rows), F32),
            vm((layers, dp) + small, F32),
            dma((slots, 4)),
            dma((slots, 4)),
            dma((layers, 3)),
            dma((layers, 3)),
            dma((4,)),
            dma((4,)),
            dma((layers, 4, dp)),
            dma((layers, 4, dp)),
            dma((layers, 4, dp)),
            dma((layers, 4, dp)),
            dma((layers, 4)),
            dma((layers, 4)),
            dma((layers, 4, dp)),
            dma((layers, 4, dp)),
            dma((layers, 4, 2)),
            dma((4,)),
            dma((4,)),
            dma((3,)),
            dma((3,)),
            dma((2, dp)),
            dma((2, dp)),
            dma((2, dp)),
            dma((2, dp)),
            dma((8,)),
        ],
        compiler_params=pltpu.CompilerParams(
            collective_id=0, has_side_effects=True, vmem_limit_bytes=60 * 1024 * 1024
        ),
    )(*inputs)


def finish_kernel(dims, *refs):
    inner, ff, heads, chunk, table_rows = dims
    sum_hbm, sect_ref, ingrad_ref, enc_ref, small_hbm = refs[:5]
    (sect_out, ingrad_out, enc_out, q_out, k_out, v_out, o_out, cq_out, ck_out, cv_out) = refs[5:15]
    co_out, gate_out, up_out, down_out, gain_out, tab_out = refs[15:21]
    sum_ref, small_ref, sem = refs[21:]
    _, summed = layout(inner, ff)

    def take(a, n):
        offset = 0
        for start, width in summed:
            if start <= a < start + width:
                pieces = []
                for side in range(2):
                    low = max(a, start + side * (width // 2))
                    high = min(a + n, start + (side + 1) * (width // 2))
                    if low < high:
                        at = offset + low - start - side * (width // 2)
                        pieces.append(sum_ref[side, :, at : at + high - low])
                return pieces[0] if len(pieces) == 1 else jnp.concatenate(pieces, axis=1)
            offset += width // 2

    copies = [
        pltpu.make_async_copy(src, dst, sem.at[n])
        for n, (src, dst) in enumerate(
            ((sum_hbm, sum_ref), (small_hbm, small_ref), (sect_ref, sect_out))
            + ((ingrad_ref, ingrad_out), (enc_ref, enc_out))
        )
    ]
    for copy in copies:
        copy.start()
    copies[1].wait()
    small = jnp.sum(small_ref[...], axis=(0, 1))
    for n in range(3):
        gain_out[n] = small[n : n + 1, 0:chunk]
    for h in range(heads):
        tab_out[h] = small[8 + h : 9 + h, 0:table_rows]
    copies[0].wait()
    c = 3 * ff
    for n, out in enumerate((q_out, k_out, v_out, o_out, cq_out, ck_out, cv_out, co_out)):
        value = take(c + n * inner, inner)
        out[...] = value.T if n % 4 == 3 else value
    gate_out[...] = take(0, ff)
    up_out[...] = take(ff, ff)
    down_out[...] = take(2 * ff, ff)
    for copy in copies[2:]:
        copy.wait()


def run_finish(parts, inner, ff, chunk, table_rows):
    heads = inner // HEAD
    total, sect, ingrad, enc, small = parts
    into, outer = (chunk, inner), (inner, chunk)
    shapes = [sect.shape, ingrad.shape, enc.shape]
    shapes += [into, into, into, outer] * 2
    shapes += [(chunk, ff), (chunk, ff), (chunk, ff), (3, 1, chunk), (heads, 1, table_rows)]
    types = [BF16] + [F32] * 15
    return pl.pallas_call(
        functools.partial(finish_kernel, (inner, ff, heads, chunk, table_rows)),
        out_shape=tuple(jax.ShapeDtypeStruct(s, d) for s, d in zip(shapes, types)),
        in_specs=[pl.BlockSpec(memory_space=pltpu.HBM)] * 5,
        out_specs=(pl.BlockSpec(memory_space=pltpu.VMEM),) * 16,
        scratch_shapes=[
            pltpu.VMEM(total.shape, F32),
            pltpu.VMEM(small.shape, F32),
            pltpu.SemaphoreType.DMA((5,)),
        ],
        compiler_params=pltpu.CompilerParams(vmem_limit_bytes=60 * 1024 * 1024),
    )(*parts)


def body(*args):
    layers = lax.axis_size("pipe")
    dp = lax.axis_size("dp")
    inputs = list(args[:5]) + [args[5].reshape(1, -1)] + [value[0] for value in args[6:]]
    inputs[16], inputs[18] = inputs[16].T, inputs[18].T
    chunk, inner = inputs[6].shape
    ff, table_rows = inputs[14].shape[1], inputs[18].shape[1]
    parts = run_main(inputs, layers, dp)
    outs = run_finish(parts, inner, ff, chunk, table_rows)
    outs = list(outs)
    outs[2] = outs[2].transpose(0, 2, 1)
    outs[13] = outs[13].T
    gain, table = outs[14].transpose(1, 0, 2), outs[15].transpose(1, 2, 0)
    return tuple(value[None] for value in outs[:14]) + (gain, table)


def solution(mesh):
    inner_spec = P("pipe", "dp", "tensor")
    outer_spec = P("pipe", "tensor", "dp")
    placed = (
        P(None, "dp", None),
        P(None, "dp", None),
        P(None, "dp", None),
        P(None, "dp"),
        P(None, "dp"),
        P(),
        inner_spec,
        inner_spec,
        inner_spec,
        outer_spec,
        inner_spec,
        inner_spec,
        inner_spec,
        outer_spec,
        inner_spec,
        inner_spec,
        outer_spec,
        P("pipe", None, "dp"),
        inner_spec,
    )
    return jax.shard_map(
        body,
        mesh=mesh,
        in_specs=placed,
        out_specs=(
            P("pipe", None, "dp", None),
            P("pipe", None, "dp", None),
            P("pipe", None, "dp", "tensor"),
            inner_spec,
            inner_spec,
            inner_spec,
            outer_spec,
            inner_spec,
            inner_spec,
            inner_spec,
            outer_spec,
            inner_spec,
            inner_spec,
            outer_spec,
            P("pipe", None, "dp"),
            inner_spec,
        ),
        check_vma=False,
    )
```
